128 devices in a mesh: curve: 128 (over z, y, x, core).
Axes of the slice: x: 4, y: 4, z: 4, core: 2. Of those that a mesh axis runs over, the one named last changes fastest.
Arguments:
- state: float32 [3, 64, 65536], P(None, None, 'curve'), as said below
- neighbours: int32 [4, 65536], P(None, 'curve'), may hold values from -1 to 65535, as said below
- metric: float32 [65536], P('curve'), may hold values from 0.5 to 4
- flags: int32 [65536], P('curve'), may hold values 0 or 1
- new_owner: int32 [65536, 1], P('curve'), may hold values from 0 to 127; in each aligned block of 512 rows (0 to 511, 512 to 1023, ...) at most 8 rows name the same one
Outputs:
- migrated: float32 [4, 3, 64, 131072], P(None, None, None, 'curve')
The draws below stay inside these ranges and needn't reach their ends.
Inputs may be any that keep to these rules, and one draw needn't show every extreme that they name: `state`: the first of the three fields (depth) lies between 0.5 and 2.0 at every node. Faces pair up: if neighbours[f, e] = n >= 0 then neighbours[opposite f, n] = e, and walls (-1) come in such pairs too. The element across face 0 or 1 lies on the same device or the next or previous one; across face 2 or 3 on the same device or the device 32 after or before. At most 32 elements of a device have their neighbour across one given face on one given other device, and every device but the last has exactly 32 across face 1 on the next device. `new_owner`: the rows of one device name each owner at most 8 times, a bound that some block reaches.
All inputs are finite; a program needn't handle non-finite values. No bound on the sum of `flags` on one device may be relied on, other than what follows from the above.
Results may differ from the reference program's by a relative error of at most 0.0003.
Values sent between devices are 32-bit elements; how exact they have to be, the bound alone decides.
A program may use at most 64 MiB of HBM per device.

```python
import math
import jax
import jax.numpy as jnp
import numpy as np
from jax import lax

NODES = 64
FIELDS = 3
E_DEV = 512
ELEMS = 65536
HALF = 256
CROSS = 32
STRIDE = 32
SLOTS = 8
RECV = 131072
N_CURVE = 128


def draw_state(key, part):
    depth_key, moment_key = jax.random.split(jax.random.fold_in(key, 7))
    depth_field = jax.random.uniform(depth_key, (1, NODES, ELEMS), jnp.float32, 0.5, 2.0)
    momentum = 0.5 * jax.random.normal(moment_key, (2, NODES, ELEMS), jnp.float32)
    return jnp.concatenate([depth_field, momentum], axis=0)


def pair_map(key, offset):
    shuffle_key, wall_key = jax.random.split(key)
    unit_count = 2 * N_CURVE
    shuffled = jax.vmap(lambda k: jax.random.permutation(k, HALF))(jax.random.split(shuffle_key, unit_count)).astype(jnp.int32)
    unit_ids = jnp.arange(unit_count, dtype=jnp.int32)
    device_ids = unit_ids // 2
    upper_part = unit_ids % 2
    unit_start = device_ids * E_DEV + upper_part * HALF
    positions = unit_start[:, None] + shuffled
    partner_up = jnp.where(device_ids + offset < N_CURVE, 2 * (device_ids + offset), -1)
    partner_low = jnp.where(device_ids - offset >= 0, 2 * (device_ids - offset) + 1, -1)
    partner = jnp.where(upper_part == 1, partner_up, partner_low)
    crossing = jnp.where(partner >= 0, CROSS, 0).astype(jnp.int32)[:, None]
    step_ids = jnp.arange(HALF, dtype=jnp.int32)[None, :]
    cycle_pos = crossing + jnp.mod(step_ids - crossing + 1, HALF - crossing)
    own_target = jnp.take_along_axis(positions, jnp.where(step_ids >= crossing, cycle_pos, 0), axis=1)
    other_target = positions[jnp.maximum(partner, 0)]
    target = jnp.where(step_ids < crossing, other_target, own_target)
    walled = (jax.random.randint(wall_key, (unit_count, HALF), 0, 8) == 0) & (step_ids >= crossing)
    forward_map = jnp.zeros((ELEMS,), jnp.int32).at[positions.reshape(-1)].set(jnp.where(walled, -1, target).reshape(-1))
    backward_map = jnp.zeros((ELEMS,), jnp.int32).at[target.reshape(-1)].set(jnp.where(walled, -1, positions).reshape(-1))
    return (backward_map, forward_map)


def draw_neighbours(key, part):
    near_key, far_key = jax.random.split(jax.random.fold_in(key, 11))
    west_map, east_map = pair_map(near_key, 1)
    south_map, north_map = pair_map(far_key, STRIDE)
    return jnp.stack([west_map, east_map, south_map, north_map])


def with_ends(values, stream_key, least, high):
    longest = values.shape.index(max(values.shape))
    spots = []
    for shift in (0, 1):
        where = [jax.random.randint(jax.random.fold_in(stream_key, axis), (), 0, length) for axis, length in enumerate(values.shape)]
        where[longest] = (where[longest] + shift) % values.shape[longest]
        spots.append(tuple(where))
    return values.at[spots[0]].set(least).at[spots[1]].set(high)


def block_scale(key, dims, cuts, smallest, high):
    def one(axis_at, shards_of):
        draws = jax.random.uniform(jax.random.fold_in(jax.random.fold_in(key, 6), axis_at), (shards_of,), jnp.float32, smallest / len(cuts), high / len(cuts))
        return jnp.repeat(jnp.exp(draws), dims[axis_at] // shards_of).reshape((-1,) + (1,) * (len(dims) - axis_at - 1))

    gain = one(*cuts[0])
    for cut in cuts[1:]:
        gain = gain * one(*cut)
    return gain


def shared_out(rng, own, number, rows, amount, top, reach, slope):
    order = jax.random.permutation(rng, amount)
    packed, ordinary = shares(amount, rows * top, reach, slope, True), shares(amount, rows * top, reach, slope, False)
    places = jnp.arange(amount)

    def named(tallies, turn):
        used = int((tallies > 0).sum())
        fixed = max(1, used // 4)
        moved = fixed + (places - fixed + turn * (used - fixed)) % max(1, amount - fixed)
        return jnp.zeros((amount,), jnp.int32).at[order[jnp.where(places < fixed, places, moved)]].set(jnp.asarray(tallies, jnp.int32))

    tallies = jnp.where(number % 4 == 0, named(packed, number // 4), named(ordinary, number - number // 4 - 1))
    mixed = jax.random.permutation(jax.random.fold_in(own, 3), amount)
    source_of, sink = mixed[0:amount // 2 * 2:2], mixed[1:amount // 2 * 2:2]
    margin = jnp.minimum(tallies[source_of] - 1, reach - tallies[sink]) // 2
    margin = jnp.where((source_of == order[0]) | (sink == order[0]) | (tallies[sink] == 0), 0, jnp.maximum(margin, 0))
    moved = jax.random.randint(jax.random.fold_in(own, 4), (amount // 2,), 0, 1 << 20) % (margin + 1)
    tallies = tallies.at[source_of].add(-moved).at[sink].add(moved)
    members = jnp.searchsorted(jnp.cumsum(tallies), jnp.arange(rows * top), side="right").astype(jnp.int32)
    listing = members.reshape(top, rows).T
    listing = listing[jax.random.permutation(jax.random.fold_in(own, 1), rows)]
    turn = jax.random.randint(jax.random.fold_in(own, 2), (rows, 1), 0, top)
    return jnp.take_along_axis(listing, (jnp.arange(top)[None, :] + turn) % top, axis=1)


def shares(count, total, limit, slope, full):
    weights = [(1 << 20) // math.isqrt(rank ** slope) + 1 for rank in range(1, count + 1)]
    largest = limit if full else min(limit, max(-(-total // count), total * weights[0] // sum(weights)))
    least = 1 if total - largest >= count - 1 else 0
    counts, rest = [largest] + [least] * (count - 1), total - largest - least * (count - 1)
    while rest > 0:
        movable = [i for i in range(1, count) if counts[i] < largest] or [i for i in range(1, count) if counts[i] < limit]
        whole, left = sum([weights[i] for i in movable]), rest
        for i in movable:
            addition = min(limit - counts[i], max(1, left * weights[i] // whole), rest)
            counts[i] = counts[i] + addition
            rest = rest - addition
    return np.array(counts)


def setup_inputs(seed: int = 0) -> dict:
    streams_of = jax.random.split(jax.random.key(seed), 6)
    state = draw_state(jax.random.fold_in(streams_of[5], 71), 0)
    neighbours = draw_neighbours(jax.random.fold_in(streams_of[5], 71), 0)
    metric = jnp.clip(jnp.exp(math.log(4.0) - 2.0794415 * jax.random.uniform(streams_of[2], (ELEMS,), jnp.float32) ** block_scale(streams_of[2], (ELEMS,), ((0, 128),), -0.2, 0.2)), 0.5, 4.0)
    flags = with_ends((jax.random.randint(streams_of[3], (ELEMS,), 0, 4) < 1).astype(jnp.int32), jax.random.fold_in(streams_of[3], 1), 0, 1)
    new_owner_keys = jax.random.split(jax.random.fold_in(streams_of[4], 1), ELEMS // E_DEV)
    new_owner_turns = jax.random.permutation(jax.random.fold_in(streams_of[4], 3), ELEMS // E_DEV)
    new_owner = jax.vmap(lambda own, number: shared_out(jax.random.fold_in(streams_of[4], 2), own, number, E_DEV, N_CURVE, 1, SLOTS, 1))(new_owner_keys, new_owner_turns).reshape((ELEMS, 1))
    return {"state": state, "neighbours": neighbours, "metric": metric, "flags": flags, "new_owner": new_owner}


lgl_nodes = np.array([-1.0, -0.8717401485096066, -0.5917001814331423, -0.2092992179024789, 0.2092992179024789, 0.5917001814331423, 0.8717401485096066, 1.0])
end_weight = 1.0 / 28.0
earth_pressure = 1.2
friction = 0.4
slope_x = 0.3
slope_y = 0.1
time_step = 0.01
face_nodes = np.array([[8 * r for r in range(8)], [8 * r + 7 for r in range(8)], [r for r in range(8)], [56 + r for r in range(8)]])
opposite = [1, 0, 3, 2]
outward = [-1.0, 1.0, -1.0, 1.0]

def lagrange_table(points):
    values_table = np.ones((len(points), 8))
    for j in range(8):
        for m in range(8):
            if m != j:
                values_table[:, j] = values_table[:, j] * (points - lgl_nodes[m]) / (lgl_nodes[j] - lgl_nodes[m])
    return values_table

def basis_tables():
    bary = np.array([1.0 / np.prod([lgl_nodes[j] - lgl_nodes[m] for m in range(8) if m != j]) for j in range(8)])
    derivative = np.zeros((8, 8))
    for i in range(8):
        for j in range(8):
            if i != j:
                derivative[i, j] = bary[j] / bary[i] / (lgl_nodes[i] - lgl_nodes[j])
        derivative[i, i] = -np.sum(derivative[i])
    identity = np.eye(8)
    lower_half = lagrange_table((lgl_nodes - 1.0) / 2.0)
    upper_half = lagrange_table((lgl_nodes + 1.0) / 2.0)
    halves = [lower_half, upper_half]
    prolong = np.stack([np.kron(halves[row_half], halves[col_half]) for row_half in range(2) for col_half in range(2)])
    return (jnp.asarray(np.kron(identity, derivative), jnp.float32), jnp.asarray(np.kron(derivative, identity), jnp.float32), jnp.asarray(prolong, jnp.float32))

def face_flux(values, face_id):
    depth_field = values[0]
    moment_x = values[1]
    moment_y = values[2]
    speed_x = moment_x / depth_field
    speed_y = moment_y / depth_field
    pressure = 0.5 * earth_pressure * depth_field * depth_field
    if face_id < 2:
        normal = speed_x
        flux_term = jnp.stack([moment_x, moment_x * speed_x + pressure, moment_y * speed_x])
    else:
        normal = speed_y
        flux_term = jnp.stack([moment_y, moment_x * speed_y, moment_y * speed_y + pressure])
    return (outward[face_id] * flux_term, jnp.abs(normal) + jnp.sqrt(earth_pressure * depth_field))

def mirror(values, face_id):
    if face_id < 2:
        return jnp.stack([values[0], -values[1], values[2]])
    return jnp.stack([values[0], values[1], -values[2]])

def tendency(fields, metric, outsides, deriv_x, deriv_y):
    depth_field = fields[0]
    moment_x = fields[1]
    moment_y = fields[2]
    speed_x = moment_x / depth_field
    speed_y = moment_y / depth_field
    pressure = 0.5 * earth_pressure * depth_field * depth_field
    flux_x = jnp.stack([moment_x, moment_x * speed_x + pressure, moment_y * speed_x])
    flux_y = jnp.stack([moment_y, moment_x * speed_y, moment_y * speed_y + pressure])
    volume = jnp.einsum('ab,fbe->fae', deriv_x, flux_x, precision=lax.Precision.HIGHEST) + jnp.einsum('ab,fbe->fae', deriv_y, flux_y, precision=lax.Precision.HIGHEST)
    magnitude = jnp.sqrt(speed_x * speed_x + speed_y * speed_y + 1.0)
    source = jnp.stack([jnp.zeros_like(depth_field), depth_field * (slope_x - friction * speed_x / magnitude), depth_field * (slope_y - friction * speed_y / magnitude)])
    scale_row = metric[None, None, :]
    result = source - scale_row * volume
    for face_id in range(4):
        inside = fields[:, face_nodes[face_id], :]
        flux_in, wave_in = face_flux(inside, face_id)
        flux_out, wave_out = face_flux(outsides[face_id], face_id)
        largest = jnp.maximum(wave_in, wave_out)
        star = 0.5 * (flux_in + flux_out) - 0.5 * largest[None] * (outsides[face_id] - inside)
        result = result.at[:, face_nodes[face_id], :].add(scale_row / end_weight * (flux_in - star))
    return result

def make_children(fields, flag_values, prolong):
    prolonged = jnp.einsum('cab,fbe->cfae', prolong, fields, precision=lax.Precision.HIGHEST)
    empty_field = jnp.zeros_like(fields)
    unchanged = jnp.stack([fields, empty_field, empty_field, empty_field])
    return jnp.where((flag_values == 1)[None, None, None, :], prolonged, unchanged)

def slot_columns(destination, devices_count, slots):
    hits_table = (destination[:, None] == jnp.arange(devices_count, dtype=jnp.int32)[None, :]).astype(jnp.int32)
    before = lax.optimization_barrier(jnp.sum(jnp.cumsum(hits_table, axis=0) * hits_table, axis=1)) - 1
    return destination * slots + before

def reference(state, neighbours, metric, flags, new_owner):
    deriv_x, deriv_y, prolong = basis_tables()
    outsides = []
    for face_id in range(4):
        partner = neighbours[face_id]
        across = state[:, face_nodes[opposite[face_id]], :][:, :, jnp.maximum(partner, 0)]
        own_trace = state[:, face_nodes[face_id], :]
        outsides.append(jnp.where(partner[None, None, :] < 0, mirror(own_trace, face_id), across))
    stepped = state + time_step * tendency(state, metric, outsides, deriv_x, deriv_y)

    def place_block(source, output):
        start = (source * E_DEV).astype(jnp.int32)
        fields = lax.dynamic_slice_in_dim(stepped, start, E_DEV, 2)
        flag_values = lax.dynamic_slice_in_dim(flags, start, E_DEV, 0)
        destination = lax.dynamic_slice_in_dim(new_owner[:, 0], start, E_DEV, 0)
        local_cols = slot_columns(destination, N_CURVE, SLOTS)
        columns = (destination * (N_CURVE * SLOTS - SLOTS) + local_cols + source * SLOTS).astype(jnp.int32)
        children = make_children(fields, flag_values, prolong)
        return output.at[:, :, :, columns].set(children)
    start_out = jnp.zeros((4, FIELDS, NODES, RECV), jnp.float32)
    return lax.fori_loop(0, N_CURVE, place_block, start_out)
```

```python
import random

import jax
import jax.numpy as jnp
import numpy as np
from jax import lax
from jax.experimental import pallas as pl
from jax.experimental.pallas import tpu as pltpu
from jax.sharding import PartitionSpec as P

lgl_nodes = np.array(
    [
        -1.0,
        -0.8717401485096066,
        -0.5917001814331423,
        -0.2092992179024789,
        0.2092992179024789,
        0.5917001814331423,
        0.8717401485096066,
        1.0,
    ]
)
lift_weight = 28.0
earth_pressure = 1.2
friction = 0.4
slope_x = 0.3
slope_y = 0.1
time_step = 0.01
face_nodes = np.array(
    [
        [8 * r for r in range(8)],
        [8 * r + 7 for r in range(8)],
        [r for r in range(8)],
        [56 + r for r in range(8)],
    ]
)
inner_nodes = np.array([8 * iy + ix for iy in range(1, 7) for ix in range(1, 7)])
opposite = [1, 0, 3, 2]
outward = [-1.0, 1.0, -1.0, 1.0]

DEVICES = 128
ELEMS = 512
SLOTS = 8
LANES = 128
INNER = 40
OUTER = 32
FLAG_ROW = 3 * INNER
MESH = pl.DeviceIdType.MESH
bf16 = jnp.bfloat16
f32 = jnp.float32


def lagrange_table(points):
    values_table = np.ones((len(points), 8))
    for j in range(8):
        for m in range(8):
            if m != j:
                values_table[:, j] = (
                    values_table[:, j] * (points - lgl_nodes[m]) / (lgl_nodes[j] - lgl_nodes[m])
                )
    return values_table


def basis_tables():
    bary = np.array(
        [1.0 / np.prod([lgl_nodes[j] - lgl_nodes[m] for m in range(8) if m != j]) for j in range(8)]
    )
    derivative = np.zeros((8, 8))
    for i in range(8):
        for j in range(8):
            if i != j:
                derivative[i, j] = bary[j] / bary[i] / (lgl_nodes[i] - lgl_nodes[j])
        derivative[i, i] = -np.sum(derivative[i])
    identity = np.eye(8)
    lower_half = lagrange_table((lgl_nodes - 1.0) / 2.0)
    upper_half = lagrange_table((lgl_nodes + 1.0) / 2.0)
    halves = [lower_half, upper_half]
    prolong = np.stack(
        [
            np.kron(halves[row_half], halves[col_half])
            for row_half in range(2)
            for col_half in range(2)
        ]
    )
    return np.kron(identity, derivative), np.kron(derivative, identity), prolong


def two_parts(table):
    high = np.asarray(table, np.float32).astype(bf16)
    low = (np.asarray(table, np.float64) - high.astype(np.float64)).astype(bf16)
    return high, low


def corner_copy(face_id, r):
    return face_id < 2 and r in (0, 7)


def step_table():
    deriv_x, deriv_y, _ = basis_tables()
    full = np.concatenate([np.eye(64), deriv_x, deriv_y], axis=1)
    table = np.zeros((INNER + OUTER, 192))
    table[:36] = full[inner_nodes]
    for face_id in range(4):
        for r in range(8):
            if not corner_copy(face_id, r):
                table[INNER + 8 * face_id + r] = full[face_nodes[face_id][r]]
    high, low = two_parts(table)
    return np.concatenate([high, high, low[:, 64:]], axis=1)


def child_table():
    _, _, prolong = basis_tables()
    rows = np.concatenate([prolong.reshape(256, 64), np.eye(64)], axis=0)
    table = np.zeros((5, 3, 64, 2 * LANES))
    for field in range(3):
        block = np.zeros((5 * 64, 2 * LANES))
        block[:, INNER * field : INNER * field + 36] = rows[:, inner_nodes]
        for face_id in range(4):
            for r in range(8):
                at = LANES + OUTER * field + 8 * face_id + r
                block[:, at] = rows[:, face_nodes[face_id][r]]
        table[:, field] = block.reshape(5, 64, 2 * LANES)
    flag = np.zeros((8, 2 * LANES))
    flag[0, FLAG_ROW] = 1.0
    high, low = two_parts(np.concatenate([table.reshape(960, 2 * LANES), flag], axis=0))
    return high, low[:768]


def send_order():
    order = [
        (z, y, x, c) for z in range(4) for y in range(4) for x in range(4) for c in range(2)
    ][1:]
    random.Random(0).shuffle(order)
    order.sort(key=lambda d: -sum(min(v, 4 - v) for v in d[:3]))
    return order


def split2(values):
    high = values.astype(bf16)
    return high, (values - high.astype(f32)).astype(bf16)


def face_flux(values, face_id):
    depth, moment_x, moment_y = values
    inv = 1.0 / depth
    pressure = 0.5 * earth_pressure * depth * depth
    sign = outward[face_id]
    if face_id < 2:
        normal = moment_x * inv
        terms = [moment_x, moment_x * normal + pressure, moment_y * normal]
    else:
        normal = moment_y * inv
        terms = [moment_y, moment_x * normal, moment_y * normal + pressure]
    return [sign * t for t in terms], jnp.abs(normal) + jnp.sqrt(earth_pressure * depth)


def mirror(values, face_id):
    if face_id < 2:
        return [values[0], -values[1], values[2]]
    return [values[0], values[1], -values[2]]


def step_kernel(
    state, neighbours, metric, flags, owner, table,
    inner_in, outer_in,
    tiles, trace, ghost, inner_out, outer_out, onehot,
    halo_send, halo_recv, inner_send, inner_recv, outer_send, outer_recv, own_sem,
):
    me = lax.axis_index("curve")
    mz, my, mx, mc = me // 32, (me // 8) % 4, (me // 2) % 4, me % 2
    order = send_order()

    def device_at(d):
        z, y, x, c = d
        return (
            ((lax.rem(mz + z, 4) * 4 + lax.rem(my + y, 4)) * 4 + lax.rem(mx + x, 4)) * 2
            + lax.rem(mc + c, 2)
        )

    barrier = pltpu.get_barrier_semaphore()
    for d in order:
        pl.semaphore_signal(barrier, inc=1, device_id=(device_at(d),), device_id_type=MESH)

    for t in range(ELEMS // LANES):
        tiles[192 * t : 192 * t + 192, :] = state[:, LANES * t : LANES * t + LANES]
    for face_id in range(4):
        for field in range(3):
            at = (face_id % 2) * 24 + field * 8
            if face_id < 2:
                for t in range(ELEMS // LANES):
                    start = 192 * t + 64 * field + 7 * face_id
                    trace[0, at : at + 8, LANES * t : LANES * t + LANES] = tiles[
                        pl.ds(start, 8, stride=8), :
                    ]
            else:
                start = 64 * field + 56 * (face_id - 2)
                trace[1, at : at + 8, :] = state[start : start + 8, :]

    scale = (-time_step) * metric[...]
    depth, moment_x, moment_y = (state[64 * f : 64 * f + 64, :] for f in range(3))
    inv = 1.0 / depth
    speed_x, speed_y = moment_x * inv, moment_y * inv
    pressure = 0.5 * earth_pressure * depth * depth
    drag = friction / jnp.sqrt(speed_x * speed_x + speed_y * speed_y + 1.0)
    cross = moment_x * speed_y
    parts = [
        (depth, moment_x, moment_y),
        (
            moment_x + time_step * (depth * (slope_x - drag * speed_x)),
            moment_x * speed_x + pressure,
            cross,
        ),
        (
            moment_y + time_step * (depth * (slope_y - drag * speed_y)),
            cross,
            moment_y * speed_y + pressure,
        ),
    ]
    stepped = []
    for q, flux_x, flux_y in parts:
        q_high, q_low = split2(q)
        x_high, x_low = split2(scale * flux_x)
        y_high, y_low = split2(scale * flux_y)
        operand = jnp.concatenate(
            [q_high, x_high, y_high, q_low, x_low, y_low, x_high, y_high], axis=0
        )
        stepped.append(jnp.dot(table[...], operand, preferred_element_type=f32))

    owners = owner[...]
    hits = owners == lax.broadcasted_iota(jnp.int32, (DEVICES, ELEMS), 0)
    earlier = lax.broadcasted_iota(jnp.int32, (ELEMS, ELEMS), 0) < lax.broadcasted_iota(
        jnp.int32, (ELEMS, ELEMS), 1
    )
    hits = jnp.where(hits, 1.0, 0.0)
    before = jnp.dot(
        hits.astype(bf16),
        jnp.where(earlier, 1.0, 0.0).astype(bf16),
        preferred_element_type=f32,
    )
    rank = jnp.sum(hits * before, axis=0, keepdims=True)
    column = owners * SLOTS + rank.astype(jnp.int32)
    slot_rows = lax.broadcasted_iota(jnp.int32, (DEVICES * SLOTS, ELEMS), 0)
    onehot[...] = jnp.where(slot_rows == column, 1.0, 0.0).astype(bf16)

    def place(rows, target):
        high, low = split2(rows)
        both = lax.dot_general(
            onehot[...],
            jnp.concatenate([high, low], axis=0),
            (((1,), (1,)), ((), ())),
            preferred_element_type=f32,
        )
        placed = both[:, :LANES] + both[:, LANES:]
        target[...] = placed.reshape(DEVICES, SLOTS, LANES)

    flag_rows = jnp.where(
        lax.broadcasted_iota(jnp.int32, (8, ELEMS), 0) == 0, flags[...].astype(f32), 0.0
    )
    place(jnp.concatenate([s[:INNER] for s in stepped] + [flag_rows], axis=0), inner_out)

    pl.semaphore_wait(barrier, DEVICES - 1)

    def halo(pair, above):
        distance = 32 if pair else 1
        target = lax.rem(me + (distance if above else DEVICES - distance), DEVICES)
        side = 0 if above else 1
        return pltpu.make_async_remote_copy(
            src_ref=trace.at[pair],
            dst_ref=ghost.at[pair, side],
            send_sem=halo_send.at[pair, side],
            recv_sem=halo_recv.at[pair, side],
            device_id=(target,),
            device_id_type=MESH,
        )

    halos = [halo(pair, above) for pair in (0, 1) for above in (True, False)]
    for copy in halos:
        copy.start()

    def exchange(source, target, send_sem, recv_sem):
        for d in order:
            to = device_at(d)
            pltpu.make_async_remote_copy(
                src_ref=source.at[to],
                dst_ref=target.at[me],
                send_sem=send_sem,
                recv_sem=recv_sem,
                device_id=(to,),
                device_id_type=MESH,
            ).start()

    exchange(inner_out, inner_in, inner_send, inner_recv)
    own_inner = pltpu.make_async_copy(inner_out.at[me], inner_in.at[me], own_sem.at[0])
    own_inner.start()

    for copy in halos:
        copy.wait()

    lift_scale = (time_step * lift_weight * 0.5) * metric[...]
    lifted = [[None] * 4 for _ in range(3)]
    for face_id in range(4):
        pair, distance = (0, 1) if face_id < 2 else (1, 32)
        partner = neighbours[face_id : face_id + 1, :]
        wall = partner < 0
        home = lax.shift_right_arithmetic(partner, 9)
        local = jnp.bitwise_and(partner, ELEMS - 1)
        side = jnp.where(home == me, 0, jnp.where(home == me - distance, 1, 2))
        piece = side * 4 + lax.shift_right_arithmetic(local, 7)
        lane = jnp.bitwise_and(local, LANES - 1)
        at = (opposite[face_id] % 2) * 24
        across = [[], [], []]
        for t in range(ELEMS // LANES):
            cols = slice(t * LANES, (t + 1) * LANES)
            index = jnp.broadcast_to(lane[:, cols], (8, LANES))
            piece_t = jnp.broadcast_to(piece[:, cols], (8, LANES))
            found = [None, None, None]
            for c in range(12):
                there = slice((c % 4) * LANES, (c % 4 + 1) * LANES)
                mask = piece_t == c
                for field in range(3):
                    rows = slice(at + field * 8, at + field * 8 + 8)
                    if c < 4:
                        values = trace[pair, rows, there]
                    else:
                        values = ghost[pair, c // 4 - 1, rows, there]
                    got = jnp.take_along_axis(values, index, axis=1, mode="promise_in_bounds")
                    found[field] = got if c == 0 else jnp.where(mask, got, found[field])
            for field in range(3):
                across[field].append(found[field])
        at = (face_id % 2) * 24
        inside = [trace[pair, at + 8 * field : at + 8 * field + 8, :] for field in range(3)]
        outside = [
            jnp.where(wall, m, jnp.concatenate(a, axis=1))
            for m, a in zip(mirror(inside, face_id), across)
        ]
        flux_in, wave_in = face_flux(inside, face_id)
        flux_out, wave_out = face_flux(outside, face_id)
        largest = jnp.maximum(wave_in, wave_out)
        for field in range(3):
            jump = flux_in[field] - flux_out[field]
            lifted[field][face_id] = lift_scale * (
                jump + largest * (outside[field] - inside[field])
            )
    outer = [
        stepped[field][INNER:] + jnp.concatenate(lifted[field], axis=0) for field in range(3)
    ]
    place(jnp.concatenate(outer + [jnp.zeros((32, ELEMS), f32)], axis=0), outer_out)

    exchange(outer_out, outer_in, outer_send, outer_recv)
    own_outer = pltpu.make_async_copy(outer_out.at[me], outer_in.at[me], own_sem.at[1])
    own_outer.start()

    def wait_all(source, target, send_sem, recv_sem):
        others = pl.ds(0, DEVICES - 1)
        copies = pltpu.make_async_remote_copy(
            src_ref=source.at[others],
            dst_ref=target.at[others],
            send_sem=send_sem,
            recv_sem=recv_sem,
            device_id=(me,),
            device_id_type=MESH,
        )
        copies.wait_send()
        copies.wait_recv()

    own_inner.wait()
    own_outer.wait()
    wait_all(inner_out, inner_in, inner_send, inner_recv)
    wait_all(outer_out, outer_in, outer_send, outer_recv)


def child_kernel(inner, outer, high_table, low_table, out):
    columns = inner.shape[0]
    inner_high, inner_low = split2(inner[...])
    outer_high, outer_low = split2(outer[...])
    high = jnp.concatenate([inner_high, outer_high], axis=1)
    low = jnp.concatenate([inner_low, outer_low], axis=1)
    dims = (((1,), (1,)), ((), ()))
    main = lax.dot_general(
        high_table[...], high, dims, preferred_element_type=f32
    ) + lax.dot_general(high_table[...], low, dims, preferred_element_type=f32)
    fine = lax.dot_general(low_table[...], high, dims, preferred_element_type=f32)
    refined = jnp.broadcast_to(main[960:961] > 0.5, (192, columns))
    out[0:192, :] = jnp.where(refined, main[0:192] + fine[0:192], main[768:960])
    for c in range(1, 4):
        rows = slice(192 * c, 192 * c + 192)
        out[rows, :] = jnp.where(refined, main[rows] + fine[rows], 0.0)


def on_device(state, neighbours, metric, flags, new_owner):
    vmem = pl.BlockSpec(memory_space=pltpu.VMEM)
    hbm = pl.BlockSpec(memory_space=pl.ANY)
    block = jax.ShapeDtypeStruct((DEVICES, SLOTS, LANES), f32)
    buffer = pltpu.VMEM((DEVICES, SLOTS, LANES), f32)
    dma = pltpu.SemaphoreType.DMA
    inner, outer = pl.pallas_call(
        step_kernel,
        out_shape=(block, block),
        in_specs=[vmem] * 6,
        out_specs=(hbm, hbm),
        scratch_shapes=[
            pltpu.VMEM((192 * ELEMS // LANES, LANES), f32),
            pltpu.VMEM((2, 48, ELEMS), f32),
            pltpu.VMEM((2, 2, 48, ELEMS), f32),
            buffer,
            buffer,
            pltpu.VMEM((DEVICES * SLOTS, ELEMS), bf16),
            dma((2, 2)),
            dma((2, 2)),
            dma,
            dma,
            dma,
            dma,
            dma((2,)),
        ],
        compiler_params=pltpu.CompilerParams(collective_id=0, has_side_effects=True),
        name="step_and_migrate",
    )(
        state.reshape(192, ELEMS),
        neighbours,
        metric.reshape(1, ELEMS),
        flags.reshape(1, ELEMS),
        new_owner.reshape(1, ELEMS),
        jnp.asarray(step_table(), bf16),
    )
    slots = DEVICES * SLOTS
    tile = 256
    high_table, low_table = child_table()
    children = pl.pallas_call(
        child_kernel,
        grid=(slots // tile,),
        out_shape=jax.ShapeDtypeStruct((768, slots), f32),
        in_specs=[
            pl.BlockSpec((tile, LANES), lambda i: (i, 0)),
            pl.BlockSpec((tile, LANES), lambda i: (i, 0)),
            pl.BlockSpec((968, 2 * LANES), lambda i: (0, 0)),
            pl.BlockSpec((768, 2 * LANES), lambda i: (0, 0)),
        ],
        out_specs=pl.BlockSpec((768, tile), lambda i: (0, i)),
        name="make_children",
    )(
        inner.reshape(slots, LANES),
        outer.reshape(slots, LANES),
        jnp.asarray(high_table, bf16),
        jnp.asarray(low_table, bf16),
    )
    return children.reshape(4, 3, 64, slots)


def solution(mesh):
    placed = (P(None, None, "curve"), P(None, "curve"), P("curve"), P("curve"), P("curve", None))
    return jax.shard_map(
        on_device,
        mesh=mesh,
        in_specs=placed,
        out_specs=P(None, None, None, "curve"),
        check_vma=False,
    )
```

```python
import random

import jax
import jax.numpy as jnp
import numpy as np
from jax import lax
from jax.experimental import pallas as pl
from jax.experimental.pallas import tpu as pltpu
from jax.sharding import PartitionSpec as P

lgl_nodes = np.array(
    [
        -1.0,
        -0.8717401485096066,
        -0.5917001814331423,
        -0.2092992179024789,
        0.2092992179024789,
        0.5917001814331423,
        0.8717401485096066,
        1.0,
    ]
)
lift_weight = 28.0
earth_pressure = 1.2
friction = 0.4
slope_x = 0.3
slope_y = 0.1
time_step = 0.01
face_nodes = np.array(
    [
        [8 * r for r in range(8)],
        [8 * r + 7 for r in range(8)],
        [r for r in range(8)],
        [56 + r for r in range(8)],
    ]
)
inner_nodes = np.array([8 * iy + ix for iy in range(1, 7) for ix in range(1, 7)])
opposite = [1, 0, 3, 2]
outward = [-1.0, 1.0, -1.0, 1.0]

DEVICES = 128
ELEMS = 512
SLOTS = 8
LANES = 128
INNER = 40
OUTER = 32
FLAG_ROW = 3 * INNER
CROSS = 32
NAME_BASE = 2
MESH = pl.DeviceIdType.MESH
bf16 = jnp.bfloat16
f32 = jnp.float32


def lagrange_table(points):
    values_table = np.ones((len(points), 8))
    for j in range(8):
        for m in range(8):
            if m != j:
                values_table[:, j] = (
                    values_table[:, j] * (points - lgl_nodes[m]) / (lgl_nodes[j] - lgl_nodes[m])
                )
    return values_table


def basis_tables():
    bary = np.array(
        [1.0 / np.prod([lgl_nodes[j] - lgl_nodes[m] for m in range(8) if m != j]) for j in range(8)]
    )
    derivative = np.zeros((8, 8))
    for i in range(8):
        for j in range(8):
            if i != j:
                derivative[i, j] = bary[j] / bary[i] / (lgl_nodes[i] - lgl_nodes[j])
        derivative[i, i] = -np.sum(derivative[i])
    identity = np.eye(8)
    lower_half = lagrange_table((lgl_nodes - 1.0) / 2.0)
    upper_half = lagrange_table((lgl_nodes + 1.0) / 2.0)
    halves = [lower_half, upper_half]
    prolong = np.stack(
        [
            np.kron(halves[row_half], halves[col_half])
            for row_half in range(2)
            for col_half in range(2)
        ]
    )
    return np.kron(identity, derivative), np.kron(derivative, identity), prolong


def two_parts(table):
    high = np.asarray(table, np.float32).astype(bf16)
    low = (np.asarray(table, np.float64) - high.astype(np.float64)).astype(bf16)
    return high, low


def corner_copy(face_id, r):
    return face_id < 2 and r in (0, 7)


def step_table():
    deriv_x, deriv_y, _ = basis_tables()
    full = np.concatenate([np.eye(64), deriv_x, deriv_y], axis=1)
    table = np.zeros((INNER + OUTER, 192))
    table[:36] = full[inner_nodes]
    for face_id in range(4):
        for r in range(8):
            if not corner_copy(face_id, r):
                table[INNER + 8 * face_id + r] = full[face_nodes[face_id][r]]
    high, low = two_parts(table)
    return np.concatenate([high, high, low[:, 64:]], axis=1)


def child_table():
    _, _, prolong = basis_tables()
    rows = np.concatenate([prolong.reshape(256, 64), np.eye(64)], axis=0)
    table = np.zeros((5, 3, 64, 2 * LANES))
    for field in range(3):
        block = np.zeros((5 * 64, 2 * LANES))
        block[:, INNER * field : INNER * field + 36] = rows[:, inner_nodes]
        for face_id in range(4):
            for r in range(8):
                at = LANES + OUTER * field + 8 * face_id + r
                block[:, at] = rows[:, face_nodes[face_id][r]]
        table[:, field] = block.reshape(5, 64, 2 * LANES)
    flag = np.zeros((8, 2 * LANES))
    flag[0, FLAG_ROW] = 1.0
    high, low = two_parts(np.concatenate([table.reshape(960, 2 * LANES), flag], axis=0))
    return high, low[:768]


def send_order():
    order = [
        (z, y, x, c) for z in range(4) for y in range(4) for x in range(4) for c in range(2)
    ][1:]
    random.Random(0).shuffle(order)
    order.sort(key=lambda d: -sum(min(v, 4 - v) for v in d[:3]))
    return order


def split2(values):
    high = values.astype(bf16)
    return high, (values - high.astype(f32)).astype(bf16)


def face_flux(values, face_id):
    depth, moment_x, moment_y = values
    inv = 1.0 / depth
    pressure = 0.5 * earth_pressure * depth * depth
    sign = outward[face_id]
    if face_id < 2:
        normal = moment_x * inv
        terms = [moment_x, moment_x * normal + pressure, moment_y * normal]
    else:
        normal = moment_y * inv
        terms = [moment_y, moment_x * normal, moment_y * normal + pressure]
    return [sign * t for t in terms], jnp.abs(normal) + jnp.sqrt(earth_pressure * depth)


def mirror(values, face_id):
    if face_id < 2:
        return [values[0], -values[1], values[2]]
    return [values[0], values[1], -values[2]]


def step_kernel(
    state_in, neighbours_in, metric_in, flags_in, owner_in, table_in,
    inner_in, outer_in,
    state, neighbours, metric, flags, owner, table,
    tiles, trace, own_flux, across, crossing, ghost, inner_out, outer_out, onehot,
    load_sem, halo_send, halo_recv, inner_send, inner_recv, outer_send, outer_recv, own_sem,
):
    pairs = (
        (state_in, state), (neighbours_in, neighbours), (metric_in, metric),
        (flags_in, flags), (owner_in, owner), (table_in, table),
    )
    loads = [pltpu.make_async_copy(a, b, load_sem.at[i]) for i, (a, b) in enumerate(pairs)]
    for load in loads:
        load.start()

    me = lax.axis_index("curve")
    order = send_order()
    z_part = [lax.rem(me // 32 + z, 4) * 32 for z in range(4)]
    y_part = [lax.rem((me // 8) % 4 + y, 4) * 8 for y in range(4)]
    x_part = [lax.rem((me // 2) % 4 + x, 4) * 2 for x in range(4)]
    c_part = [lax.rem(me % 2 + c, 2) for c in range(2)]
    zy_part = [[z + y for y in y_part] for z in z_part]
    xc_part = [[x + c for c in c_part] for x in x_part]
    others = [zy_part[z][y] + xc_part[x][c] for z, y, x, c in order]

    barrier = pltpu.get_barrier_semaphore()
    for to in others:
        pl.semaphore_signal(barrier, inc=1, device_id=(to,), device_id_type=MESH)
    for load in loads:
        load.wait()

    partners = neighbours[...]
    distance = jnp.where(lax.broadcasted_iota(jnp.int32, (4, ELEMS), 0) < 2, 1, 32)
    homes = lax.shift_right_arithmetic(partners, 9)
    real = partners >= 0
    below = jnp.where(real & (homes == me - distance), 1.0, 0.0)
    above = jnp.where(real & (homes == me + distance), 1.0, 0.0)
    owners = owner[...]
    hits = owners == lax.broadcasted_iota(jnp.int32, (DEVICES, ELEMS), 0)
    hits = jnp.where(hits, 1.0, 0.0)
    earlier = lax.broadcasted_iota(jnp.int32, (ELEMS, ELEMS), 0) < lax.broadcasted_iota(
        jnp.int32, (ELEMS, ELEMS), 1
    )
    nothing = jnp.zeros((4, ELEMS), f32)
    before = jnp.dot(
        jnp.concatenate([hits, below, nothing, above, nothing], axis=0).astype(bf16),
        jnp.where(earlier, 1.0, 0.0).astype(bf16),
        preferred_element_type=f32,
    )
    rank = jnp.sum(hits * before[:DEVICES], axis=0, keepdims=True)
    column = owners * SLOTS + rank.astype(jnp.int32)
    slot_rows = lax.broadcasted_iota(jnp.int32, (DEVICES * SLOTS, ELEMS), 0)
    onehot[...] = jnp.where(slot_rows == column, 1.0, 0.0).astype(bf16)
    spot = jnp.where(
        below > 0.5,
        before[DEVICES : DEVICES + 4],
        jnp.where(above > 0.5, before[DEVICES + 8 : DEVICES + 12] + CROSS, -1000.0),
    ).astype(jnp.int32)

    for t in range(ELEMS // LANES):
        tiles[192 * t : 192 * t + 192, :] = state[:, LANES * t : LANES * t + LANES]
    for face_id in range(4):
        for field in range(3):
            at = (face_id % 2) * 24 + field * 8
            if face_id < 2:
                for t in range(ELEMS // LANES):
                    start = 192 * t + 64 * field + 7 * face_id
                    trace[0, at : at + 8, LANES * t : LANES * t + LANES] = tiles[
                        pl.ds(start, 8, stride=8), :
                    ]
            else:
                start = 64 * field + 56 * (face_id - 2)
                trace[1, at : at + 8, :] = state[start : start + 8, :]

    first_row = lax.broadcasted_iota(jnp.int32, (8, ELEMS), 0) == 0
    name = (
        lax.broadcasted_iota(jnp.int32, (8, ELEMS), 1) + (me * ELEMS + NAME_BASE)
    ).astype(f32)
    name = jnp.where(first_row, name, 0.0)
    lane_rows = lax.broadcasted_iota(jnp.int32, (LANES, ELEMS), 0)
    nt_dims = (((1,), (1,)), ((), ()))
    for pair in (0, 1):
        packed = None
        for position in (0, 1):
            face_id = 2 * pair + position
            rows = jnp.concatenate([trace[pair, 24 * position : 24 * position + 24, :], name])
            chosen = lane_rows == spot[face_id : face_id + 1] + 2 * CROSS * position
            part = lax.dot_general(
                jnp.concatenate(split2(rows), axis=0),
                jnp.where(chosen, 1.0, 0.0).astype(bf16),
                nt_dims,
                preferred_element_type=f32,
            )
            packed = part if packed is None else packed + part
        crossing[pair] = packed[:32] + packed[32:]

    scale = (-time_step) * metric[...]
    depth, moment_x, moment_y = (state[64 * f : 64 * f + 64, :] for f in range(3))
    inv = 1.0 / depth
    speed_x, speed_y = moment_x * inv, moment_y * inv
    pressure = 0.5 * earth_pressure * depth * depth
    drag = friction / jnp.sqrt(speed_x * speed_x + speed_y * speed_y + 1.0)
    cross = moment_x * speed_y
    parts = [
        (depth, moment_x, moment_y),
        (
            moment_x + time_step * (depth * (slope_x - drag * speed_x)),
            moment_x * speed_x + pressure,
            cross,
        ),
        (
            moment_y + time_step * (depth * (slope_y - drag * speed_y)),
            cross,
            moment_y * speed_y + pressure,
        ),
    ]
    stepped = []
    for q, flux_x, flux_y in parts:
        q_high, q_low = split2(q)
        x_high, x_low = split2(scale * flux_x)
        y_high, y_low = split2(scale * flux_y)
        operand = jnp.concatenate(
            [q_high, x_high, y_high, q_low, x_low, y_low, x_high, y_high], axis=0
        )
        stepped.append(jnp.dot(table[...], operand, preferred_element_type=f32))

    def place(rows, target):
        both = lax.dot_general(
            onehot[...],
            jnp.concatenate(split2(rows), axis=0),
            nt_dims,
            preferred_element_type=f32,
        )
        placed = both[:, :LANES] + both[:, LANES:]
        target[...] = placed.reshape(DEVICES, SLOTS, LANES)

    flag_rows = jnp.where(first_row, flags[...].astype(f32), 0.0)
    place(jnp.concatenate([s[:INNER] for s in stepped] + [flag_rows], axis=0), inner_out)

    for face_id in range(4):
        pair = face_id // 2
        at = (face_id % 2) * 24
        inside = [trace[pair, at + 8 * field : at + 8 * field + 8, :] for field in range(3)]
        flux_in, wave_in = face_flux(inside, face_id)
        for i, values in enumerate(flux_in + [wave_in]):
            own_flux[face_id, 8 * i : 8 * i + 8, :] = values
        partner = partners[face_id : face_id + 1]
        local = jnp.bitwise_and(partner, ELEMS - 1)
        piece = lax.shift_right_arithmetic(local, 7)
        lane = jnp.bitwise_and(local, LANES - 1)
        at = (opposite[face_id] % 2) * 24
        for t in range(ELEMS // LANES):
            cols = slice(t * LANES, (t + 1) * LANES)
            index = jnp.broadcast_to(lane[:, cols], (8, LANES))
            piece_t = jnp.broadcast_to(piece[:, cols], (8, LANES))
            for field in range(3):
                rows = slice(at + field * 8, at + field * 8 + 8)
                found = None
                for c in range(ELEMS // LANES):
                    values = trace[pair, rows, c * LANES : (c + 1) * LANES]
                    got = jnp.take_along_axis(values, index, axis=1, mode="promise_in_bounds")
                    found = got if c == 0 else jnp.where(piece_t == c, got, found)
                across[face_id, 8 * field : 8 * field + 8, cols] = found

    pl.semaphore_wait(barrier, DEVICES - 1)

    def halo(pair, upward):
        far = 32 if pair else 1
        target = lax.rem(me + (far if upward else DEVICES - far), DEVICES)
        side = 0 if upward else 1
        return pltpu.make_async_remote_copy(
            src_ref=crossing.at[pair],
            dst_ref=ghost.at[pair, side],
            send_sem=halo_send.at[pair, side],
            recv_sem=halo_recv.at[pair, side],
            device_id=(target,),
            device_id_type=MESH,
        )

    halos = [halo(pair, upward) for pair in (0, 1) for upward in (True, False)]
    for copy in halos:
        copy.start()

    def exchange(source, target, send_sem, recv_sem):
        for to in others:
            pltpu.make_async_remote_copy(
                src_ref=source.at[to],
                dst_ref=target.at[me],
                send_sem=send_sem,
                recv_sem=recv_sem,
                device_id=(to,),
                device_id_type=MESH,
            ).start()

    exchange(inner_out, inner_in, inner_send, inner_recv)
    own_inner = pltpu.make_async_copy(inner_out.at[me], inner_in.at[me], own_sem.at[0])
    own_inner.start()

    for copy in halos:
        copy.wait()

    lift_scale = (time_step * lift_weight * 0.5) * metric[...]
    from_below = jnp.bitwise_and(lax.broadcasted_iota(jnp.int32, (32, LANES), 1), CROSS) != 0
    named = (partners + NAME_BASE).astype(f32)
    lifted = [[None] * 4 for _ in range(3)]
    zeros = jnp.zeros((2 * CROSS, ELEMS), bf16)
    for pair in (0, 1):
        merged = jnp.where(from_below, ghost[pair, 0], ghost[pair, 1])
        names = jnp.transpose(merged[24:32])[:, 0:1]
        chosen = []
        for position in (0, 1):
            face_id = 2 * pair + position
            start = 2 * CROSS * (1 - position)
            match = names[start : start + 2 * CROSS] == named[face_id : face_id + 1]
            match = jnp.where(match, 1.0, 0.0).astype(bf16)
            chosen.append(jnp.concatenate([zeros, match] if start else [match, zeros], axis=0))
        got = jnp.dot(
            jnp.concatenate(split2(merged), axis=0),
            jnp.concatenate(chosen, axis=1),
            preferred_element_type=f32,
        )
        got = got[:32] + got[32:]
        for position in (0, 1):
            face_id = 2 * pair + position
            wall = jnp.logical_not(real[face_id : face_id + 1])
            local = homes[face_id : face_id + 1] == me
            at = position * 24
            inside = [trace[pair, at + 8 * field : at + 8 * field + 8, :] for field in range(3)]
            reflected = mirror(inside, face_id)
            outside = []
            for field in range(3):
                rows = slice(8 * field, 8 * field + 8)
                there = got[rows, ELEMS * position : ELEMS * position + ELEMS]
                there = jnp.where(local, across[face_id, rows, :], there)
                outside.append(jnp.where(wall, reflected[field], there))
            flux_out, wave_out = face_flux(outside, face_id)
            largest = jnp.maximum(own_flux[face_id, 24:32, :], wave_out)
            for field in range(3):
                jump = own_flux[face_id, 8 * field : 8 * field + 8, :] - flux_out[field]
                lifted[field][face_id] = lift_scale * (
                    jump + largest * (outside[field] - inside[field])
                )
    outer = [
        stepped[field][INNER:] + jnp.concatenate(lifted[field], axis=0) for field in range(3)
    ]
    place(jnp.concatenate(outer + [jnp.zeros((32, ELEMS), f32)], axis=0), outer_out)

    exchange(outer_out, outer_in, outer_send, outer_recv)
    own_outer = pltpu.make_async_copy(outer_out.at[me], outer_in.at[me], own_sem.at[1])
    own_outer.start()

    def wait_all(source, target, send_sem, recv_sem):
        every = pl.ds(0, DEVICES - 1)
        copies = pltpu.make_async_remote_copy(
            src_ref=source.at[every],
            dst_ref=target.at[every],
            send_sem=send_sem,
            recv_sem=recv_sem,
            device_id=(me,),
            device_id_type=MESH,
        )
        copies.wait_send()
        copies.wait_recv()

    own_inner.wait()
    own_outer.wait()
    wait_all(inner_out, inner_in, inner_send, inner_recv)
    wait_all(outer_out, outer_in, outer_send, outer_recv)


def child_kernel(inner, outer, high_table, low_table, out):
    columns = inner.shape[0]
    inner_high, inner_low = split2(inner[...])
    outer_high, outer_low = split2(outer[...])
    high = jnp.concatenate([inner_high, outer_high], axis=1)
    low = jnp.concatenate([inner_low, outer_low], axis=1)
    dims = (((1,), (1,)), ((), ()))
    main = lax.dot_general(
        high_table[...], high, dims, preferred_element_type=f32
    ) + lax.dot_general(high_table[...], low, dims, preferred_element_type=f32)
    fine = lax.dot_general(low_table[...], high, dims, preferred_element_type=f32)
    refined = jnp.broadcast_to(main[960:961] > 0.5, (192, columns))
    out[0:192, :] = jnp.where(refined, main[0:192] + fine[0:192], main[768:960])
    for c in range(1, 4):
        rows = slice(192 * c, 192 * c + 192)
        out[rows, :] = jnp.where(refined, main[rows] + fine[rows], 0.0)


def on_device(state, neighbours, metric, flags, new_owner):
    hbm = pl.BlockSpec(memory_space=pl.ANY)
    block = jax.ShapeDtypeStruct((DEVICES, SLOTS, LANES), f32)
    buffer = pltpu.VMEM((DEVICES, SLOTS, LANES), f32)
    dma = pltpu.SemaphoreType.DMA
    inner, outer = pl.pallas_call(
        step_kernel,
        out_shape=(block, block),
        in_specs=[hbm] * 6,
        out_specs=(hbm, hbm),
        scratch_shapes=[
            pltpu.VMEM((192, ELEMS), f32),
            pltpu.VMEM((4, ELEMS), jnp.int32),
            pltpu.VMEM((1, ELEMS), f32),
            pltpu.VMEM((1, ELEMS), jnp.int32),
            pltpu.VMEM((1, ELEMS), jnp.int32),
            pltpu.VMEM((INNER + OUTER, 512), bf16),
            pltpu.VMEM((192 * ELEMS // LANES, LANES), f32),
            pltpu.VMEM((2, 48, ELEMS), f32),
            pltpu.VMEM((4, 32, ELEMS), f32),
            pltpu.VMEM((4, 24, ELEMS), f32),
            pltpu.VMEM((2, 32, LANES), f32),
            pltpu.VMEM((2, 2, 32, LANES), f32),
            buffer,
            buffer,
            pltpu.VMEM((DEVICES * SLOTS, ELEMS), bf16),
            dma((6,)),
            dma((2, 2)),
            dma((2, 2)),
            dma,
            dma,
            dma,
            dma,
            dma((2,)),
        ],
        compiler_params=pltpu.CompilerParams(collective_id=0, has_side_effects=True),
        name="step_and_migrate",
    )(
        state.reshape(192, ELEMS),
        neighbours,
        metric.reshape(1, ELEMS),
        flags.reshape(1, ELEMS),
        new_owner.reshape(1, ELEMS),
        jnp.asarray(step_table(), bf16),
    )
    slots = DEVICES * SLOTS
    tile = 256
    high_table, low_table = child_table()
    children = pl.pallas_call(
        child_kernel,
        grid=(slots // tile,),
        out_shape=jax.ShapeDtypeStruct((768, slots), f32),
        in_specs=[
            pl.BlockSpec((tile, LANES), lambda i: (i, 0)),
            pl.BlockSpec((tile, LANES), lambda i: (i, 0)),
            pl.BlockSpec((968, 2 * LANES), lambda i: (0, 0)),
            pl.BlockSpec((768, 2 * LANES), lambda i: (0, 0)),
        ],
        out_specs=pl.BlockSpec((768, tile), lambda i: (0, i)),
        name="make_children",
    )(
        inner.reshape(slots, LANES),
        outer.reshape(slots, LANES),
        jnp.asarray(high_table, bf16),
        jnp.asarray(low_table, bf16),
    )
    return children.reshape(4, 3, 64, slots)


def solution(mesh):
    placed = (P(None, None, "curve"), P(None, "curve"), P("curve"), P("curve"), P("curve", None))
    return jax.shard_map(
        on_device,
        mesh=mesh,
        in_specs=placed,
        out_specs=P(None, None, None, "curve"),
        check_vma=False,
    )
```

```python
import random

import jax
import jax.numpy as jnp
import numpy as np
from jax import lax
from jax.experimental import pallas as pl
from jax.experimental.pallas import tpu as pltpu
from jax.sharding import PartitionSpec as P

lgl_nodes = np.array(
    [
        -1.0,
        -0.8717401485096066,
        -0.5917001814331423,
        -0.2092992179024789,
        0.2092992179024789,
        0.5917001814331423,
        0.8717401485096066,
        1.0,
    ]
)
lift_weight = 28.0
earth_pressure = 1.2
friction = 0.4
slope_x = 0.3
slope_y = 0.1
time_step = 0.01
face_nodes = np.array(
    [
        [8 * r for r in range(8)],
        [8 * r + 7 for r in range(8)],
        [r for r in range(8)],
        [56 + r for r in range(8)],
    ]
)
inner_nodes = np.array([8 * iy + ix for iy in range(1, 7) for ix in range(1, 7)])
opposite = [1, 0, 3, 2]
outward = [-1.0, 1.0, -1.0, 1.0]

DEVICES = 128
ELEMS = 512
SLOTS = 8
LANES = 128
MAIN = 32
OUTER = 32
EXTRA = 16
INNER = 3 * MAIN + EXTRA
FLAG = 12
INNER_ROWS = 7
OUTER_ROWS = 6
CROSS = 32
NAME_BASE = 2
MESH = pl.DeviceIdType.MESH
bf16 = jnp.bfloat16
f32 = jnp.float32


def lagrange_table(points):
    values_table = np.ones((len(points), 8))
    for j in range(8):
        for m in range(8):
            if m != j:
                values_table[:, j] = (
                    values_table[:, j] * (points - lgl_nodes[m]) / (lgl_nodes[j] - lgl_nodes[m])
                )
    return values_table


def basis_tables():
    bary = np.array(
        [1.0 / np.prod([lgl_nodes[j] - lgl_nodes[m] for m in range(8) if m != j]) for j in range(8)]
    )
    derivative = np.zeros((8, 8))
    for i in range(8):
        for j in range(8):
            if i != j:
                derivative[i, j] = bary[j] / bary[i] / (lgl_nodes[i] - lgl_nodes[j])
        derivative[i, i] = -np.sum(derivative[i])
    identity = np.eye(8)
    lower_half = lagrange_table((lgl_nodes - 1.0) / 2.0)
    upper_half = lagrange_table((lgl_nodes + 1.0) / 2.0)
    halves = [lower_half, upper_half]
    prolong = np.stack(
        [
            np.kron(halves[row_half], halves[col_half])
            for row_half in range(2)
            for col_half in range(2)
        ]
    )
    return np.kron(identity, derivative), np.kron(derivative, identity), prolong


def two_parts(table):
    high = np.asarray(table, np.float32).astype(bf16)
    low = (np.asarray(table, np.float64) - high.astype(np.float64)).astype(bf16)
    return high, low


def corner_copy(face_id, r):
    return face_id < 2 and r in (0, 7)


def step_table():
    deriv_x, deriv_y, _ = basis_tables()
    full = np.concatenate([np.eye(64), deriv_x, deriv_y], axis=1)
    table = np.zeros((3, MAIN + OUTER + EXTRA, 192))
    for field in range(3):
        table[field, :MAIN] = full[inner_nodes[:MAIN]]
        for face_id in range(4):
            for r in range(8):
                if not corner_copy(face_id, r):
                    table[field, MAIN + 8 * face_id + r] = full[face_nodes[face_id][r]]
        start = MAIN + OUTER + 4 * field
        table[field, start : start + 4] = full[inner_nodes[MAIN:]]
    high, low = two_parts(table.reshape(-1, 192))
    return np.concatenate([high, high, low[:, 64:]], axis=1)


def child_tables():
    _, _, prolong = basis_tables()
    rows = np.concatenate([prolong.reshape(256, 64), np.eye(64)], axis=0)
    tables = []
    for shift in (0, 4):
        table = np.zeros((320, 80))
        table[:, :MAIN] = rows[:, inner_nodes[:MAIN]]
        for face_id in range(4):
            for r in range(8):
                table[:, MAIN + 8 * face_id + r] = rows[:, face_nodes[face_id][r]]
        start = MAIN + OUTER + shift
        table[:, start : start + 4] = rows[:, inner_nodes[MAIN:]]
        high, low = two_parts(table)
        tables.append(np.concatenate([high, high, low, np.zeros((320, 16), bf16)], axis=1))
    return np.stack(tables)


def send_order():
    order = [
        (z, y, x, c) for z in range(4) for y in range(4) for x in range(4) for c in range(2)
    ][1:]
    random.Random(0).shuffle(order)
    order.sort(key=lambda d: -sum(min(v, 4 - v) for v in d[:3]))
    return order


def split2(values):
    high = values.astype(bf16)
    return high, (values - high.astype(f32)).astype(bf16)


def face_flux(values, face_id):
    depth, moment_x, moment_y = values
    inv = 1.0 / depth
    pressure = 0.5 * earth_pressure * depth * depth
    sign = outward[face_id]
    if face_id < 2:
        normal = moment_x * inv
        terms = [moment_x, moment_x * normal + pressure, moment_y * normal]
    else:
        normal = moment_y * inv
        terms = [moment_y, moment_x * normal, moment_y * normal + pressure]
    return [sign * t for t in terms], jnp.abs(normal) + jnp.sqrt(earth_pressure * depth)


def mirror(values, face_id):
    if face_id < 2:
        return [values[0], -values[1], values[2]]
    return [values[0], values[1], -values[2]]


def step_kernel(
    state_in, neighbours_in, metric_in, flags_in, owner_in, table_in,
    inner_turned_out, outer_in,
    state, neighbours, metric, flags, owner, table,
    tiles, trace, own_flux, across, crossing, ghost,
    placed, inner_out, outer_out, inner_in, inner_turned, onehot,
    load_sem, halo_send, halo_recv, inner_send, inner_recv, outer_send, outer_recv, own_sem,
):
    pairs = (
        (state_in, state), (neighbours_in, neighbours), (metric_in, metric),
        (flags_in, flags), (owner_in, owner), (table_in, table),
    )
    loads = [pltpu.make_async_copy(a, b, load_sem.at[i]) for i, (a, b) in enumerate(pairs)]
    for load in loads:
        load.start()

    me = lax.axis_index("curve")
    order = send_order()
    z_part = [lax.rem(me // 32 + z, 4) * 32 for z in range(4)]
    y_part = [lax.rem((me // 8) % 4 + y, 4) * 8 for y in range(4)]
    x_part = [lax.rem((me // 2) % 4 + x, 4) * 2 for x in range(4)]
    c_part = [lax.rem(me % 2 + c, 2) for c in range(2)]
    zy_part = [[z + y for y in y_part] for z in z_part]
    xc_part = [[x + c for c in c_part] for x in x_part]
    others = [zy_part[z][y] + xc_part[x][c] for z, y, x, c in order]

    barrier = pltpu.get_barrier_semaphore()
    for to in others:
        pl.semaphore_signal(barrier, inc=1, device_id=(to,), device_id_type=MESH)
    for load in loads:
        load.wait()

    partners = neighbours[...]
    distance = jnp.where(lax.broadcasted_iota(jnp.int32, (4, ELEMS), 0) < 2, 1, 32)
    homes = lax.shift_right_arithmetic(partners, 9)
    real = partners >= 0
    below = jnp.where(real & (homes == me - distance), 1.0, 0.0)
    above = jnp.where(real & (homes == me + distance), 1.0, 0.0)
    owners = owner[...]
    hits = owners == lax.broadcasted_iota(jnp.int32, (DEVICES, ELEMS), 0)
    hits = jnp.where(hits, 1.0, 0.0)
    earlier = lax.broadcasted_iota(jnp.int32, (ELEMS, ELEMS), 0) < lax.broadcasted_iota(
        jnp.int32, (ELEMS, ELEMS), 1
    )
    nothing = jnp.zeros((4, ELEMS), f32)
    before = jnp.dot(
        jnp.concatenate([hits, below, nothing, above, nothing], axis=0).astype(bf16),
        jnp.where(earlier, 1.0, 0.0).astype(bf16),
        preferred_element_type=f32,
    )
    rank = jnp.sum(hits * before[:DEVICES], axis=0, keepdims=True)
    column = owners * SLOTS + rank.astype(jnp.int32)
    slot_rows = lax.broadcasted_iota(jnp.int32, (DEVICES * SLOTS, ELEMS), 0)
    onehot[...] = jnp.where(slot_rows == column, 1.0, 0.0).astype(bf16)
    spot = jnp.where(
        below > 0.5,
        before[DEVICES : DEVICES + 4],
        jnp.where(above > 0.5, before[DEVICES + 8 : DEVICES + 12] + CROSS, -1000.0),
    ).astype(jnp.int32)

    for t in range(ELEMS // LANES):
        tiles[192 * t : 192 * t + 192, :] = state[:, LANES * t : LANES * t + LANES]
    for face_id in range(4):
        for field in range(3):
            at = (face_id % 2) * 24 + field * 8
            if face_id < 2:
                for t in range(ELEMS // LANES):
                    start = 192 * t + 64 * field + 7 * face_id
                    trace[0, at : at + 8, LANES * t : LANES * t + LANES] = tiles[
                        pl.ds(start, 8, stride=8), :
                    ]
            else:
                start = 64 * field + 56 * (face_id - 2)
                trace[1, at : at + 8, :] = state[start : start + 8, :]

    first_row = lax.broadcasted_iota(jnp.int32, (8, ELEMS), 0) == 0
    name = (
        lax.broadcasted_iota(jnp.int32, (8, ELEMS), 1) + (me * ELEMS + NAME_BASE)
    ).astype(f32)
    name = jnp.where(first_row, name, 0.0)
    lane_rows = lax.broadcasted_iota(jnp.int32, (LANES, ELEMS), 0)
    nt_dims = (((1,), (1,)), ((), ()))
    for pair in (0, 1):
        packed = None
        for position in (0, 1):
            face_id = 2 * pair + position
            rows = jnp.concatenate([trace[pair, 24 * position : 24 * position + 24, :], name])
            chosen = lane_rows == spot[face_id : face_id + 1] + 2 * CROSS * position
            part = lax.dot_general(
                jnp.concatenate(split2(rows), axis=0),
                jnp.where(chosen, 1.0, 0.0).astype(bf16),
                nt_dims,
                preferred_element_type=f32,
            )
            packed = part if packed is None else packed + part
        crossing[pair] = packed[:32] + packed[32:]

    scale = (-time_step) * metric[...]
    depth, moment_x, moment_y = (state[64 * f : 64 * f + 64, :] for f in range(3))
    inv = 1.0 / depth
    speed_x, speed_y = moment_x * inv, moment_y * inv
    pressure = 0.5 * earth_pressure * depth * depth
    drag = friction / jnp.sqrt(speed_x * speed_x + speed_y * speed_y + 1.0)
    cross = moment_x * speed_y
    parts = [
        (depth, moment_x, moment_y),
        (
            moment_x + time_step * (depth * (slope_x - drag * speed_x)),
            moment_x * speed_x + pressure,
            cross,
        ),
        (
            moment_y + time_step * (depth * (slope_y - drag * speed_y)),
            cross,
            moment_y * speed_y + pressure,
        ),
    ]
    stepped = []
    for q, flux_x, flux_y in parts:
        q_high, q_low = split2(q)
        x_high, x_low = split2(scale * flux_x)
        y_high, y_low = split2(scale * flux_y)
        operand = jnp.concatenate(
            [q_high, x_high, y_high, q_low, x_low, y_low, x_high, y_high], axis=0
        )
        rows = slice(80 * len(stepped), 80 * len(stepped) + 80)
        stepped.append(jnp.dot(table[rows, :], operand, preferred_element_type=f32))

    def place(rows):
        both = lax.dot_general(
            onehot[...],
            jnp.concatenate(split2(rows), axis=0),
            nt_dims,
            preferred_element_type=f32,
        )
        placed[...] = both[:, :LANES] + both[:, LANES:]
        return [placed[pl.ds(j, DEVICES, stride=SLOTS), :] for j in range(SLOTS)]

    lane_at = lax.broadcasted_iota(jnp.int32, (DEVICES, LANES), 1)
    extra = stepped[0][-EXTRA:] + stepped[1][-EXTRA:] + stepped[2][-EXTRA:]
    flag_row = lax.broadcasted_iota(jnp.int32, (EXTRA, ELEMS), 0) == FLAG
    extra = extra + jnp.where(flag_row, flags[...].astype(f32), 0.0)
    slots = place(
        jnp.concatenate(
            [s[:MAIN] for s in stepped] + [extra, jnp.zeros((LANES - INNER, ELEMS), f32)], axis=0
        )
    )
    for r in range(INNER_ROWS):
        tail = pltpu.roll(slots[7], INNER - 16 * r, 1)
        inner_out[pl.ds(r, DEVICES, stride=8), :] = jnp.where(lane_at < INNER, slots[r], tail)

    for face_id in range(4):
        pair = face_id // 2
        at = (face_id % 2) * 24
        inside = [trace[pair, at + 8 * field : at + 8 * field + 8, :] for field in range(3)]
        flux_in, wave_in = face_flux(inside, face_id)
        for i, values in enumerate(flux_in + [wave_in]):
            own_flux[face_id, 8 * i : 8 * i + 8, :] = values
        partner = partners[face_id : face_id + 1]
        local = jnp.bitwise_and(partner, ELEMS - 1)
        piece = lax.shift_right_arithmetic(local, 7)
        lane = jnp.bitwise_and(local, LANES - 1)
        at = (opposite[face_id] % 2) * 24
        for t in range(ELEMS // LANES):
            cols = slice(t * LANES, (t + 1) * LANES)
            index = jnp.broadcast_to(lane[:, cols], (8, LANES))
            piece_t = jnp.broadcast_to(piece[:, cols], (8, LANES))
            for field in range(3):
                rows = slice(at + field * 8, at + field * 8 + 8)
                found = None
                for c in range(ELEMS // LANES):
                    values = trace[pair, rows, c * LANES : (c + 1) * LANES]
                    got = jnp.take_along_axis(values, index, axis=1, mode="promise_in_bounds")
                    found = got if c == 0 else jnp.where(piece_t == c, got, found)
                across[face_id, 8 * field : 8 * field + 8, cols] = found

    pl.semaphore_wait(barrier, DEVICES - 1)

    def halo(pair, upward):
        far = 32 if pair else 1
        target = lax.rem(me + (far if upward else DEVICES - far), DEVICES)
        side = 0 if upward else 1
        return pltpu.make_async_remote_copy(
            src_ref=crossing.at[pair],
            dst_ref=ghost.at[pair, side],
            send_sem=halo_send.at[pair, side],
            recv_sem=halo_recv.at[pair, side],
            device_id=(target,),
            device_id_type=MESH,
        )

    halos = [halo(pair, upward) for pair in (0, 1) for upward in (True, False)]
    for copy in halos:
        copy.start()

    def block(ref, device, rows):
        return ref.at[pl.ds(pl.multiple_of(device * 8, 8), rows)]

    def exchange(source, target, rows, send_sem, recv_sem):
        for to in others:
            pltpu.make_async_remote_copy(
                src_ref=block(source, to, rows),
                dst_ref=block(target, me, rows),
                send_sem=send_sem,
                recv_sem=recv_sem,
                device_id=(to,),
                device_id_type=MESH,
            ).start()

    exchange(inner_out, inner_in, INNER_ROWS, inner_send, inner_recv)
    own_inner = pltpu.make_async_copy(
        block(inner_out, me, INNER_ROWS), block(inner_in, me, INNER_ROWS), own_sem.at[0]
    )
    own_inner.start()

    for copy in halos:
        copy.wait()

    lift_scale = (time_step * lift_weight * 0.5) * metric[...]
    from_below = jnp.bitwise_and(lax.broadcasted_iota(jnp.int32, (32, LANES), 1), CROSS) != 0
    named = (partners + NAME_BASE).astype(f32)
    lifted = [[None] * 4 for _ in range(3)]
    zeros = jnp.zeros((2 * CROSS, ELEMS), bf16)
    for pair in (0, 1):
        merged = jnp.where(from_below, ghost[pair, 0], ghost[pair, 1])
        names = jnp.transpose(merged[24:32])[:, 0:1]
        chosen = []
        for position in (0, 1):
            face_id = 2 * pair + position
            start = 2 * CROSS * (1 - position)
            match = names[start : start + 2 * CROSS] == named[face_id : face_id + 1]
            match = jnp.where(match, 1.0, 0.0).astype(bf16)
            chosen.append(jnp.concatenate([zeros, match] if start else [match, zeros], axis=0))
        got = jnp.dot(
            jnp.concatenate(split2(merged), axis=0),
            jnp.concatenate(chosen, axis=1),
            preferred_element_type=f32,
        )
        got = got[:32] + got[32:]
        for position in (0, 1):
            face_id = 2 * pair + position
            wall = jnp.logical_not(real[face_id : face_id + 1])
            local = homes[face_id : face_id + 1] == me
            at = position * 24
            inside = [trace[pair, at + 8 * field : at + 8 * field + 8, :] for field in range(3)]
            reflected = mirror(inside, face_id)
            outside = []
            for field in range(3):
                rows = slice(8 * field, 8 * field + 8)
                there = got[rows, ELEMS * position : ELEMS * position + ELEMS]
                there = jnp.where(local, across[face_id, rows, :], there)
                outside.append(jnp.where(wall, reflected[field], there))
            flux_out, wave_out = face_flux(outside, face_id)
            largest = jnp.maximum(own_flux[face_id, 24:32, :], wave_out)
            for field in range(3):
                jump = own_flux[face_id, 8 * field : 8 * field + 8, :] - flux_out[field]
                lifted[field][face_id] = lift_scale * (
                    jump + largest * (outside[field] - inside[field])
                )
    outer = [
        stepped[field][MAIN : MAIN + OUTER] + jnp.concatenate(lifted[field], axis=0)
        for field in range(3)
    ]
    slots = place(jnp.concatenate(outer + [jnp.zeros((LANES - 96, ELEMS), f32)], axis=0))
    for r in range(4):
        pair_of = jnp.where(lane_at < 64, slots[r], pltpu.roll(slots[r + 4], 64, 1))
        outer_out[pl.ds(r, DEVICES, stride=8), :] = pair_of
    for q in range(2):
        row = pltpu.roll(slots[4 * q], 64, 1)
        for k in range(1, 4):
            piece = slots[4 * q + k] if k == 2 else pltpu.roll(slots[4 * q + k], (32 * k - 64) % 128, 1)
            row = jnp.where(lane_at >= 32 * k, piece, row)
        outer_out[pl.ds(4 + q, DEVICES, stride=8), :] = row

    exchange(outer_out, outer_in, OUTER_ROWS, outer_send, outer_recv)
    own_outer = pltpu.make_async_copy(
        block(outer_out, me, OUTER_ROWS), block(outer_in, me, OUTER_ROWS), own_sem.at[1]
    )
    own_outer.start()

    def wait_all(source, target, rows, send_sem, recv_sem):
        every = pl.ds(0, (DEVICES - 1) * rows)
        copies = pltpu.make_async_remote_copy(
            src_ref=source.at[every],
            dst_ref=target.at[every],
            send_sem=send_sem,
            recv_sem=recv_sem,
            device_id=(me,),
            device_id_type=MESH,
        )
        copies.wait_send()
        copies.wait_recv()

    own_inner.wait()
    wait_all(inner_out, inner_in, INNER_ROWS, inner_send, inner_recv)
    last = None
    for r in range(INNER_ROWS):
        tail = pltpu.roll(inner_in[pl.ds(r, DEVICES, stride=8), :], 16 * r + 16, 1)
        last = tail if r == 0 else jnp.where(lane_at >= 16 * r, tail, last)
    inner_in[pl.ds(7, DEVICES, stride=8), :] = last
    inner_turned[...] = jnp.transpose(inner_in[...])[:INNER]
    turned = pltpu.make_async_copy(inner_turned, inner_turned_out, own_sem.at[2])
    turned.start()
    own_outer.wait()
    turned.wait()
    wait_all(outer_out, outer_in, OUTER_ROWS, outer_send, outer_recv)


def child_kernel(inner_in, outer_in, tables_in, out_hbm, inner, outer, tables, flat, out, load_sem, store_sem):
    loads = [
        pltpu.make_async_copy(outer_in, outer, load_sem.at[0]),
        pltpu.make_async_copy(inner_in, inner, load_sem.at[1]),
        pltpu.make_async_copy(tables_in, tables, load_sem.at[2]),
    ]
    for load in loads:
        load.start()
    loads[0].wait()
    lane_at = lax.broadcasted_iota(jnp.int32, (DEVICES, LANES), 1)
    for j in range(SLOTS):
        body = outer[pl.ds(j % 4, DEVICES, stride=8), :]
        rest = outer[pl.ds(4 + j // 4, DEVICES, stride=8), :]
        body = pltpu.roll(body, 64, 1) if j >= 4 else body
        rest = rest if j % 4 == 2 else pltpu.roll(rest, (64 - 32 * (j % 4)) % 128, 1)
        flat[pl.ds(j, DEVICES, stride=8), :] = jnp.where(lane_at < 64, body, rest)
    faces = jnp.transpose(flat[...])
    loads[1].wait()
    loads[2].wait()
    slots = DEVICES * SLOTS
    refined = inner[3 * MAIN + FLAG : 3 * MAIN + FLAG + 1, :] > 0.5
    stores = []
    for field in range(3):
        own = slice(MAIN * field, MAIN * field + MAIN)
        start = 3 * MAIN + 8 * (field // 2)
        values = jnp.concatenate(
            [inner[own, :], faces[own], inner[start : start + 8, :], jnp.zeros((8, slots), f32)],
            axis=0,
        )
        high, low = split2(values)
        operand = jnp.concatenate([high, low, high, jnp.zeros((16, slots), bf16)], axis=0)
        nodes = jnp.dot(tables[field % 2], operand, preferred_element_type=f32)
        for c in range(4):
            start = 192 * c + 64 * field
            rows = pl.ds(start, 64)
            other = nodes[256:320] if c == 0 else 0.0
            out[start : start + 64, :] = jnp.where(refined, nodes[64 * c : 64 * c + 64], other)
            store = pltpu.make_async_copy(
                out.at[rows], out_hbm.at[rows], store_sem.at[4 * field + c]
            )
            store.start()
            stores.append(store)
    for store in stores:
        store.wait()


def on_device(state, neighbours, metric, flags, new_owner):
    hbm = pl.BlockSpec(memory_space=pl.ANY)
    slots = DEVICES * SLOTS
    buffer = pltpu.VMEM((slots, LANES), f32)
    dma = pltpu.SemaphoreType.DMA
    inner, outer = pl.pallas_call(
        step_kernel,
        out_shape=(
            jax.ShapeDtypeStruct((INNER, slots), f32),
            jax.ShapeDtypeStruct((slots, LANES), f32),
        ),
        in_specs=[hbm] * 6,
        out_specs=(hbm, hbm),
        scratch_shapes=[
            pltpu.VMEM((192, ELEMS), f32),
            pltpu.VMEM((4, ELEMS), jnp.int32),
            pltpu.VMEM((1, ELEMS), f32),
            pltpu.VMEM((1, ELEMS), jnp.int32),
            pltpu.VMEM((1, ELEMS), jnp.int32),
            pltpu.VMEM((240, 512), bf16),
            pltpu.VMEM((192 * ELEMS // LANES, LANES), f32),
            pltpu.VMEM((2, 48, ELEMS), f32),
            pltpu.VMEM((4, 32, ELEMS), f32),
            pltpu.VMEM((4, 24, ELEMS), f32),
            pltpu.VMEM((2, 32, LANES), f32),
            pltpu.VMEM((2, 2, 32, LANES), f32),
            buffer,
            buffer,
            buffer,
            buffer,
            pltpu.VMEM((INNER, slots), f32),
            pltpu.VMEM((slots, ELEMS), bf16),
            dma((6,)),
            dma((2, 2)),
            dma((2, 2)),
            dma,
            dma,
            dma,
            dma,
            dma((3,)),
        ],
        compiler_params=pltpu.CompilerParams(collective_id=0, has_side_effects=True),
        name="step_and_migrate",
    )(
        state.reshape(192, ELEMS),
        neighbours,
        metric.reshape(1, ELEMS),
        flags.reshape(1, ELEMS),
        new_owner.reshape(1, ELEMS),
        jnp.asarray(step_table(), bf16),
    )
    children = pl.pallas_call(
        child_kernel,
        out_shape=jax.ShapeDtypeStruct((768, slots), f32),
        in_specs=[hbm] * 3,
        out_specs=hbm,
        scratch_shapes=[
            pltpu.VMEM((INNER, slots), f32),
            buffer,
            pltpu.VMEM((2, 320, 256), bf16),
            buffer,
            pltpu.VMEM((768, slots), f32),
            dma((3,)),
            dma((12,)),
        ],
        name="make_children",
    )(inner, outer, jnp.asarray(child_tables(), bf16))
    return children.reshape(4, 3, 64, slots)


def solution(mesh):
    placed = (P(None, None, "curve"), P(None, "curve"), P("curve"), P("curve"), P("curve", None))
    return jax.shard_map(
        on_device,
        mesh=mesh,
        in_specs=placed,
        out_specs=P(None, None, None, "curve"),
        check_vma=False,
    )
```

```python
import random

import jax
import jax.numpy as jnp
import numpy as np
from jax import lax
from jax.experimental import pallas as pl
from jax.experimental.pallas import tpu as pltpu
from jax.sharding import PartitionSpec as P

lgl_nodes = np.array(
    [
        -1.0,
        -0.8717401485096066,
        -0.5917001814331423,
        -0.2092992179024789,
        0.2092992179024789,
        0.5917001814331423,
        0.8717401485096066,
        1.0,
    ]
)
lift_weight = 28.0
earth_pressure = 1.2
friction = 0.4
slope_x = 0.3
slope_y = 0.1
time_step = 0.01
face_nodes = np.array(
    [
        [8 * r for r in range(8)],
        [8 * r + 7 for r in range(8)],
        [r for r in range(8)],
        [56 + r for r in range(8)],
    ]
)
inner_nodes = np.array([8 * iy + ix for iy in range(1, 7) for ix in range(1, 7)])
opposite = [1, 0, 3, 2]
outward = [-1.0, 1.0, -1.0, 1.0]

DEVICES = 128
ELEMS = 512
SLOTS = 8
LANES = 128
MAIN = 32
OUTER = 32
EXTRA = 16
INNER = 3 * MAIN + EXTRA
FLAG = 12
INNER_ROWS = 7
OUTER_ROWS = 6
CROSS = 32
NAME_BASE = 2
MESH = pl.DeviceIdType.MESH
bf16 = jnp.bfloat16
f32 = jnp.float32


def lagrange_table(points):
    values_table = np.ones((len(points), 8))
    for j in range(8):
        for m in range(8):
            if m != j:
                values_table[:, j] = (
                    values_table[:, j] * (points - lgl_nodes[m]) / (lgl_nodes[j] - lgl_nodes[m])
                )
    return values_table


def basis_tables():
    bary = np.array(
        [1.0 / np.prod([lgl_nodes[j] - lgl_nodes[m] for m in range(8) if m != j]) for j in range(8)]
    )
    derivative = np.zeros((8, 8))
    for i in range(8):
        for j in range(8):
            if i != j:
                derivative[i, j] = bary[j] / bary[i] / (lgl_nodes[i] - lgl_nodes[j])
        derivative[i, i] = -np.sum(derivative[i])
    identity = np.eye(8)
    lower_half = lagrange_table((lgl_nodes - 1.0) / 2.0)
    upper_half = lagrange_table((lgl_nodes + 1.0) / 2.0)
    halves = [lower_half, upper_half]
    prolong = np.stack(
        [
            np.kron(halves[row_half], halves[col_half])
            for row_half in range(2)
            for col_half in range(2)
        ]
    )
    return np.kron(identity, derivative), np.kron(derivative, identity), prolong


def two_parts(table):
    high = np.asarray(table, np.float32).astype(bf16)
    low = (np.asarray(table, np.float64) - high.astype(np.float64)).astype(bf16)
    return high, low


def corner_copy(face_id, r):
    return face_id < 2 and r in (0, 7)


def step_table():
    deriv_x, deriv_y, _ = basis_tables()
    full = np.concatenate([np.eye(64), deriv_x, deriv_y], axis=1)
    table = np.zeros((3, MAIN + OUTER + EXTRA, 192))
    for field in range(3):
        table[field, :MAIN] = full[inner_nodes[:MAIN]]
        for face_id in range(4):
            for r in range(8):
                if not corner_copy(face_id, r):
                    table[field, MAIN + 8 * face_id + r] = full[face_nodes[face_id][r]]
        start = MAIN + OUTER + 4 * field
        table[field, start : start + 4] = full[inner_nodes[MAIN:]]
    high, low = two_parts(table.reshape(-1, 192))
    return np.concatenate([high, high, low[:, 64:]], axis=1)


def child_tables():
    _, _, prolong = basis_tables()
    rows = np.concatenate([prolong.reshape(256, 64), np.eye(64)], axis=0)
    tables = []
    for shift in (0, 4):
        table = np.zeros((320, 80))
        table[:, :MAIN] = rows[:, inner_nodes[:MAIN]]
        for face_id in range(4):
            for r in range(8):
                table[:, MAIN + 8 * face_id + r] = rows[:, face_nodes[face_id][r]]
        start = MAIN + OUTER + shift
        table[:, start : start + 4] = rows[:, inner_nodes[MAIN:]]
        high, low = two_parts(table)
        tables.append(np.concatenate([high, high, low, np.zeros((320, 16), bf16)], axis=1))
    return np.stack(tables)


def send_order():
    order = [
        (z, y, x, c) for z in range(4) for y in range(4) for x in range(4) for c in range(2)
    ][1:]
    random.Random(0).shuffle(order)
    order.sort(key=lambda d: -sum(min(v, 4 - v) for v in d[:3]))
    return order


def split2(values):
    high = values.astype(bf16)
    return high, (values - high.astype(f32)).astype(bf16)


def face_flux(values, face_id):
    depth, moment_x, moment_y = values
    inv = 1.0 / depth
    pressure = 0.5 * earth_pressure * depth * depth
    sign = outward[face_id]
    if face_id < 2:
        normal = moment_x * inv
        terms = [moment_x, moment_x * normal + pressure, moment_y * normal]
    else:
        normal = moment_y * inv
        terms = [moment_y, moment_x * normal, moment_y * normal + pressure]
    return [sign * t for t in terms], jnp.abs(normal) + jnp.sqrt(earth_pressure * depth)


def mirror(values, face_id):
    if face_id < 2:
        return [values[0], -values[1], values[2]]
    return [values[0], values[1], -values[2]]


def step_kernel(
    state_in, neighbours_in, metric_in, flags_in, owner_in, table_in, tables_in,
    inner_turned_out, outer_in, tables_out,
    state, neighbours, metric, flags, owner, table,
    tiles, trace, own_flux, across, crossing, ghost,
    placed, inner_out, outer_out, inner_in, inner_turned, onehot,
    load_sem, halo_send, halo_recv, inner_send, inner_recv, outer_send, outer_recv, own_sem,
):
    pairs = (
        (state_in, state), (neighbours_in, neighbours), (metric_in, metric),
        (flags_in, flags), (owner_in, owner), (table_in, table),
    )
    loads = [pltpu.make_async_copy(a, b, load_sem.at[i]) for i, (a, b) in enumerate(pairs)]
    for load in loads:
        load.start()

    me = lax.axis_index("curve")
    order = send_order()
    z_part = [lax.rem(me // 32 + z, 4) * 32 for z in range(4)]
    y_part = [lax.rem((me // 8) % 4 + y, 4) * 8 for y in range(4)]
    x_part = [lax.rem((me // 2) % 4 + x, 4) * 2 for x in range(4)]
    c_part = [lax.rem(me % 2 + c, 2) for c in range(2)]
    zy_part = [[z + y for y in y_part] for z in z_part]
    xc_part = [[x + c for c in c_part] for x in x_part]
    others = [zy_part[z][y] + xc_part[x][c] for z, y, x, c in order]

    barrier = pltpu.get_barrier_semaphore()
    for to in others:
        pl.semaphore_signal(barrier, inc=1, device_id=(to,), device_id_type=MESH)
    for load in loads:
        load.wait()

    partners = neighbours[...]
    distance = jnp.where(lax.broadcasted_iota(jnp.int32, (4, ELEMS), 0) < 2, 1, 32)
    homes = lax.shift_right_arithmetic(partners, 9)
    real = partners >= 0
    below = jnp.where(real & (homes == me - distance), 1.0, 0.0)
    above = jnp.where(real & (homes == me + distance), 1.0, 0.0)
    owners = owner[...]
    hits = owners == lax.broadcasted_iota(jnp.int32, (DEVICES, ELEMS), 0)
    hits = jnp.where(hits, 1.0, 0.0)
    earlier = lax.broadcasted_iota(jnp.int32, (ELEMS, ELEMS), 0) < lax.broadcasted_iota(
        jnp.int32, (ELEMS, ELEMS), 1
    )
    nothing = jnp.zeros((4, ELEMS), f32)
    before = jnp.dot(
        jnp.concatenate([hits, below, nothing, above, nothing], axis=0).astype(bf16),
        jnp.where(earlier, 1.0, 0.0).astype(bf16),
        preferred_element_type=f32,
    )
    rank = jnp.sum(hits * before[:DEVICES], axis=0, keepdims=True)
    column = owners * SLOTS + rank.astype(jnp.int32)
    slot_rows = lax.broadcasted_iota(jnp.int32, (DEVICES * SLOTS, ELEMS), 0)
    onehot[...] = jnp.where(slot_rows == column, 1.0, 0.0).astype(bf16)
    spot = jnp.where(
        below > 0.5,
        before[DEVICES : DEVICES + 4],
        jnp.where(above > 0.5, before[DEVICES + 8 : DEVICES + 12] + CROSS, -1000.0),
    ).astype(jnp.int32)

    for t in range(ELEMS // LANES):
        tiles[192 * t : 192 * t + 192, :] = state[:, LANES * t : LANES * t + LANES]
    for face_id in range(4):
        for field in range(3):
            at = (face_id % 2) * 24 + field * 8
            if face_id < 2:
                for t in range(ELEMS // LANES):
                    start = 192 * t + 64 * field + 7 * face_id
                    trace[0, at : at + 8, LANES * t : LANES * t + LANES] = tiles[
                        pl.ds(start, 8, stride=8), :
                    ]
            else:
                start = 64 * field + 56 * (face_id - 2)
                trace[1, at : at + 8, :] = state[start : start + 8, :]

    first_row = lax.broadcasted_iota(jnp.int32, (8, ELEMS), 0) == 0
    name = (
        lax.broadcasted_iota(jnp.int32, (8, ELEMS), 1) + (me * ELEMS + NAME_BASE)
    ).astype(f32)
    name = jnp.where(first_row, name, 0.0)
    lane_rows = lax.broadcasted_iota(jnp.int32, (LANES, ELEMS), 0)
    nt_dims = (((1,), (1,)), ((), ()))
    for pair in (0, 1):
        packed = None
        for position in (0, 1):
            face_id = 2 * pair + position
            rows = jnp.concatenate([trace[pair, 24 * position : 24 * position + 24, :], name])
            chosen = lane_rows == spot[face_id : face_id + 1] + 2 * CROSS * position
            part = lax.dot_general(
                jnp.concatenate(split2(rows), axis=0),
                jnp.where(chosen, 1.0, 0.0).astype(bf16),
                nt_dims,
                preferred_element_type=f32,
            )
            packed = part if packed is None else packed + part
        crossing[pair] = packed[:32] + packed[32:]

    scale = (-time_step) * metric[...]
    depth, moment_x, moment_y = (state[64 * f : 64 * f + 64, :] for f in range(3))
    inv = 1.0 / depth
    speed_x, speed_y = moment_x * inv, moment_y * inv
    pressure = 0.5 * earth_pressure * depth * depth
    drag = friction / jnp.sqrt(speed_x * speed_x + speed_y * speed_y + 1.0)
    cross = moment_x * speed_y
    parts = [
        (depth, moment_x, moment_y),
        (
            moment_x + time_step * (depth * (slope_x - drag * speed_x)),
            moment_x * speed_x + pressure,
            cross,
        ),
        (
            moment_y + time_step * (depth * (slope_y - drag * speed_y)),
            cross,
            moment_y * speed_y + pressure,
        ),
    ]
    stepped = []
    for q, flux_x, flux_y in parts:
        q_high, q_low = split2(q)
        x_high, x_low = split2(scale * flux_x)
        y_high, y_low = split2(scale * flux_y)
        operand = jnp.concatenate(
            [q_high, x_high, y_high, q_low, x_low, y_low, x_high, y_high], axis=0
        )
        rows = slice(80 * len(stepped), 80 * len(stepped) + 80)
        stepped.append(jnp.dot(table[rows, :], operand, preferred_element_type=f32))

    def place(rows):
        both = lax.dot_general(
            onehot[...],
            jnp.concatenate(split2(rows), axis=0),
            nt_dims,
            preferred_element_type=f32,
        )
        placed[...] = both[:, :LANES] + both[:, LANES:]
        return [placed[pl.ds(j, DEVICES, stride=SLOTS), :] for j in range(SLOTS)]

    lane_at = lax.broadcasted_iota(jnp.int32, (DEVICES, LANES), 1)
    extra = stepped[0][-EXTRA:] + stepped[1][-EXTRA:] + stepped[2][-EXTRA:]
    flag_row = lax.broadcasted_iota(jnp.int32, (EXTRA, ELEMS), 0) == FLAG
    extra = extra + jnp.where(flag_row, flags[...].astype(f32), 0.0)
    slots = place(
        jnp.concatenate(
            [s[:MAIN] for s in stepped] + [extra, jnp.zeros((LANES - INNER, ELEMS), f32)], axis=0
        )
    )
    for r in range(INNER_ROWS):
        tail = pltpu.roll(slots[7], INNER - 16 * r, 1)
        inner_out[pl.ds(r, DEVICES, stride=8), :] = jnp.where(lane_at < INNER, slots[r], tail)

    for face_id in range(4):
        pair = face_id // 2
        at = (face_id % 2) * 24
        inside = [trace[pair, at + 8 * field : at + 8 * field + 8, :] for field in range(3)]
        flux_in, wave_in = face_flux(inside, face_id)
        for i, values in enumerate(flux_in + [wave_in]):
            own_flux[face_id, 8 * i : 8 * i + 8, :] = values
        partner = partners[face_id : face_id + 1]
        local = jnp.bitwise_and(partner, ELEMS - 1)
        piece = lax.shift_right_arithmetic(local, 7)
        lane = jnp.bitwise_and(local, LANES - 1)
        at = (opposite[face_id] % 2) * 24
        for t in range(ELEMS // LANES):
            cols = slice(t * LANES, (t + 1) * LANES)
            index = jnp.broadcast_to(lane[:, cols], (8, LANES))
            piece_t = jnp.broadcast_to(piece[:, cols], (8, LANES))
            for field in range(3):
                rows = slice(at + field * 8, at + field * 8 + 8)
                found = None
                for c in range(ELEMS // LANES):
                    values = trace[pair, rows, c * LANES : (c + 1) * LANES]
                    got = jnp.take_along_axis(values, index, axis=1, mode="promise_in_bounds")
                    found = got if c == 0 else jnp.where(piece_t == c, got, found)
                across[face_id, 8 * field : 8 * field + 8, cols] = found

    pl.semaphore_wait(barrier, DEVICES - 1)

    def halo(pair, upward):
        far = 32 if pair else 1
        target = lax.rem(me + (far if upward else DEVICES - far), DEVICES)
        side = 0 if upward else 1
        return pltpu.make_async_remote_copy(
            src_ref=crossing.at[pair],
            dst_ref=ghost.at[pair, side],
            send_sem=halo_send.at[pair, side],
            recv_sem=halo_recv.at[pair, side],
            device_id=(target,),
            device_id_type=MESH,
        )

    halos = [halo(pair, upward) for pair in (0, 1) for upward in (True, False)]
    for copy in halos:
        copy.start()

    def block(ref, device, rows):
        return ref.at[pl.ds(pl.multiple_of(device * 8, 8), rows)]

    def exchange(source, target, rows, send_sem, recv_sem):
        for to in others:
            pltpu.make_async_remote_copy(
                src_ref=block(source, to, rows),
                dst_ref=block(target, me, rows),
                send_sem=send_sem,
                recv_sem=recv_sem,
                device_id=(to,),
                device_id_type=MESH,
            ).start()

    exchange(inner_out, inner_in, INNER_ROWS, inner_send, inner_recv)
    own_inner = pltpu.make_async_copy(
        block(inner_out, me, INNER_ROWS), block(inner_in, me, INNER_ROWS), own_sem.at[0]
    )
    own_inner.start()

    for copy in halos:
        copy.wait()

    lift_scale = (time_step * lift_weight * 0.5) * metric[...]
    from_below = jnp.bitwise_and(lax.broadcasted_iota(jnp.int32, (32, LANES), 1), CROSS) != 0
    named = (partners + NAME_BASE).astype(f32)
    lifted = [[None] * 4 for _ in range(3)]
    zeros = jnp.zeros((2 * CROSS, ELEMS), bf16)
    for pair in (0, 1):
        merged = jnp.where(from_below, ghost[pair, 0], ghost[pair, 1])
        names = jnp.transpose(merged[24:32])[:, 0:1]
        chosen = []
        for position in (0, 1):
            face_id = 2 * pair + position
            start = 2 * CROSS * (1 - position)
            match = names[start : start + 2 * CROSS] == named[face_id : face_id + 1]
            match = jnp.where(match, 1.0, 0.0).astype(bf16)
            chosen.append(jnp.concatenate([zeros, match] if start else [match, zeros], axis=0))
        got = jnp.dot(
            jnp.concatenate(split2(merged), axis=0),
            jnp.concatenate(chosen, axis=1),
            preferred_element_type=f32,
        )
        got = got[:32] + got[32:]
        for position in (0, 1):
            face_id = 2 * pair + position
            wall = jnp.logical_not(real[face_id : face_id + 1])
            local = homes[face_id : face_id + 1] == me
            at = position * 24
            inside = [trace[pair, at + 8 * field : at + 8 * field + 8, :] for field in range(3)]
            reflected = mirror(inside, face_id)
            outside = []
            for field in range(3):
                rows = slice(8 * field, 8 * field + 8)
                there = got[rows, ELEMS * position : ELEMS * position + ELEMS]
                there = jnp.where(local, across[face_id, rows, :], there)
                outside.append(jnp.where(wall, reflected[field], there))
            flux_out, wave_out = face_flux(outside, face_id)
            largest = jnp.maximum(own_flux[face_id, 24:32, :], wave_out)
            for field in range(3):
                jump = own_flux[face_id, 8 * field : 8 * field + 8, :] - flux_out[field]
                lifted[field][face_id] = lift_scale * (
                    jump + largest * (outside[field] - inside[field])
                )
    outer = [
        stepped[field][MAIN : MAIN + OUTER] + jnp.concatenate(lifted[field], axis=0)
        for field in range(3)
    ]
    slots = place(jnp.concatenate(outer + [jnp.zeros((LANES - 96, ELEMS), f32)], axis=0))
    for r in range(4):
        pair_of = jnp.where(lane_at < 64, slots[r], pltpu.roll(slots[r + 4], 64, 1))
        outer_out[pl.ds(r, DEVICES, stride=8), :] = pair_of
    for q in range(2):
        row = pltpu.roll(slots[4 * q], 64, 1)
        for k in range(1, 4):
            piece = slots[4 * q + k] if k == 2 else pltpu.roll(slots[4 * q + k], (32 * k - 64) % 128, 1)
            row = jnp.where(lane_at >= 32 * k, piece, row)
        outer_out[pl.ds(4 + q, DEVICES, stride=8), :] = row

    exchange(outer_out, outer_in, OUTER_ROWS, outer_send, outer_recv)
    own_outer = pltpu.make_async_copy(
        block(outer_out, me, OUTER_ROWS), block(outer_in, me, OUTER_ROWS), own_sem.at[1]
    )
    own_outer.start()

    def wait_all(source, target, rows, send_sem, recv_sem):
        every = pl.ds(0, (DEVICES - 1) * rows)
        copies = pltpu.make_async_remote_copy(
            src_ref=source.at[every],
            dst_ref=target.at[every],
            send_sem=send_sem,
            recv_sem=recv_sem,
            device_id=(me,),
            device_id_type=MESH,
        )
        copies.wait_send()
        copies.wait_recv()

    tables_load = pltpu.make_async_copy(tables_in, tables_out, own_sem.at[3])
    tables_load.start()
    own_inner.wait()
    wait_all(inner_out, inner_in, INNER_ROWS, inner_send, inner_recv)
    last = None
    for r in range(INNER_ROWS):
        tail = pltpu.roll(inner_in[pl.ds(r, DEVICES, stride=8), :], 16 * r + 16, 1)
        last = tail if r == 0 else jnp.where(lane_at >= 16 * r, tail, last)
    inner_in[pl.ds(7, DEVICES, stride=8), :] = last
    inner_turned[...] = jnp.transpose(inner_in[...])[:INNER]
    turned = pltpu.make_async_copy(inner_turned, inner_turned_out, own_sem.at[2])
    turned.start()
    own_outer.wait()
    turned.wait()
    tables_load.wait()
    wait_all(outer_out, outer_in, OUTER_ROWS, outer_send, outer_recv)


def child_kernel(inner, outer, tables, out_hbm, flat, out, store_sem):
    lane_at = lax.broadcasted_iota(jnp.int32, (DEVICES, LANES), 1)
    for j in range(SLOTS):
        body = outer[pl.ds(j % 4, DEVICES, stride=8), :]
        rest = outer[pl.ds(4 + j // 4, DEVICES, stride=8), :]
        body = pltpu.roll(body, 64, 1) if j >= 4 else body
        rest = rest if j % 4 == 2 else pltpu.roll(rest, (64 - 32 * (j % 4)) % 128, 1)
        flat[pl.ds(j, DEVICES, stride=8), :] = jnp.where(lane_at < 64, body, rest)
    faces = jnp.transpose(flat[...])
    slots = DEVICES * SLOTS
    refined = inner[3 * MAIN + FLAG : 3 * MAIN + FLAG + 1, :] > 0.5
    stores = []
    for field in range(3):
        own = slice(MAIN * field, MAIN * field + MAIN)
        start = 3 * MAIN + 8 * (field // 2)
        values = jnp.concatenate(
            [inner[own, :], faces[own], inner[start : start + 8, :], jnp.zeros((8, slots), f32)],
            axis=0,
        )
        high, low = split2(values)
        operand = jnp.concatenate([high, low, high, jnp.zeros((16, slots), bf16)], axis=0)
        nodes = jnp.dot(tables[field % 2], operand, preferred_element_type=f32)
        for c in range(4):
            start = 192 * c + 64 * field
            rows = pl.ds(start, 64)
            other = nodes[256:320] if c == 0 else 0.0
            out[start : start + 64, :] = jnp.where(refined, nodes[64 * c : 64 * c + 64], other)
            store = pltpu.make_async_copy(
                out.at[rows], out_hbm.at[rows], store_sem.at[4 * field + c]
            )
            store.start()
            stores.append(store)
    for store in stores:
        store.wait()


def on_device(state, neighbours, metric, flags, new_owner):
    hbm = pl.BlockSpec(memory_space=pl.ANY)
    slots = DEVICES * SLOTS
    buffer = pltpu.VMEM((slots, LANES), f32)
    dma = pltpu.SemaphoreType.DMA
    inner, outer, tables = pl.pallas_call(
        step_kernel,
        out_shape=(
            jax.ShapeDtypeStruct((INNER, slots), f32),
            jax.ShapeDtypeStruct((slots, LANES), f32),
            jax.ShapeDtypeStruct((2, 320, 256), bf16),
        ),
        in_specs=[pl.BlockSpec(memory_space=pltpu.HBM)] * 7,
        out_specs=(hbm, hbm, hbm),
        scratch_shapes=[
            pltpu.VMEM((192, ELEMS), f32),
            pltpu.VMEM((4, ELEMS), jnp.int32),
            pltpu.VMEM((1, ELEMS), f32),
            pltpu.VMEM((1, ELEMS), jnp.int32),
            pltpu.VMEM((1, ELEMS), jnp.int32),
            pltpu.VMEM((240, 512), bf16),
            pltpu.VMEM((192 * ELEMS // LANES, LANES), f32),
            pltpu.VMEM((2, 48, ELEMS), f32),
            pltpu.VMEM((4, 32, ELEMS), f32),
            pltpu.VMEM((4, 24, ELEMS), f32),
            pltpu.VMEM((2, 32, LANES), f32),
            pltpu.VMEM((2, 2, 32, LANES), f32),
            buffer,
            buffer,
            buffer,
            buffer,
            pltpu.VMEM((INNER, slots), f32),
            pltpu.VMEM((slots, ELEMS), bf16),
            dma((6,)),
            dma((2, 2)),
            dma((2, 2)),
            dma,
            dma,
            dma,
            dma,
            dma((4,)),
        ],
        compiler_params=pltpu.CompilerParams(collective_id=0, has_side_effects=True, vmem_limit_bytes=16 << 20),
        name="step_and_migrate",
    )(
        *(
            pltpu.with_memory_space_constraint(x, pltpu.HBM)
            for x in (
                state.reshape(192, ELEMS),
                neighbours,
                metric.reshape(1, ELEMS),
                flags.reshape(1, ELEMS),
                new_owner.reshape(1, ELEMS),
                jnp.asarray(step_table(), bf16),
                jnp.asarray(child_tables(), bf16),
            )
        )
    )
    children = pl.pallas_call(
        child_kernel,
        out_shape=jax.ShapeDtypeStruct((768, slots), f32),
        in_specs=[pl.BlockSpec(memory_space=pltpu.VMEM)] * 3,
        out_specs=pl.BlockSpec(memory_space=pltpu.HBM),
        scratch_shapes=[
            buffer,
            pltpu.VMEM((768, slots), f32),
            dma((12,)),
        ],
        compiler_params=pltpu.CompilerParams(vmem_limit_bytes=16 << 20),
        name="make_children",
    )(inner, outer, tables)
    return children.reshape(4, 3, 64, slots)


def solution(mesh):
    placed = (P(None, None, "curve"), P(None, "curve"), P("curve"), P("curve"), P("curve", None))
    return jax.shard_map(
        on_device,
        mesh=mesh,
        in_specs=placed,
        out_specs=P(None, None, None, "curve"),
        check_vma=False,
    )
```

```python
import random

import jax
import jax.numpy as jnp
import numpy as np
from jax import lax
from jax.experimental import pallas as pl
from jax.experimental.pallas import tpu as pltpu
from jax.sharding import PartitionSpec as P

lgl_nodes = np.array(
    [
        -1.0,
        -0.8717401485096066,
        -0.5917001814331423,
        -0.2092992179024789,
        0.2092992179024789,
        0.5917001814331423,
        0.8717401485096066,
        1.0,
    ]
)
lift_weight = 28.0
earth_pressure = 1.2
friction = 0.4
slope_x = 0.3
slope_y = 0.1
time_step = 0.01
face_nodes = np.array(
    [
        [8 * r for r in range(8)],
        [8 * r + 7 for r in range(8)],
        [r for r in range(8)],
        [56 + r for r in range(8)],
    ]
)
inner_nodes = np.array([8 * iy + ix for iy in range(1, 7) for ix in range(1, 7)])
opposite = [1, 0, 3, 2]
outward = [-1.0, 1.0, -1.0, 1.0]

DEVICES = 128
ELEMS = 512
SLOTS = 8
LANES = 128
MAIN = 32
OUTER = 32
EXTRA = 16
INNER = 3 * MAIN + EXTRA
FLAG = 12
INNER_ROWS = 7
OUTER_ROWS = 6
CROSS = 32
NAME_BASE = 2
MESH = pl.DeviceIdType.MESH
bf16 = jnp.bfloat16
f32 = jnp.float32


def lagrange_table(points):
    values_table = np.ones((len(points), 8))
    for j in range(8):
        for m in range(8):
            if m != j:
                values_table[:, j] = (
                    values_table[:, j] * (points - lgl_nodes[m]) / (lgl_nodes[j] - lgl_nodes[m])
                )
    return values_table


def basis_tables():
    bary = np.array(
        [1.0 / np.prod([lgl_nodes[j] - lgl_nodes[m] for m in range(8) if m != j]) for j in range(8)]
    )
    derivative = np.zeros((8, 8))
    for i in range(8):
        for j in range(8):
            if i != j:
                derivative[i, j] = bary[j] / bary[i] / (lgl_nodes[i] - lgl_nodes[j])
        derivative[i, i] = -np.sum(derivative[i])
    identity = np.eye(8)
    lower_half = lagrange_table((lgl_nodes - 1.0) / 2.0)
    upper_half = lagrange_table((lgl_nodes + 1.0) / 2.0)
    halves = [lower_half, upper_half]
    prolong = np.stack(
        [
            np.kron(halves[row_half], halves[col_half])
            for row_half in range(2)
            for col_half in range(2)
        ]
    )
    return np.kron(identity, derivative), np.kron(derivative, identity), prolong


def two_parts(table):
    high = np.asarray(table, np.float32).astype(bf16)
    low = (np.asarray(table, np.float64) - high.astype(np.float64)).astype(bf16)
    return high, low


def corner_copy(face_id, r):
    return face_id < 2 and r in (0, 7)


def step_table():
    deriv_x, deriv_y, _ = basis_tables()
    full = np.concatenate([np.eye(64), deriv_x, deriv_y], axis=1)
    table = np.zeros((3, MAIN + OUTER + EXTRA, 192))
    for field in range(3):
        table[field, :MAIN] = full[inner_nodes[:MAIN]]
        for face_id in range(4):
            for r in range(8):
                if not corner_copy(face_id, r):
                    table[field, MAIN + 8 * face_id + r] = full[face_nodes[face_id][r]]
        start = MAIN + OUTER + 4 * field
        table[field, start : start + 4] = full[inner_nodes[MAIN:]]
    high, low = two_parts(table.reshape(-1, 192))
    return np.concatenate([high, high, low[:, 64:]], axis=1)


def child_tables():
    _, _, prolong = basis_tables()
    rows = np.concatenate([prolong.reshape(256, 64), np.eye(64)], axis=0)
    tables = []
    for shift in (0, 4):
        table = np.zeros((320, 80))
        table[:, :MAIN] = rows[:, inner_nodes[:MAIN]]
        for face_id in range(4):
            for r in range(8):
                table[:, MAIN + 8 * face_id + r] = rows[:, face_nodes[face_id][r]]
        start = MAIN + OUTER + shift
        table[:, start : start + 4] = rows[:, inner_nodes[MAIN:]]
        high, low = two_parts(table)
        tables.append(np.concatenate([high, high, low, np.zeros((320, 16), bf16)], axis=1))
    return np.stack(tables)


def distances(seed, far_first):
    order = [
        (z, y, x, c) for z in range(4) for y in range(4) for x in range(4) for c in range(2)
    ][1:]
    random.Random(seed).shuffle(order)
    if far_first:
        order.sort(key=lambda d: -sum(min(v, 4 - v) for v in d[:3]))
    return order


def split2(values):
    high = values.astype(bf16)
    return high, (values - high.astype(f32)).astype(bf16)


def face_flux(values, face_id):
    depth, moment_x, moment_y = values
    inv = 1.0 / depth
    pressure = 0.5 * earth_pressure * depth * depth
    sign = outward[face_id]
    if face_id < 2:
        normal = moment_x * inv
        terms = [moment_x, moment_x * normal + pressure, moment_y * normal]
    else:
        normal = moment_y * inv
        terms = [moment_y, moment_x * normal, moment_y * normal + pressure]
    return [sign * t for t in terms], jnp.abs(normal) + jnp.sqrt(earth_pressure * depth)


def mirror(values, face_id):
    if face_id < 2:
        return [values[0], -values[1], values[2]]
    return [values[0], values[1], -values[2]]


def step_kernel(
    state_in, neighbours_in, metric_in, flags_in, owner_in, table_in, tables_in,
    inner_turned_out, outer_in, tables_out,
    state, neighbours, metric, flags, owner, table,
    tiles, trace, own_flux, across, crossing, ghost,
    placed, inner_out, outer_out, inner_in, inner_turned, onehot,
    load_sem, halo_send, halo_recv, inner_send, inner_recv, outer_send, outer_recv, own_sem,
):
    pairs = (
        (state_in, state), (neighbours_in, neighbours), (metric_in, metric),
        (flags_in, flags), (owner_in, owner), (table_in, table),
    )
    loads = [pltpu.make_async_copy(a, b, load_sem.at[i]) for i, (a, b) in enumerate(pairs)]
    for load in loads:
        load.start()

    me = lax.axis_index("curve")
    z_part = [lax.rem(me // 32 + z, 4) * 32 for z in range(4)]
    y_part = [lax.rem((me // 8) % 4 + y, 4) * 8 for y in range(4)]
    x_part = [lax.rem((me // 2) % 4 + x, 4) * 2 for x in range(4)]
    c_part = [lax.rem(me % 2 + c, 2) for c in range(2)]
    zy_part = [[z + y for y in y_part] for z in z_part]
    xc_part = [[x + c for c in c_part] for x in x_part]

    def others(seed, far_first):
        return [zy_part[z][y] + xc_part[x][c] for z, y, x, c in distances(seed, far_first)]

    barrier = pltpu.get_barrier_semaphore()
    for to in others(0, True):
        pl.semaphore_signal(barrier, inc=1, device_id=(to,), device_id_type=MESH)
    for load in loads:
        load.wait()

    partners = neighbours[...]
    distance = jnp.where(lax.broadcasted_iota(jnp.int32, (4, ELEMS), 0) < 2, 1, 32)
    homes = lax.shift_right_arithmetic(partners, 9)
    real = partners >= 0
    below = jnp.where(real & (homes == me - distance), 1.0, 0.0)
    above = jnp.where(real & (homes == me + distance), 1.0, 0.0)
    owners = owner[...]
    hits = owners == lax.broadcasted_iota(jnp.int32, (DEVICES, ELEMS), 0)
    hits = jnp.where(hits, 1.0, 0.0)
    earlier = lax.broadcasted_iota(jnp.int32, (ELEMS, ELEMS), 0) < lax.broadcasted_iota(
        jnp.int32, (ELEMS, ELEMS), 1
    )
    nothing = jnp.zeros((4, ELEMS), f32)
    before = jnp.dot(
        jnp.concatenate([hits, below, nothing, above, nothing], axis=0).astype(bf16),
        jnp.where(earlier, 1.0, 0.0).astype(bf16),
        preferred_element_type=f32,
    )
    rank = jnp.sum(hits * before[:DEVICES], axis=0, keepdims=True)
    column = owners * SLOTS + rank.astype(jnp.int32)
    slot_rows = lax.broadcasted_iota(jnp.int32, (DEVICES * SLOTS, ELEMS), 0)
    onehot[...] = jnp.where(slot_rows == column, 1.0, 0.0).astype(bf16)
    spot = jnp.where(
        below > 0.5,
        before[DEVICES : DEVICES + 4],
        jnp.where(above > 0.5, before[DEVICES + 8 : DEVICES + 12] + CROSS, -1000.0),
    ).astype(jnp.int32)

    for t in range(ELEMS // LANES):
        tiles[192 * t : 192 * t + 192, :] = state[:, LANES * t : LANES * t + LANES]
    for face_id in range(4):
        for field in range(3):
            at = (face_id % 2) * 24 + field * 8
            if face_id < 2:
                for t in range(ELEMS // LANES):
                    start = 192 * t + 64 * field + 7 * face_id
                    trace[0, at : at + 8, LANES * t : LANES * t + LANES] = tiles[
                        pl.ds(start, 8, stride=8), :
                    ]
            else:
                start = 64 * field + 56 * (face_id - 2)
                trace[1, at : at + 8, :] = state[start : start + 8, :]

    first_row = lax.broadcasted_iota(jnp.int32, (8, ELEMS), 0) == 0
    name = (
        lax.broadcasted_iota(jnp.int32, (8, ELEMS), 1) + (me * ELEMS + NAME_BASE)
    ).astype(f32)
    name = jnp.where(first_row, name, 0.0)
    lane_rows = lax.broadcasted_iota(jnp.int32, (LANES, ELEMS), 0)
    nt_dims = (((1,), (1,)), ((), ()))
    for pair in (0, 1):
        packed = None
        for position in (0, 1):
            face_id = 2 * pair + position
            rows = jnp.concatenate([trace[pair, 24 * position : 24 * position + 24, :], name])
            chosen = lane_rows == spot[face_id : face_id + 1] + 2 * CROSS * position
            part = lax.dot_general(
                jnp.concatenate(split2(rows), axis=0),
                jnp.where(chosen, 1.0, 0.0).astype(bf16),
                nt_dims,
                preferred_element_type=f32,
            )
            packed = part if packed is None else packed + part
        crossing[pair] = packed[:32] + packed[32:]

    scale = (-time_step) * metric[...]
    depth, moment_x, moment_y = (state[64 * f : 64 * f + 64, :] for f in range(3))
    inv = 1.0 / depth
    speed_x, speed_y = moment_x * inv, moment_y * inv
    pressure = 0.5 * earth_pressure * depth * depth
    drag = friction / jnp.sqrt(speed_x * speed_x + speed_y * speed_y + 1.0)
    cross = moment_x * speed_y
    parts = [
        (depth, moment_x, moment_y),
        (
            moment_x + time_step * (depth * (slope_x - drag * speed_x)),
            moment_x * speed_x + pressure,
            cross,
        ),
        (
            moment_y + time_step * (depth * (slope_y - drag * speed_y)),
            cross,
            moment_y * speed_y + pressure,
        ),
    ]
    stepped = []
    for q, flux_x, flux_y in parts:
        q_high, q_low = split2(q)
        x_high, x_low = split2(scale * flux_x)
        y_high, y_low = split2(scale * flux_y)
        operand = jnp.concatenate(
            [q_high, x_high, y_high, q_low, x_low, y_low, x_high, y_high], axis=0
        )
        rows = slice(80 * len(stepped), 80 * len(stepped) + 80)
        stepped.append(jnp.dot(table[rows, :], operand, preferred_element_type=f32))

    def place(rows):
        both = lax.dot_general(
            onehot[...],
            jnp.concatenate(split2(rows), axis=0),
            nt_dims,
            preferred_element_type=f32,
        )
        placed[...] = both[:, :LANES] + both[:, LANES:]
        return [placed[pl.ds(j, DEVICES, stride=SLOTS), :] for j in range(SLOTS)]

    lane_at = lax.broadcasted_iota(jnp.int32, (DEVICES, LANES), 1)
    extra = stepped[0][-EXTRA:] + stepped[1][-EXTRA:] + stepped[2][-EXTRA:]
    flag_row = lax.broadcasted_iota(jnp.int32, (EXTRA, ELEMS), 0) == FLAG
    extra = extra + jnp.where(flag_row, flags[...].astype(f32), 0.0)
    slots = place(
        jnp.concatenate(
            [s[:MAIN] for s in stepped] + [extra, jnp.zeros((LANES - INNER, ELEMS), f32)], axis=0
        )
    )
    for r in range(INNER_ROWS):
        tail = pltpu.roll(slots[7], INNER - 16 * r, 1)
        inner_out[pl.ds(r, DEVICES, stride=8), :] = jnp.where(lane_at < INNER, slots[r], tail)

    for face_id in range(4):
        pair = face_id // 2
        at = (face_id % 2) * 24
        inside = [trace[pair, at + 8 * field : at + 8 * field + 8, :] for field in range(3)]
        flux_in, wave_in = face_flux(inside, face_id)
        for i, values in enumerate(flux_in + [wave_in]):
            own_flux[face_id, 8 * i : 8 * i + 8, :] = values
        partner = partners[face_id : face_id + 1]
        local = jnp.bitwise_and(partner, ELEMS - 1)
        piece = lax.shift_right_arithmetic(local, 7)
        lane = jnp.bitwise_and(local, LANES - 1)
        at = (opposite[face_id] % 2) * 24
        for t in range(ELEMS // LANES):
            cols = slice(t * LANES, (t + 1) * LANES)
            index = jnp.broadcast_to(lane[:, cols], (8, LANES))
            piece_t = jnp.broadcast_to(piece[:, cols], (8, LANES))
            for field in range(3):
                rows = slice(at + field * 8, at + field * 8 + 8)
                found = None
                for c in range(ELEMS // LANES):
                    values = trace[pair, rows, c * LANES : (c + 1) * LANES]
                    got = jnp.take_along_axis(values, index, axis=1, mode="promise_in_bounds")
                    found = got if c == 0 else jnp.where(piece_t == c, got, found)
                across[face_id, 8 * field : 8 * field + 8, cols] = found

    pl.semaphore_wait(barrier, DEVICES - 1)

    def halo(pair, upward):
        far = 32 if pair else 1
        target = lax.rem(me + (far if upward else DEVICES - far), DEVICES)
        side = 0 if upward else 1
        return pltpu.make_async_remote_copy(
            src_ref=crossing.at[pair],
            dst_ref=ghost.at[pair, side],
            send_sem=halo_send.at[pair, side],
            recv_sem=halo_recv.at[pair, side],
            device_id=(target,),
            device_id_type=MESH,
        )

    halos = [halo(pair, upward) for pair in (0, 1) for upward in (True, False)]
    for copy in halos:
        copy.start()

    def block(ref, device, rows):
        return ref.at[pl.ds(pl.multiple_of(device * 8, 8), rows)]

    def exchange(order, source, target, rows, send_sem, recv_sem):
        for to in order:
            pltpu.make_async_remote_copy(
                src_ref=block(source, to, rows),
                dst_ref=block(target, me, rows),
                send_sem=send_sem,
                recv_sem=recv_sem,
                device_id=(to,),
                device_id_type=MESH,
            ).start()

    exchange(others(2, False), inner_out, inner_in, INNER_ROWS, inner_send, inner_recv)
    own_inner = pltpu.make_async_copy(
        block(inner_out, me, INNER_ROWS), block(inner_in, me, INNER_ROWS), own_sem.at[0]
    )
    own_inner.start()

    for copy in halos:
        copy.wait()

    lift_scale = (time_step * lift_weight * 0.5) * metric[...]
    from_below = jnp.bitwise_and(lax.broadcasted_iota(jnp.int32, (32, LANES), 1), CROSS) != 0
    named = (partners + NAME_BASE).astype(f32)
    lifted = [[None] * 4 for _ in range(3)]
    zeros = jnp.zeros((2 * CROSS, ELEMS), bf16)
    for pair in (0, 1):
        merged = jnp.where(from_below, ghost[pair, 0], ghost[pair, 1])
        names = jnp.transpose(merged[24:32])[:, 0:1]
        chosen = []
        for position in (0, 1):
            face_id = 2 * pair + position
            start = 2 * CROSS * (1 - position)
            match = names[start : start + 2 * CROSS] == named[face_id : face_id + 1]
            match = jnp.where(match, 1.0, 0.0).astype(bf16)
            chosen.append(jnp.concatenate([zeros, match] if start else [match, zeros], axis=0))
        got = jnp.dot(
            jnp.concatenate(split2(merged), axis=0),
            jnp.concatenate(chosen, axis=1),
            preferred_element_type=f32,
        )
        got = got[:32] + got[32:]
        for position in (0, 1):
            face_id = 2 * pair + position
            wall = jnp.logical_not(real[face_id : face_id + 1])
            local = homes[face_id : face_id + 1] == me
            at = position * 24
            inside = [trace[pair, at + 8 * field : at + 8 * field + 8, :] for field in range(3)]
            reflected = mirror(inside, face_id)
            outside = []
            for field in range(3):
                rows = slice(8 * field, 8 * field + 8)
                there = got[rows, ELEMS * position : ELEMS * position + ELEMS]
                there = jnp.where(local, across[face_id, rows, :], there)
                outside.append(jnp.where(wall, reflected[field], there))
            flux_out, wave_out = face_flux(outside, face_id)
            largest = jnp.maximum(own_flux[face_id, 24:32, :], wave_out)
            for field in range(3):
                jump = own_flux[face_id, 8 * field : 8 * field + 8, :] - flux_out[field]
                lifted[field][face_id] = lift_scale * (
                    jump + largest * (outside[field] - inside[field])
                )
    outer = [
        stepped[field][MAIN : MAIN + OUTER] + jnp.concatenate(lifted[field], axis=0)
        for field in range(3)
    ]
    slots = place(jnp.concatenate(outer + [jnp.zeros((LANES - 96, ELEMS), f32)], axis=0))
    for r in range(4):
        pair_of = jnp.where(lane_at < 64, slots[r], pltpu.roll(slots[r + 4], 64, 1))
        outer_out[pl.ds(r, DEVICES, stride=8), :] = pair_of
    for q in range(2):
        row = pltpu.roll(slots[4 * q], 64, 1)
        for k in range(1, 4):
            piece = slots[4 * q + k] if k == 2 else pltpu.roll(slots[4 * q + k], (32 * k - 64) % 128, 1)
            row = jnp.where(lane_at >= 32 * k, piece, row)
        outer_out[pl.ds(4 + q, DEVICES, stride=8), :] = row

    exchange(others(1, True), outer_out, outer_in, OUTER_ROWS, outer_send, outer_recv)
    own_outer = pltpu.make_async_copy(
        block(outer_out, me, OUTER_ROWS), block(outer_in, me, OUTER_ROWS), own_sem.at[1]
    )
    own_outer.start()

    def wait_all(source, target, rows, send_sem, recv_sem):
        every = pl.ds(0, (DEVICES - 1) * rows)
        copies = pltpu.make_async_remote_copy(
            src_ref=source.at[every],
            dst_ref=target.at[every],
            send_sem=send_sem,
            recv_sem=recv_sem,
            device_id=(me,),
            device_id_type=MESH,
        )
        copies.wait_send()
        copies.wait_recv()

    tables_load = pltpu.make_async_copy(tables_in, tables_out, own_sem.at[3])
    tables_load.start()
    own_inner.wait()
    wait_all(inner_out, inner_in, INNER_ROWS, inner_send, inner_recv)
    last = None
    for r in range(INNER_ROWS):
        tail = pltpu.roll(inner_in[pl.ds(r, DEVICES, stride=8), :], 16 * r + 16, 1)
        last = tail if r == 0 else jnp.where(lane_at >= 16 * r, tail, last)
    inner_in[pl.ds(7, DEVICES, stride=8), :] = last
    inner_turned[...] = jnp.transpose(inner_in[...])[:INNER]
    turned = pltpu.make_async_copy(inner_turned, inner_turned_out, own_sem.at[2])
    turned.start()
    own_outer.wait()
    turned.wait()
    tables_load.wait()
    wait_all(outer_out, outer_in, OUTER_ROWS, outer_send, outer_recv)


def child_kernel(inner, outer, tables, out_hbm, flat, out, store_sem):
    lane_at = lax.broadcasted_iota(jnp.int32, (DEVICES, LANES), 1)
    for j in range(SLOTS):
        body = outer[pl.ds(j % 4, DEVICES, stride=8), :]
        rest = outer[pl.ds(4 + j // 4, DEVICES, stride=8), :]
        body = pltpu.roll(body, 64, 1) if j >= 4 else body
        rest = rest if j % 4 == 2 else pltpu.roll(rest, (64 - 32 * (j % 4)) % 128, 1)
        flat[pl.ds(j, DEVICES, stride=8), :] = jnp.where(lane_at < 64, body, rest)
    faces = jnp.transpose(flat[...])
    slots = DEVICES * SLOTS
    refined = inner[3 * MAIN + FLAG : 3 * MAIN + FLAG + 1, :] > 0.5
    stores = []
    for field in range(3):
        own = slice(MAIN * field, MAIN * field + MAIN)
        start = 3 * MAIN + 8 * (field // 2)
        values = jnp.concatenate(
            [inner[own, :], faces[own], inner[start : start + 8, :], jnp.zeros((8, slots), f32)],
            axis=0,
        )
        high, low = split2(values)
        operand = jnp.concatenate([high, low, high, jnp.zeros((16, slots), bf16)], axis=0)
        nodes = jnp.dot(tables[field % 2], operand, preferred_element_type=f32)
        for c in range(4):
            start = 192 * c + 64 * field
            rows = pl.ds(start, 64)
            other = nodes[256:320] if c == 0 else 0.0
            out[start : start + 64, :] = jnp.where(refined, nodes[64 * c : 64 * c + 64], other)
            store = pltpu.make_async_copy(
                out.at[rows], out_hbm.at[rows], store_sem.at[4 * field + c]
            )
            store.start()
            stores.append(store)
    for store in stores:
        store.wait()


def on_device(state, neighbours, metric, flags, new_owner):
    hbm = pl.BlockSpec(memory_space=pl.ANY)
    slots = DEVICES * SLOTS
    buffer = pltpu.VMEM((slots, LANES), f32)
    dma = pltpu.SemaphoreType.DMA
    inner, outer, tables = pl.pallas_call(
        step_kernel,
        out_shape=(
            jax.ShapeDtypeStruct((INNER, slots), f32),
            jax.ShapeDtypeStruct((slots, LANES), f32),
            jax.ShapeDtypeStruct((2, 320, 256), bf16),
        ),
        in_specs=[pl.BlockSpec(memory_space=pltpu.HBM)] * 7,
        out_specs=(hbm, hbm, hbm),
        scratch_shapes=[
            pltpu.VMEM((192, ELEMS), f32),
            pltpu.VMEM((4, ELEMS), jnp.int32),
            pltpu.VMEM((1, ELEMS), f32),
            pltpu.VMEM((1, ELEMS), jnp.int32),
            pltpu.VMEM((1, ELEMS), jnp.int32),
            pltpu.VMEM((240, 512), bf16),
            pltpu.VMEM((192 * ELEMS // LANES, LANES), f32),
            pltpu.VMEM((2, 48, ELEMS), f32),
            pltpu.VMEM((4, 32, ELEMS), f32),
            pltpu.VMEM((4, 24, ELEMS), f32),
            pltpu.VMEM((2, 32, LANES), f32),
            pltpu.VMEM((2, 2, 32, LANES), f32),
            buffer,
            buffer,
            buffer,
            buffer,
            pltpu.VMEM((INNER, slots), f32),
            pltpu.VMEM((slots, ELEMS), bf16),
            dma((6,)),
            dma((2, 2)),
            dma((2, 2)),
            dma,
            dma,
            dma,
            dma,
            dma((4,)),
        ],
        compiler_params=pltpu.CompilerParams(collective_id=0, has_side_effects=True, vmem_limit_bytes=16 << 20),
        name="step_and_migrate",
    )(
        *(
            pltpu.with_memory_space_constraint(x, pltpu.HBM)
            for x in (
                state.reshape(192, ELEMS),
                neighbours,
                metric.reshape(1, ELEMS),
                flags.reshape(1, ELEMS),
                new_owner.reshape(1, ELEMS),
                jnp.asarray(step_table(), bf16),
                jnp.asarray(child_tables(), bf16),
            )
        )
    )
    children = pl.pallas_call(
        child_kernel,
        out_shape=jax.ShapeDtypeStruct((768, slots), f32),
        in_specs=[pl.BlockSpec(memory_space=pltpu.VMEM)] * 3,
        out_specs=pl.BlockSpec(memory_space=pltpu.HBM),
        scratch_shapes=[
            buffer,
            pltpu.VMEM((768, slots), f32),
            dma((12,)),
        ],
        compiler_params=pltpu.CompilerParams(vmem_limit_bytes=16 << 20),
        name="make_children",
    )(inner, outer, tables)
    return children.reshape(4, 3, 64, slots)


def solution(mesh):
    placed = (P(None, None, "curve"), P(None, "curve"), P("curve"), P("curve"), P("curve", None))
    return jax.shard_map(
        on_device,
        mesh=mesh,
        in_specs=placed,
        out_specs=P(None, None, None, "curve"),
        check_vma=False,
    )
```

```python
import random

import jax
import jax.numpy as jnp
import numpy as np
from jax import lax
from jax.experimental import pallas as pl
from jax.experimental.pallas import tpu as pltpu
from jax.sharding import PartitionSpec as P

lgl_nodes = np.array(
    [
        -1.0,
        -0.8717401485096066,
        -0.5917001814331423,
        -0.2092992179024789,
        0.2092992179024789,
        0.5917001814331423,
        0.8717401485096066,
        1.0,
    ]
)
lift_weight = 28.0
earth_pressure = 1.2
friction = 0.4
slope_x = 0.3
slope_y = 0.1
time_step = 0.01
face_nodes = np.array(
    [
        [8 * r for r in range(8)],
        [8 * r + 7 for r in range(8)],
        [r for r in range(8)],
        [56 + r for r in range(8)],
    ]
)
inner_nodes = np.array([8 * iy + ix for iy in range(1, 7) for ix in range(1, 7)])
opposite = [1, 0, 3, 2]
outward = [-1.0, 1.0, -1.0, 1.0]

DEVICES = 128
ELEMS = 512
SLOTS = 8
LANES = 128
MAIN = 32
OUTER = 32
EXTRA = 16
INNER = 3 * MAIN + EXTRA
FLAG = 12
INNER_ROWS = 7
OUTER_ROWS = 6
CROSS = 32
NAME_BASE = 2
MESH = pl.DeviceIdType.MESH
bf16 = jnp.bfloat16
f32 = jnp.float32


def lagrange_table(points):
    values_table = np.ones((len(points), 8))
    for j in range(8):
        for m in range(8):
            if m != j:
                values_table[:, j] = (
                    values_table[:, j] * (points - lgl_nodes[m]) / (lgl_nodes[j] - lgl_nodes[m])
                )
    return values_table


def basis_tables():
    bary = np.array(
        [1.0 / np.prod([lgl_nodes[j] - lgl_nodes[m] for m in range(8) if m != j]) for j in range(8)]
    )
    derivative = np.zeros((8, 8))
    for i in range(8):
        for j in range(8):
            if i != j:
                derivative[i, j] = bary[j] / bary[i] / (lgl_nodes[i] - lgl_nodes[j])
        derivative[i, i] = -np.sum(derivative[i])
    identity = np.eye(8)
    lower_half = lagrange_table((lgl_nodes - 1.0) / 2.0)
    upper_half = lagrange_table((lgl_nodes + 1.0) / 2.0)
    halves = [lower_half, upper_half]
    prolong = np.stack(
        [
            np.kron(halves[row_half], halves[col_half])
            for row_half in range(2)
            for col_half in range(2)
        ]
    )
    return np.kron(identity, derivative), np.kron(derivative, identity), prolong


def two_parts(table):
    high = np.asarray(table, np.float32).astype(bf16)
    low = (np.asarray(table, np.float64) - high.astype(np.float64)).astype(bf16)
    return high, low


def corner_copy(face_id, r):
    return face_id < 2 and r in (0, 7)


def step_table():
    deriv_x, deriv_y, _ = basis_tables()
    full = np.concatenate([np.eye(64), deriv_x, deriv_y], axis=1)
    table = np.zeros((3, MAIN + OUTER + EXTRA, 192))
    for field in range(3):
        table[field, :MAIN] = full[inner_nodes[:MAIN]]
        for face_id in range(4):
            for r in range(8):
                if not corner_copy(face_id, r):
                    table[field, MAIN + 8 * face_id + r] = full[face_nodes[face_id][r]]
        start = MAIN + OUTER + 4 * field
        table[field, start : start + 4] = full[inner_nodes[MAIN:]]
    high, low = two_parts(table.reshape(-1, 192))
    return np.concatenate([high, high, low[:, 64:]], axis=1)


def child_tables():
    _, _, prolong = basis_tables()
    rows = np.concatenate([prolong.reshape(256, 64), np.eye(64)], axis=0)
    tables = []
    for shift in (0, 4):
        table = np.zeros((320, 80))
        table[:, :MAIN] = rows[:, inner_nodes[:MAIN]]
        for face_id in range(4):
            for r in range(8):
                table[:, MAIN + 8 * face_id + r] = rows[:, face_nodes[face_id][r]]
        start = MAIN + OUTER + shift
        table[:, start : start + 4] = rows[:, inner_nodes[MAIN:]]
        high, low = two_parts(table)
        tables.append(np.concatenate([high, high, low, np.zeros((320, 16), bf16)], axis=1))
    return np.stack(tables)


def distances(seed, far_first):
    order = [
        (z, y, x, c) for z in range(4) for y in range(4) for x in range(4) for c in range(2)
    ][1:]
    random.Random(seed).shuffle(order)
    if far_first:
        order.sort(key=lambda d: -sum(min(v, 4 - v) for v in d[:3]))
    return order


def split2(values):
    high = values.astype(bf16)
    return high, (values - high.astype(f32)).astype(bf16)


def face_flux(values, face_id):
    depth, moment_x, moment_y = values
    inv = 1.0 / depth
    pressure = 0.5 * earth_pressure * depth * depth
    sign = outward[face_id]
    if face_id < 2:
        normal = moment_x * inv
        terms = [moment_x, moment_x * normal + pressure, moment_y * normal]
    else:
        normal = moment_y * inv
        terms = [moment_y, moment_x * normal, moment_y * normal + pressure]
    return [sign * t for t in terms], jnp.abs(normal) + jnp.sqrt(earth_pressure * depth)


def mirror(values, face_id):
    if face_id < 2:
        return [values[0], -values[1], values[2]]
    return [values[0], values[1], -values[2]]


def step_kernel(
    state_in, neighbours_in, metric_in, flags_in, owner_in, table_in, tables_in,
    inner_turned_out, outer_in, tables_out,
    state, neighbours, metric, flags, owner, table,
    tiles, trace, own_flux, across, crossing, ghost,
    inner_out, outer_out, inner_in, inner_turned, onehot,
    load_sem, halo_send, halo_recv, inner_send, inner_recv, outer_send, outer_recv, own_sem,
):
    pairs = (
        (state_in, state), (neighbours_in, neighbours), (metric_in, metric),
        (flags_in, flags), (owner_in, owner), (table_in, table),
    )
    loads = [pltpu.make_async_copy(a, b, load_sem.at[i]) for i, (a, b) in enumerate(pairs)]
    for load in loads:
        load.start()

    me = lax.axis_index("curve")
    z_part = [lax.rem(me // 32 + z, 4) * 32 for z in range(4)]
    y_part = [lax.rem((me // 8) % 4 + y, 4) * 8 for y in range(4)]
    x_part = [lax.rem((me // 2) % 4 + x, 4) * 2 for x in range(4)]
    c_part = [lax.rem(me % 2 + c, 2) for c in range(2)]
    zy_part = [[z + y for y in y_part] for z in z_part]
    xc_part = [[x + c for c in c_part] for x in x_part]

    def others(seed, far_first):
        return [zy_part[z][y] + xc_part[x][c] for z, y, x, c in distances(seed, far_first)]

    barrier = pltpu.get_barrier_semaphore()
    for to in others(0, True):
        pl.semaphore_signal(barrier, inc=1, device_id=(to,), device_id_type=MESH)
    for load in loads:
        load.wait()

    partners = neighbours[...]
    distance = jnp.where(lax.broadcasted_iota(jnp.int32, (4, ELEMS), 0) < 2, 1, 32)
    homes = lax.shift_right_arithmetic(partners, 9)
    real = partners >= 0
    below = jnp.where(real & (homes == me - distance), 1.0, 0.0)
    above = jnp.where(real & (homes == me + distance), 1.0, 0.0)
    owners = owner[...]
    hits = owners == lax.broadcasted_iota(jnp.int32, (DEVICES, ELEMS), 0)
    hits = jnp.where(hits, 1.0, 0.0)
    nothing = jnp.zeros((4, ELEMS), f32)
    marks = jnp.concatenate([hits, below, nothing, above, nothing], axis=0).astype(bf16)
    at_row = lax.broadcasted_iota(jnp.int32, (LANES, 2 * LANES), 0)
    at_lane = lax.broadcasted_iota(jnp.int32, (LANES, 2 * LANES), 1)
    earlier = jnp.where((at_row < at_lane) | (at_lane >= LANES), 1.0, 0.0).astype(bf16)
    before, total = [], None
    for t in range(ELEMS // LANES):
        count = jnp.dot(
            marks[:, LANES * t : LANES * t + LANES], earlier, preferred_element_type=f32
        )
        before.append(count[:, :LANES] if t == 0 else count[:, :LANES] + total)
        total = count[:, LANES:] if t == 0 else count[:, LANES:] + total
    before = jnp.concatenate(before, axis=1)
    rank = jnp.sum(hits * before[:DEVICES], axis=0, keepdims=True)
    column = rank.astype(jnp.int32) * DEVICES + owners
    slot_rows = lax.broadcasted_iota(jnp.int32, (DEVICES * SLOTS, ELEMS), 0)
    onehot[...] = jnp.where(slot_rows == column, 1.0, 0.0).astype(bf16)
    spot = jnp.where(
        below > 0.5,
        before[DEVICES : DEVICES + 4],
        jnp.where(above > 0.5, before[DEVICES + 8 : DEVICES + 12] + CROSS, -1000.0),
    ).astype(jnp.int32)

    for t in range(ELEMS // LANES):
        tiles[192 * t : 192 * t + 192, :] = state[:, LANES * t : LANES * t + LANES]
    for face_id in range(4):
        for field in range(3):
            at = (face_id % 2) * 24 + field * 8
            if face_id < 2:
                for t in range(ELEMS // LANES):
                    start = 192 * t + 64 * field + 7 * face_id
                    trace[0, at : at + 8, LANES * t : LANES * t + LANES] = tiles[
                        pl.ds(start, 8, stride=8), :
                    ]
            else:
                start = 64 * field + 56 * (face_id - 2)
                trace[1, at : at + 8, :] = state[start : start + 8, :]

    first_row = lax.broadcasted_iota(jnp.int32, (8, ELEMS), 0) == 0
    name = (
        lax.broadcasted_iota(jnp.int32, (8, ELEMS), 1) + (me * ELEMS + NAME_BASE)
    ).astype(f32)
    name = jnp.where(first_row, name, 0.0)
    lane_rows = lax.broadcasted_iota(jnp.int32, (LANES, ELEMS), 0)
    nt_dims = (((1,), (1,)), ((), ()))
    for pair in (0, 1):
        packed = None
        for position in (0, 1):
            face_id = 2 * pair + position
            rows = jnp.concatenate([trace[pair, 24 * position : 24 * position + 24, :], name])
            chosen = lane_rows == spot[face_id : face_id + 1] + 2 * CROSS * position
            part = lax.dot_general(
                jnp.concatenate(split2(rows), axis=0),
                jnp.where(chosen, 1.0, 0.0).astype(bf16),
                nt_dims,
                preferred_element_type=f32,
            )
            packed = part if packed is None else packed + part
        crossing[pair] = packed[:32] + packed[32:]

    scale = (-time_step) * metric[...]
    depth, moment_x, moment_y = (state[64 * f : 64 * f + 64, :] for f in range(3))
    inv = 1.0 / depth
    speed_x, speed_y = moment_x * inv, moment_y * inv
    pressure = 0.5 * earth_pressure * depth * depth
    drag = friction / jnp.sqrt(speed_x * speed_x + speed_y * speed_y + 1.0)
    cross = moment_x * speed_y
    parts = [
        (depth, moment_x, moment_y),
        (
            moment_x + time_step * (depth * (slope_x - drag * speed_x)),
            moment_x * speed_x + pressure,
            cross,
        ),
        (
            moment_y + time_step * (depth * (slope_y - drag * speed_y)),
            cross,
            moment_y * speed_y + pressure,
        ),
    ]
    stepped = []
    for q, flux_x, flux_y in parts:
        q_high, q_low = split2(q)
        x_high, x_low = split2(scale * flux_x)
        y_high, y_low = split2(scale * flux_y)
        operand = jnp.concatenate(
            [q_high, x_high, y_high, q_low, x_low, y_low, x_high, y_high], axis=0
        )
        rows = slice(80 * len(stepped), 80 * len(stepped) + 80)
        stepped.append(jnp.dot(table[rows, :], operand, preferred_element_type=f32))

    def place(rows):
        both = lax.dot_general(
            onehot[...],
            jnp.concatenate(split2(rows), axis=0),
            nt_dims,
            preferred_element_type=f32,
        )
        both = both[:, :LANES] + both[:, LANES:]
        return [both[j * DEVICES : (j + 1) * DEVICES] for j in range(SLOTS)]

    lane_at = lax.broadcasted_iota(jnp.int32, (DEVICES, LANES), 1)
    extra = stepped[0][-EXTRA:] + stepped[1][-EXTRA:] + stepped[2][-EXTRA:]
    flag_row = lax.broadcasted_iota(jnp.int32, (EXTRA, ELEMS), 0) == FLAG
    extra = extra + jnp.where(flag_row, flags[...].astype(f32), 0.0)
    slots = place(
        jnp.concatenate(
            [s[:MAIN] for s in stepped] + [extra, jnp.zeros((LANES - INNER, ELEMS), f32)], axis=0
        )
    )
    for r in range(INNER_ROWS):
        tail = pltpu.roll(slots[7], INNER - 16 * r, 1)
        inner_out[pl.ds(r, DEVICES, stride=8), :] = jnp.where(lane_at < INNER, slots[r], tail)

    pl.semaphore_wait(barrier, DEVICES - 1)

    def halo(pair, upward):
        far = 32 if pair else 1
        target = lax.rem(me + (far if upward else DEVICES - far), DEVICES)
        side = 0 if upward else 1
        return pltpu.make_async_remote_copy(
            src_ref=crossing.at[pair],
            dst_ref=ghost.at[pair, side],
            send_sem=halo_send.at[pair, side],
            recv_sem=halo_recv.at[pair, side],
            device_id=(target,),
            device_id_type=MESH,
        )

    halos = [halo(pair, upward) for pair in (0, 1) for upward in (True, False)]
    for copy in halos:
        copy.start()

    def block(ref, device, rows):
        return ref.at[pl.ds(pl.multiple_of(device * 8, 8), rows)]

    def exchange(order, source, target, rows, send_sem, recv_sem):
        for to in order:
            pltpu.make_async_remote_copy(
                src_ref=block(source, to, rows),
                dst_ref=block(target, me, rows),
                send_sem=send_sem,
                recv_sem=recv_sem,
                device_id=(to,),
                device_id_type=MESH,
            ).start()

    exchange(others(2, False), inner_out, inner_in, INNER_ROWS, inner_send, inner_recv)
    own_inner = pltpu.make_async_copy(
        block(inner_out, me, INNER_ROWS), block(inner_in, me, INNER_ROWS), own_sem.at[0]
    )
    own_inner.start()

    for face_id in range(4):
        pair = face_id // 2
        at = (face_id % 2) * 24
        inside = [trace[pair, at + 8 * field : at + 8 * field + 8, :] for field in range(3)]
        flux_in, wave_in = face_flux(inside, face_id)
        for i, values in enumerate(flux_in + [wave_in]):
            own_flux[face_id, 8 * i : 8 * i + 8, :] = values
        partner = partners[face_id : face_id + 1]
        local = jnp.bitwise_and(partner, ELEMS - 1)
        piece = lax.shift_right_arithmetic(local, 7)
        lane = jnp.bitwise_and(local, LANES - 1)
        at = (opposite[face_id] % 2) * 24
        for t in range(ELEMS // LANES):
            cols = slice(t * LANES, (t + 1) * LANES)
            index = jnp.broadcast_to(lane[:, cols], (8, LANES))
            piece_t = jnp.broadcast_to(piece[:, cols], (8, LANES))
            for field in range(3):
                rows = slice(at + field * 8, at + field * 8 + 8)
                found = None
                for c in range(ELEMS // LANES):
                    values = trace[pair, rows, c * LANES : (c + 1) * LANES]
                    got = jnp.take_along_axis(values, index, axis=1, mode="promise_in_bounds")
                    found = got if c == 0 else jnp.where(piece_t == c, got, found)
                across[face_id, 8 * field : 8 * field + 8, cols] = found

    for copy in halos:
        copy.wait()

    lift_scale = (time_step * lift_weight * 0.5) * metric[...]
    from_below = jnp.bitwise_and(lax.broadcasted_iota(jnp.int32, (32, LANES), 1), CROSS) != 0
    named = (partners + NAME_BASE).astype(f32)
    lifted = [[None] * 4 for _ in range(3)]
    zeros = jnp.zeros((2 * CROSS, ELEMS), bf16)
    for pair in (0, 1):
        merged = jnp.where(from_below, ghost[pair, 0], ghost[pair, 1])
        names = jnp.transpose(merged[24:32])[:, 0:1]
        chosen = []
        for position in (0, 1):
            face_id = 2 * pair + position
            start = 2 * CROSS * (1 - position)
            match = names[start : start + 2 * CROSS] == named[face_id : face_id + 1]
            match = jnp.where(match, 1.0, 0.0).astype(bf16)
            chosen.append(jnp.concatenate([zeros, match] if start else [match, zeros], axis=0))
        got = jnp.dot(
            jnp.concatenate(split2(merged), axis=0),
            jnp.concatenate(chosen, axis=1),
            preferred_element_type=f32,
        )
        got = got[:32] + got[32:]
        for position in (0, 1):
            face_id = 2 * pair + position
            wall = jnp.logical_not(real[face_id : face_id + 1])
            local = homes[face_id : face_id + 1] == me
            at = position * 24
            inside = [trace[pair, at + 8 * field : at + 8 * field + 8, :] for field in range(3)]
            reflected = mirror(inside, face_id)
            outside = []
            for field in range(3):
                rows = slice(8 * field, 8 * field + 8)
                there = got[rows, ELEMS * position : ELEMS * position + ELEMS]
                there = jnp.where(local, across[face_id, rows, :], there)
                outside.append(jnp.where(wall, reflected[field], there))
            flux_out, wave_out = face_flux(outside, face_id)
            largest = jnp.maximum(own_flux[face_id, 24:32, :], wave_out)
            for field in range(3):
                jump = own_flux[face_id, 8 * field : 8 * field + 8, :] - flux_out[field]
                lifted[field][face_id] = lift_scale * (
                    jump + largest * (outside[field] - inside[field])
                )
    outer = [
        stepped[field][MAIN : MAIN + OUTER] + jnp.concatenate(lifted[field], axis=0)
        for field in range(3)
    ]
    slots = place(jnp.concatenate(outer + [jnp.zeros((LANES - 96, ELEMS), f32)], axis=0))
    for r in range(4):
        pair_of = jnp.where(lane_at < 64, slots[r], pltpu.roll(slots[r + 4], 64, 1))
        outer_out[pl.ds(r, DEVICES, stride=8), :] = pair_of
    for q in range(2):
        row = pltpu.roll(slots[4 * q], 64, 1)
        for k in range(1, 4):
            piece = slots[4 * q + k] if k == 2 else pltpu.roll(slots[4 * q + k], (32 * k - 64) % 128, 1)
            row = jnp.where(lane_at >= 32 * k, piece, row)
        outer_out[pl.ds(4 + q, DEVICES, stride=8), :] = row

    exchange(others(1, True), outer_out, outer_in, OUTER_ROWS, outer_send, outer_recv)
    own_outer = pltpu.make_async_copy(
        block(outer_out, me, OUTER_ROWS), block(outer_in, me, OUTER_ROWS), own_sem.at[1]
    )
    own_outer.start()

    def wait_all(source, target, rows, send_sem, recv_sem):
        every = pl.ds(0, (DEVICES - 1) * rows)
        copies = pltpu.make_async_remote_copy(
            src_ref=source.at[every],
            dst_ref=target.at[every],
            send_sem=send_sem,
            recv_sem=recv_sem,
            device_id=(me,),
            device_id_type=MESH,
        )
        copies.wait_send()
        copies.wait_recv()

    tables_load = pltpu.make_async_copy(tables_in, tables_out, own_sem.at[3])
    tables_load.start()
    own_inner.wait()
    wait_all(inner_out, inner_in, INNER_ROWS, inner_send, inner_recv)
    last = None
    for r in range(INNER_ROWS):
        tail = pltpu.roll(inner_in[pl.ds(r, DEVICES, stride=8), :], 16 * r + 16, 1)
        last = tail if r == 0 else jnp.where(lane_at >= 16 * r, tail, last)
    inner_in[pl.ds(7, DEVICES, stride=8), :] = last
    inner_turned[...] = jnp.transpose(inner_in[...])[:INNER]
    turned = pltpu.make_async_copy(inner_turned, inner_turned_out, own_sem.at[2])
    turned.start()
    own_outer.wait()
    turned.wait()
    tables_load.wait()
    wait_all(outer_out, outer_in, OUTER_ROWS, outer_send, outer_recv)


def child_kernel(inner, outer, tables, out_hbm, flat, out, store_sem):
    parts = 2
    devices, slots = DEVICES // parts, DEVICES * SLOTS // parts
    lane_at = lax.broadcasted_iota(jnp.int32, (devices, LANES), 1)

    def unpack(part):
        first = part * slots
        for j in range(SLOTS):
            body = outer[pl.ds(first + j % 4, devices, stride=8), :]
            rest = outer[pl.ds(first + 4 + j // 4, devices, stride=8), :]
            body = pltpu.roll(body, 64, 1) if j >= 4 else body
            rest = rest if j % 4 == 2 else pltpu.roll(rest, (64 - 32 * (j % 4)) % 128, 1)
            flat[pl.ds(first + j, devices, stride=8), :] = jnp.where(lane_at < 64, body, rest)
        return jnp.transpose(flat[first : first + slots, :])

    stores = []
    ahead = unpack(0)
    for part in range(parts):
        columns = slice(part * slots, part * slots + slots)
        faces = ahead
        refined = inner[3 * MAIN + FLAG : 3 * MAIN + FLAG + 1, columns] > 0.5
        for field in range(3):
            own = slice(MAIN * field, MAIN * field + MAIN)
            start = 3 * MAIN + 8 * (field // 2)
            values = jnp.concatenate(
                [
                    inner[own, columns],
                    faces[own],
                    inner[start : start + 8, columns],
                    jnp.zeros((8, slots), f32),
                ],
                axis=0,
            )
            high, low = split2(values)
            operand = jnp.concatenate([high, low, high, jnp.zeros((16, slots), bf16)], axis=0)
            nodes = jnp.dot(tables[field % 2], operand, preferred_element_type=f32)
            if field == 0 and part + 1 < parts:
                ahead = unpack(part + 1)
            for c in range(4):
                start = 192 * c + 64 * field
                other = nodes[256:320] if c == 0 else 0.0
                out[start : start + 64, columns] = jnp.where(
                    refined, nodes[64 * c : 64 * c + 64], other
                )
                box = (pl.ds(start, 64), pl.ds(part * slots, slots))
                store = pltpu.make_async_copy(
                    out.at[box], out_hbm.at[box], store_sem.at[12 * part + 4 * field + c]
                )
                store.start()
                stores.append(store)
    for store in stores:
        store.wait()


def on_device(state, neighbours, metric, flags, new_owner):
    hbm = pl.BlockSpec(memory_space=pl.ANY)
    slots = DEVICES * SLOTS
    buffer = pltpu.VMEM((slots, LANES), f32)
    dma = pltpu.SemaphoreType.DMA
    inner, outer, tables = pl.pallas_call(
        step_kernel,
        out_shape=(
            jax.ShapeDtypeStruct((INNER, slots), f32),
            jax.ShapeDtypeStruct((slots, LANES), f32),
            jax.ShapeDtypeStruct((2, 320, 256), bf16),
        ),
        in_specs=[pl.BlockSpec(memory_space=pltpu.HBM)] * 7,
        out_specs=(hbm, hbm, hbm),
        scratch_shapes=[
            pltpu.VMEM((192, ELEMS), f32),
            pltpu.VMEM((4, ELEMS), jnp.int32),
            pltpu.VMEM((1, ELEMS), f32),
            pltpu.VMEM((1, ELEMS), jnp.int32),
            pltpu.VMEM((1, ELEMS), jnp.int32),
            pltpu.VMEM((240, 512), bf16),
            pltpu.VMEM((192 * ELEMS // LANES, LANES), f32),
            pltpu.VMEM((2, 48, ELEMS), f32),
            pltpu.VMEM((4, 32, ELEMS), f32),
            pltpu.VMEM((4, 24, ELEMS), f32),
            pltpu.VMEM((2, 32, LANES), f32),
            pltpu.VMEM((2, 2, 32, LANES), f32),
            buffer,
            buffer,
            buffer,
            pltpu.VMEM((INNER, slots), f32),
            pltpu.VMEM((slots, ELEMS), bf16),
            dma((6,)),
            dma((2, 2)),
            dma((2, 2)),
            dma,
            dma,
            dma,
            dma,
            dma((4,)),
        ],
        compiler_params=pltpu.CompilerParams(collective_id=0, has_side_effects=True, vmem_limit_bytes=16 << 20),
        name="step_and_migrate",
    )(
        *(
            pltpu.with_memory_space_constraint(x, pltpu.HBM)
            for x in (
                state.reshape(192, ELEMS),
                neighbours,
                metric.reshape(1, ELEMS),
                flags.reshape(1, ELEMS),
                new_owner.reshape(1, ELEMS),
                jnp.asarray(step_table(), bf16),
                jnp.asarray(child_tables(), bf16),
            )
        )
    )
    children = pl.pallas_call(
        child_kernel,
        out_shape=jax.ShapeDtypeStruct((768, slots), f32),
        in_specs=[pl.BlockSpec(memory_space=pltpu.VMEM)] * 3,
        out_specs=pl.BlockSpec(memory_space=pltpu.HBM),
        scratch_shapes=[
            buffer,
            pltpu.VMEM((768, slots), f32),
            dma((24,)),
        ],
        compiler_params=pltpu.CompilerParams(vmem_limit_bytes=16 << 20),
        name="make_children",
    )(inner, outer, tables)
    return children.reshape(4, 3, 64, slots)


def solution(mesh):
    placed = (P(None, None, "curve"), P(None, "curve"), P("curve"), P("curve"), P("curve", None))
    return jax.shard_map(
        on_device,
        mesh=mesh,
        in_specs=placed,
        out_specs=P(None, None, None, "curve"),
        check_vma=False,
    )
```

```python
import random

import jax
import jax.numpy as jnp
import numpy as np
from jax import lax
from jax.experimental import pallas as pl
from jax.experimental.pallas import tpu as pltpu
from jax.sharding import PartitionSpec as P

lgl_nodes = np.array(
    [
        -1.0,
        -0.8717401485096066,
        -0.5917001814331423,
        -0.2092992179024789,
        0.2092992179024789,
        0.5917001814331423,
        0.8717401485096066,
        1.0,
    ]
)
lift_weight = 28.0
earth_pressure = 1.2
friction = 0.4
slope_x = 0.3
slope_y = 0.1
time_step = 0.01
face_nodes = np.array(
    [
        [8 * r for r in range(8)],
        [8 * r + 7 for r in range(8)],
        [r for r in range(8)],
        [56 + r for r in range(8)],
    ]
)
inner_nodes = np.array([8 * iy + ix for iy in range(1, 7) for ix in range(1, 7)])
opposite = [1, 0, 3, 2]
outward = [-1.0, 1.0, -1.0, 1.0]

DEVICES = 128
ELEMS = 512
SLOTS = 8
LANES = 128
MAIN = 32
OUTER = 32
EXTRA = 16
INNER = 3 * MAIN + EXTRA
FLAG = 12
INNER_ROWS = 7
OUTER_ROWS = 6
CROSS = 32
NAME_BASE = 2
MESH = pl.DeviceIdType.MESH
bf16 = jnp.bfloat16
f32 = jnp.float32


def lagrange_table(points):
    values_table = np.ones((len(points), 8))
    for j in range(8):
        for m in range(8):
            if m != j:
                values_table[:, j] = (
                    values_table[:, j] * (points - lgl_nodes[m]) / (lgl_nodes[j] - lgl_nodes[m])
                )
    return values_table


def basis_tables():
    bary = np.array(
        [1.0 / np.prod([lgl_nodes[j] - lgl_nodes[m] for m in range(8) if m != j]) for j in range(8)]
    )
    derivative = np.zeros((8, 8))
    for i in range(8):
        for j in range(8):
            if i != j:
                derivative[i, j] = bary[j] / bary[i] / (lgl_nodes[i] - lgl_nodes[j])
        derivative[i, i] = -np.sum(derivative[i])
    identity = np.eye(8)
    lower_half = lagrange_table((lgl_nodes - 1.0) / 2.0)
    upper_half = lagrange_table((lgl_nodes + 1.0) / 2.0)
    halves = [lower_half, upper_half]
    prolong = np.stack(
        [
            np.kron(halves[row_half], halves[col_half])
            for row_half in range(2)
            for col_half in range(2)
        ]
    )
    return np.kron(identity, derivative), np.kron(derivative, identity), prolong


def two_parts(table):
    high = np.asarray(table, np.float32).astype(bf16)
    low = (np.asarray(table, np.float64) - high.astype(np.float64)).astype(bf16)
    return high, low


def corner_copy(face_id, r):
    return face_id < 2 and r in (0, 7)


def step_table():
    deriv_x, deriv_y, _ = basis_tables()
    full = np.concatenate([np.eye(64), deriv_x, deriv_y], axis=1)
    table = np.zeros((3, MAIN + OUTER + EXTRA, 192))
    for field in range(3):
        table[field, :MAIN] = full[inner_nodes[:MAIN]]
        for face_id in range(4):
            for r in range(8):
                if not corner_copy(face_id, r):
                    table[field, MAIN + 8 * face_id + r] = full[face_nodes[face_id][r]]
        start = MAIN + OUTER + 4 * field
        table[field, start : start + 4] = full[inner_nodes[MAIN:]]
    high, low = two_parts(table.reshape(-1, 192))
    return np.concatenate([high, high, low[:, 64:]], axis=1)


def child_tables():
    _, _, prolong = basis_tables()
    rows = np.concatenate([prolong.reshape(256, 64), np.eye(64)], axis=0)
    tables = []
    for shift in (0, 4):
        table = np.zeros((320, 80))
        table[:, :MAIN] = rows[:, inner_nodes[:MAIN]]
        for face_id in range(4):
            for r in range(8):
                table[:, MAIN + 8 * face_id + r] = rows[:, face_nodes[face_id][r]]
        start = MAIN + OUTER + shift
        table[:, start : start + 4] = rows[:, inner_nodes[MAIN:]]
        high, low = two_parts(table)
        tables.append(np.concatenate([high, high, low, np.zeros((320, 16), bf16)], axis=1))
    return np.stack(tables)


def distances(seed, far_first):
    order = [
        (z, y, x, c) for z in range(4) for y in range(4) for x in range(4) for c in range(2)
    ][1:]
    random.Random(seed).shuffle(order)
    if far_first:
        order.sort(key=lambda d: -sum(min(v, 4 - v) for v in d[:3]))
    return order


def split2(values):
    high = values.astype(bf16)
    return high, (values - high.astype(f32)).astype(bf16)


def face_flux(values, face_id):
    depth, moment_x, moment_y = values
    inv = 1.0 / depth
    pressure = 0.5 * earth_pressure * depth * depth
    sign = outward[face_id]
    if face_id < 2:
        normal = moment_x * inv
        terms = [moment_x, moment_x * normal + pressure, moment_y * normal]
    else:
        normal = moment_y * inv
        terms = [moment_y, moment_x * normal, moment_y * normal + pressure]
    return [sign * t for t in terms], jnp.abs(normal) + jnp.sqrt(earth_pressure * depth)


def mirror(values, face_id):
    if face_id < 2:
        return [values[0], -values[1], values[2]]
    return [values[0], values[1], -values[2]]


def step_kernel(
    state_in, neighbours_in, metric_in, flags_in, owner_in, table_in, tables_in,
    inner_turned_out, outer_in, tables_out,
    state, neighbours, metric, flags, owner, table,
    tiles, trace, own_flux, across, crossing, ghost,
    inner_out, outer_out, inner_in, inner_turned, onehot,
    load_sem, halo_send, halo_recv, inner_send, inner_recv, outer_send, outer_recv, own_sem,
):
    pairs = (
        (state_in, state), (neighbours_in, neighbours), (metric_in, metric),
        (flags_in, flags), (owner_in, owner), (table_in, table),
    )
    loads = [pltpu.make_async_copy(a, b, load_sem.at[i]) for i, (a, b) in enumerate(pairs)]
    for load in loads:
        load.start()

    me = lax.axis_index("curve")
    z_part = [lax.rem(me // 32 + z, 4) * 32 for z in range(4)]
    y_part = [lax.rem((me // 8) % 4 + y, 4) * 8 for y in range(4)]
    x_part = [lax.rem((me // 2) % 4 + x, 4) * 2 for x in range(4)]
    c_part = [lax.rem(me % 2 + c, 2) for c in range(2)]
    zy_part = [[z + y for y in y_part] for z in z_part]
    xc_part = [[x + c for c in c_part] for x in x_part]

    def others(seed, far_first):
        return [zy_part[z][y] + xc_part[x][c] for z, y, x, c in distances(seed, far_first)]

    barrier = pltpu.get_barrier_semaphore()
    for to in others(0, True):
        pl.semaphore_signal(barrier, inc=1, device_id=(to,), device_id_type=MESH)
    for load in loads:
        load.wait()

    partners = neighbours[...]
    distance = jnp.where(lax.broadcasted_iota(jnp.int32, (4, ELEMS), 0) < 2, 1, 32)
    homes = lax.shift_right_arithmetic(partners, 9)
    real = partners >= 0
    below = jnp.where(real & (homes == me - distance), 1.0, 0.0)
    above = jnp.where(real & (homes == me + distance), 1.0, 0.0)
    owners = owner[...]
    hits = owners == lax.broadcasted_iota(jnp.int32, (DEVICES, ELEMS), 0)
    hits = jnp.where(hits, 1.0, 0.0)
    nothing = jnp.zeros((4, ELEMS), f32)
    marks = jnp.concatenate([hits, below, nothing, above, nothing], axis=0).astype(bf16)
    at_row = lax.broadcasted_iota(jnp.int32, (LANES, 2 * LANES), 0)
    at_lane = lax.broadcasted_iota(jnp.int32, (LANES, 2 * LANES), 1)
    earlier = jnp.where((at_row < at_lane) | (at_lane >= LANES), 1.0, 0.0).astype(bf16)
    before, total = [], None
    for t in range(ELEMS // LANES):
        count = jnp.dot(
            marks[:, LANES * t : LANES * t + LANES], earlier, preferred_element_type=f32
        )
        before.append(count[:, :LANES] if t == 0 else count[:, :LANES] + total)
        total = count[:, LANES:] if t == 0 else count[:, LANES:] + total
    before = jnp.concatenate(before, axis=1)
    rank = jnp.sum(hits * before[:DEVICES], axis=0, keepdims=True)
    column = rank.astype(jnp.int32) * DEVICES + owners
    slot_rows = lax.broadcasted_iota(jnp.int32, (DEVICES * SLOTS, ELEMS), 0)
    onehot[...] = jnp.where(slot_rows == column, 1.0, 0.0).astype(bf16)
    spot = jnp.where(
        below > 0.5,
        before[DEVICES : DEVICES + 4],
        jnp.where(above > 0.5, before[DEVICES + 8 : DEVICES + 12] + CROSS, -1000.0),
    ).astype(jnp.int32)

    for t in range(ELEMS // LANES):
        tiles[192 * t : 192 * t + 192, :] = state[:, LANES * t : LANES * t + LANES]
    for face_id in range(4):
        for field in range(3):
            at = (face_id % 2) * 24 + field * 8
            if face_id < 2:
                for t in range(ELEMS // LANES):
                    start = 192 * t + 64 * field + 7 * face_id
                    trace[0, at : at + 8, LANES * t : LANES * t + LANES] = tiles[
                        pl.ds(start, 8, stride=8), :
                    ]
            else:
                start = 64 * field + 56 * (face_id - 2)
                trace[1, at : at + 8, :] = state[start : start + 8, :]

    first_row = lax.broadcasted_iota(jnp.int32, (8, ELEMS), 0) == 0
    name = (
        lax.broadcasted_iota(jnp.int32, (8, ELEMS), 1) + (me * ELEMS + NAME_BASE)
    ).astype(f32)
    name = jnp.where(first_row, name, 0.0)
    lane_rows = lax.broadcasted_iota(jnp.int32, (LANES, ELEMS), 0)
    nt_dims = (((1,), (1,)), ((), ()))
    for pair in (0, 1):
        packed = None
        for position in (0, 1):
            face_id = 2 * pair + position
            rows = jnp.concatenate([trace[pair, 24 * position : 24 * position + 24, :], name])
            chosen = lane_rows == spot[face_id : face_id + 1] + 2 * CROSS * position
            part = lax.dot_general(
                jnp.concatenate(split2(rows), axis=0),
                jnp.where(chosen, 1.0, 0.0).astype(bf16),
                nt_dims,
                preferred_element_type=f32,
            )
            packed = part if packed is None else packed + part
        crossing[pair] = packed[:32] + packed[32:]

    scale = (-time_step) * metric[...]
    depth, moment_x, moment_y = (state[64 * f : 64 * f + 64, :] for f in range(3))
    inv = 1.0 / depth
    speed_x, speed_y = moment_x * inv, moment_y * inv
    pressure = 0.5 * earth_pressure * depth * depth
    drag = friction / jnp.sqrt(speed_x * speed_x + speed_y * speed_y + 1.0)
    cross = moment_x * speed_y
    parts = [
        (depth, moment_x, moment_y),
        (
            moment_x + time_step * (depth * (slope_x - drag * speed_x)),
            moment_x * speed_x + pressure,
            cross,
        ),
        (
            moment_y + time_step * (depth * (slope_y - drag * speed_y)),
            cross,
            moment_y * speed_y + pressure,
        ),
    ]
    stepped = []
    for q, flux_x, flux_y in parts:
        q_high, q_low = split2(q)
        x_high, x_low = split2(scale * flux_x)
        y_high, y_low = split2(scale * flux_y)
        operand = jnp.concatenate(
            [q_high, x_high, y_high, q_low, x_low, y_low, x_high, y_high], axis=0
        )
        rows = slice(80 * len(stepped), 80 * len(stepped) + 80)
        stepped.append(jnp.dot(table[rows, :], operand, preferred_element_type=f32))

    def place(rows):
        both = lax.dot_general(
            onehot[...],
            jnp.concatenate(split2(rows), axis=0),
            nt_dims,
            preferred_element_type=f32,
        )
        both = both[:, :LANES] + both[:, LANES:]
        return [both[j * DEVICES : (j + 1) * DEVICES] for j in range(SLOTS)]

    lane_at = lax.broadcasted_iota(jnp.int32, (DEVICES, LANES), 1)
    extra = stepped[0][-EXTRA:] + stepped[1][-EXTRA:] + stepped[2][-EXTRA:]
    flag_row = lax.broadcasted_iota(jnp.int32, (EXTRA, ELEMS), 0) == FLAG
    extra = extra + jnp.where(flag_row, flags[...].astype(f32), 0.0)
    slots = place(
        jnp.concatenate(
            [s[:MAIN] for s in stepped] + [extra, jnp.zeros((LANES - INNER, ELEMS), f32)], axis=0
        )
    )
    for r in range(INNER_ROWS):
        tail = pltpu.roll(slots[7], INNER - 16 * r, 1)
        inner_out[pl.ds(r, DEVICES, stride=8), :] = jnp.where(lane_at < INNER, slots[r], tail)

    pl.semaphore_wait(barrier, DEVICES - 1)

    def halo(pair, upward):
        far = 32 if pair else 1
        target = lax.rem(me + (far if upward else DEVICES - far), DEVICES)
        side = 0 if upward else 1
        return pltpu.make_async_remote_copy(
            src_ref=crossing.at[pair],
            dst_ref=ghost.at[pair, side],
            send_sem=halo_send.at[pair, side],
            recv_sem=halo_recv.at[pair, side],
            device_id=(target,),
            device_id_type=MESH,
        )

    halos = [halo(pair, upward) for pair in (0, 1) for upward in (True, False)]
    for copy in halos:
        copy.start()

    def block(ref, device, rows):
        return ref.at[pl.ds(pl.multiple_of(device * 8, 8), rows)]

    def exchange(order, source, target, rows, send_sem, recv_sem):
        for to in order:
            pltpu.make_async_remote_copy(
                src_ref=block(source, to, rows),
                dst_ref=block(target, me, rows),
                send_sem=send_sem,
                recv_sem=recv_sem,
                device_id=(to,),
                device_id_type=MESH,
            ).start()

    exchange(others(2, False), inner_out, inner_in, INNER_ROWS, inner_send, inner_recv)
    own_inner = pltpu.make_async_copy(
        block(inner_out, me, INNER_ROWS), block(inner_in, me, INNER_ROWS), own_sem.at[0]
    )
    own_inner.start()

    for face_id in range(4):
        pair = face_id // 2
        at = (face_id % 2) * 24
        inside = [trace[pair, at + 8 * field : at + 8 * field + 8, :] for field in range(3)]
        flux_in, wave_in = face_flux(inside, face_id)
        for i, values in enumerate(flux_in + [wave_in]):
            own_flux[face_id, 8 * i : 8 * i + 8, :] = values
        partner = partners[face_id : face_id + 1]
        local = jnp.bitwise_and(partner, ELEMS - 1)
        piece = lax.shift_right_arithmetic(local, 7)
        lane = jnp.bitwise_and(local, LANES - 1)
        at = (opposite[face_id] % 2) * 24
        for t in range(ELEMS // LANES):
            cols = slice(t * LANES, (t + 1) * LANES)
            index = jnp.broadcast_to(lane[:, cols], (8, LANES))
            piece_t = jnp.broadcast_to(piece[:, cols], (8, LANES))
            for field in range(3):
                rows = slice(at + field * 8, at + field * 8 + 8)
                found = None
                for c in range(ELEMS // LANES):
                    values = trace[pair, rows, c * LANES : (c + 1) * LANES]
                    got = jnp.take_along_axis(values, index, axis=1, mode="promise_in_bounds")
                    found = got if c == 0 else jnp.where(piece_t == c, got, found)
                across[face_id, 8 * field : 8 * field + 8, cols] = found

    for copy in halos:
        copy.wait()

    lift_scale = (time_step * lift_weight * 0.5) * metric[...]
    from_below = jnp.bitwise_and(lax.broadcasted_iota(jnp.int32, (32, LANES), 1), CROSS) != 0
    named = (partners + NAME_BASE).astype(f32)
    lifted = [[None] * 4 for _ in range(3)]
    zeros = jnp.zeros((2 * CROSS, ELEMS), bf16)
    for pair in (0, 1):
        merged = jnp.where(from_below, ghost[pair, 0], ghost[pair, 1])
        names = jnp.transpose(merged[24:32])[:, 0:1]
        chosen = []
        for position in (0, 1):
            face_id = 2 * pair + position
            start = 2 * CROSS * (1 - position)
            match = names[start : start + 2 * CROSS] == named[face_id : face_id + 1]
            match = jnp.where(match, 1.0, 0.0).astype(bf16)
            chosen.append(jnp.concatenate([zeros, match] if start else [match, zeros], axis=0))
        got = jnp.dot(
            jnp.concatenate(split2(merged), axis=0),
            jnp.concatenate(chosen, axis=1),
            preferred_element_type=f32,
        )
        got = got[:32] + got[32:]
        for position in (0, 1):
            face_id = 2 * pair + position
            wall = jnp.logical_not(real[face_id : face_id + 1])
            local = homes[face_id : face_id + 1] == me
            at = position * 24
            inside = [trace[pair, at + 8 * field : at + 8 * field + 8, :] for field in range(3)]
            reflected = mirror(inside, face_id)
            outside = []
            for field in range(3):
                rows = slice(8 * field, 8 * field + 8)
                there = got[rows, ELEMS * position : ELEMS * position + ELEMS]
                there = jnp.where(local, across[face_id, rows, :], there)
                outside.append(jnp.where(wall, reflected[field], there))
            flux_out, wave_out = face_flux(outside, face_id)
            largest = jnp.maximum(own_flux[face_id, 24:32, :], wave_out)
            for field in range(3):
                jump = own_flux[face_id, 8 * field : 8 * field + 8, :] - flux_out[field]
                lifted[field][face_id] = lift_scale * (
                    jump + largest * (outside[field] - inside[field])
                )
    outer = [
        stepped[field][MAIN : MAIN + OUTER] + jnp.concatenate(lifted[field], axis=0)
        for field in range(3)
    ]
    slots = place(jnp.concatenate(outer + [jnp.zeros((LANES - 96, ELEMS), f32)], axis=0))
    for r in range(4):
        pair_of = jnp.where(lane_at < 64, slots[r], pltpu.roll(slots[r + 4], 64, 1))
        outer_out[pl.ds(r, DEVICES, stride=8), :] = pair_of
    for q in range(2):
        row = pltpu.roll(slots[4 * q], 64, 1)
        for k in range(1, 4):
            piece = slots[4 * q + k] if k == 2 else pltpu.roll(slots[4 * q + k], (32 * k - 64) % 128, 1)
            row = jnp.where(lane_at >= 32 * k, piece, row)
        outer_out[pl.ds(4 + q, DEVICES, stride=8), :] = row

    exchange(others(1, True), outer_out, outer_in, OUTER_ROWS, outer_send, outer_recv)
    own_outer = pltpu.make_async_copy(
        block(outer_out, me, OUTER_ROWS), block(outer_in, me, OUTER_ROWS), own_sem.at[1]
    )
    own_outer.start()

    def wait_all(source, target, rows, send_sem, recv_sem):
        every = pl.ds(0, (DEVICES - 1) * rows)
        copies = pltpu.make_async_remote_copy(
            src_ref=source.at[every],
            dst_ref=target.at[every],
            send_sem=send_sem,
            recv_sem=recv_sem,
            device_id=(me,),
            device_id_type=MESH,
        )
        copies.wait_send()
        copies.wait_recv()

    tables_load = pltpu.make_async_copy(tables_in, tables_out, own_sem.at[3])
    tables_load.start()
    own_inner.wait()
    wait_all(inner_out, inner_in, INNER_ROWS, inner_send, inner_recv)
    last = None
    for r in range(INNER_ROWS):
        tail = pltpu.roll(inner_in[pl.ds(r, DEVICES, stride=8), :], 16 * r + 16, 1)
        last = tail if r == 0 else jnp.where(lane_at >= 16 * r, tail, last)
    inner_in[pl.ds(7, DEVICES, stride=8), :] = last
    inner_turned[...] = jnp.transpose(inner_in[...])[:INNER]
    turned = pltpu.make_async_copy(inner_turned, inner_turned_out, own_sem.at[2])
    turned.start()
    own_outer.wait()
    turned.wait()
    tables_load.wait()
    wait_all(outer_out, outer_in, OUTER_ROWS, outer_send, outer_recv)


def child_kernel(inner, outer, tables, out_hbm, flat, out, store_sem):
    cuts = (0, 256, DEVICES * SLOTS)

    def unpack(part):
        first, slots = cuts[part], cuts[part + 1] - cuts[part]
        devices = slots // SLOTS
        lane_at = lax.broadcasted_iota(jnp.int32, (devices, LANES), 1)
        for j in range(SLOTS):
            body = outer[pl.ds(first + j % 4, devices, stride=8), :]
            rest = outer[pl.ds(first + 4 + j // 4, devices, stride=8), :]
            body = pltpu.roll(body, 64, 1) if j >= 4 else body
            rest = rest if j % 4 == 2 else pltpu.roll(rest, (64 - 32 * (j % 4)) % 128, 1)
            flat[pl.ds(first + j, devices, stride=8), :] = jnp.where(lane_at < 64, body, rest)
        return jnp.transpose(flat[first : first + slots, :])

    stores = []
    ahead = unpack(0)
    for part in range(2):
        slots = cuts[part + 1] - cuts[part]
        columns = slice(cuts[part], cuts[part + 1])
        faces = ahead
        refined = inner[3 * MAIN + FLAG : 3 * MAIN + FLAG + 1, columns] > 0.5
        for field in range(3):
            own = slice(MAIN * field, MAIN * field + MAIN)
            start = 3 * MAIN + 8 * (field // 2)
            values = jnp.concatenate(
                [
                    inner[own, columns],
                    faces[own],
                    inner[start : start + 8, columns],
                    jnp.zeros((8, slots), f32),
                ],
                axis=0,
            )
            high, low = split2(values)
            operand = jnp.concatenate([high, low, high, jnp.zeros((16, slots), bf16)], axis=0)
            nodes = jnp.dot(tables[field % 2], operand, preferred_element_type=f32)
            if field == 0 and part == 0:
                ahead = unpack(part + 1)
            for c in range(4):
                start = 192 * c + 64 * field
                other = nodes[256:320] if c == 0 else 0.0
                out[start : start + 64, columns] = jnp.where(
                    refined, nodes[64 * c : 64 * c + 64], other
                )
                box = (pl.ds(start, 64), pl.ds(cuts[part], slots))
                store = pltpu.make_async_copy(
                    out.at[box], out_hbm.at[box], store_sem.at[12 * part + 4 * field + c]
                )
                store.start()
                stores.append(store)
    for store in stores:
        store.wait()


def on_device(state, neighbours, metric, flags, new_owner):
    hbm = pl.BlockSpec(memory_space=pl.ANY)
    slots = DEVICES * SLOTS
    buffer = pltpu.VMEM((slots, LANES), f32)
    dma = pltpu.SemaphoreType.DMA
    inner, outer, tables = pl.pallas_call(
        step_kernel,
        out_shape=(
            jax.ShapeDtypeStruct((INNER, slots), f32),
            jax.ShapeDtypeStruct((slots, LANES), f32),
            jax.ShapeDtypeStruct((2, 320, 256), bf16),
        ),
        in_specs=[pl.BlockSpec(memory_space=pltpu.HBM)] * 7,
        out_specs=(hbm, hbm, hbm),
        scratch_shapes=[
            pltpu.VMEM((192, ELEMS), f32),
            pltpu.VMEM((4, ELEMS), jnp.int32),
            pltpu.VMEM((1, ELEMS), f32),
            pltpu.VMEM((1, ELEMS), jnp.int32),
            pltpu.VMEM((1, ELEMS), jnp.int32),
            pltpu.VMEM((240, 512), bf16),
            pltpu.VMEM((192 * ELEMS // LANES, LANES), f32),
            pltpu.VMEM((2, 48, ELEMS), f32),
            pltpu.VMEM((4, 32, ELEMS), f32),
            pltpu.VMEM((4, 24, ELEMS), f32),
            pltpu.VMEM((2, 32, LANES), f32),
            pltpu.VMEM((2, 2, 32, LANES), f32),
            buffer,
            buffer,
            buffer,
            pltpu.VMEM((INNER, slots), f32),
            pltpu.VMEM((slots, ELEMS), bf16),
            dma((6,)),
            dma((2, 2)),
            dma((2, 2)),
            dma,
            dma,
            dma,
            dma,
            dma((4,)),
        ],
        compiler_params=pltpu.CompilerParams(collective_id=0, has_side_effects=True, vmem_limit_bytes=16 << 20),
        name="step_and_migrate",
    )(
        *(
            pltpu.with_memory_space_constraint(x, pltpu.HBM)
            for x in (
                state.reshape(192, ELEMS),
                neighbours,
                metric.reshape(1, ELEMS),
                flags.reshape(1, ELEMS),
                new_owner.reshape(1, ELEMS),
                jnp.asarray(step_table(), bf16),
                jnp.asarray(child_tables(), bf16),
            )
        )
    )
    children = pl.pallas_call(
        child_kernel,
        out_shape=jax.ShapeDtypeStruct((768, slots), f32),
        in_specs=[pl.BlockSpec(memory_space=pltpu.VMEM)] * 3,
        out_specs=pl.BlockSpec(memory_space=pltpu.HBM),
        scratch_shapes=[
            buffer,
            pltpu.VMEM((768, slots), f32),
            dma((24,)),
        ],
        compiler_params=pltpu.CompilerParams(vmem_limit_bytes=16 << 20),
        name="make_children",
    )(inner, outer, tables)
    return children.reshape(4, 3, 64, slots)


def solution(mesh):
    placed = (P(None, None, "curve"), P(None, "curve"), P("curve"), P("curve"), P("curve", None))
    return jax.shard_map(
        on_device,
        mesh=mesh,
        in_specs=placed,
        out_specs=P(None, None, None, "curve"),
        check_vma=False,
    )
```

```python
import random

import jax
import jax.numpy as jnp
import numpy as np
from jax import lax
from jax.experimental import pallas as pl
from jax.experimental.pallas import tpu as pltpu
from jax.sharding import PartitionSpec as P

lgl_nodes = np.array(
    [
        -1.0,
        -0.8717401485096066,
        -0.5917001814331423,
        -0.2092992179024789,
        0.2092992179024789,
        0.5917001814331423,
        0.8717401485096066,
        1.0,
    ]
)
lift_weight = 28.0
earth_pressure = 1.2
friction = 0.4
slope_x = 0.3
slope_y = 0.1
time_step = 0.01
face_nodes = np.array(
    [
        [8 * r for r in range(8)],
        [8 * r + 7 for r in range(8)],
        [r for r in range(8)],
        [56 + r for r in range(8)],
    ]
)
inner_nodes = np.array([8 * iy + ix for iy in range(1, 7) for ix in range(1, 7)])
opposite = [1, 0, 3, 2]
outward = [-1.0, 1.0, -1.0, 1.0]

DEVICES = 128
ELEMS = 512
SLOTS = 8
LANES = 128
MAIN = 32
OUTER = 32
EXTRA = 16
INNER = 3 * MAIN + EXTRA
FLAG = 12
INNER_ROWS = 7
OUTER_ROWS = 6
CROSS = 32
NAME_BASE = 2
MESH = pl.DeviceIdType.MESH
bf16 = jnp.bfloat16
f32 = jnp.float32


def lagrange_table(points):
    values_table = np.ones((len(points), 8))
    for j in range(8):
        for m in range(8):
            if m != j:
                values_table[:, j] = (
                    values_table[:, j] * (points - lgl_nodes[m]) / (lgl_nodes[j] - lgl_nodes[m])
                )
    return values_table


def basis_tables():
    bary = np.array(
        [1.0 / np.prod([lgl_nodes[j] - lgl_nodes[m] for m in range(8) if m != j]) for j in range(8)]
    )
    derivative = np.zeros((8, 8))
    for i in range(8):
        for j in range(8):
            if i != j:
                derivative[i, j] = bary[j] / bary[i] / (lgl_nodes[i] - lgl_nodes[j])
        derivative[i, i] = -np.sum(derivative[i])
    identity = np.eye(8)
    lower_half = lagrange_table((lgl_nodes - 1.0) / 2.0)
    upper_half = lagrange_table((lgl_nodes + 1.0) / 2.0)
    halves = [lower_half, upper_half]
    prolong = np.stack(
        [
            np.kron(halves[row_half], halves[col_half])
            for row_half in range(2)
            for col_half in range(2)
        ]
    )
    return np.kron(identity, derivative), np.kron(derivative, identity), prolong


def two_parts(table):
    high = np.asarray(table, np.float32).astype(bf16)
    low = (np.asarray(table, np.float64) - high.astype(np.float64)).astype(bf16)
    return high, low


def corner_copy(face_id, r):
    return face_id < 2 and r in (0, 7)


def step_table():
    deriv_x, deriv_y, _ = basis_tables()
    full = np.concatenate([np.eye(64), deriv_x, deriv_y], axis=1)
    table = np.zeros((3, MAIN + OUTER + EXTRA, 192))
    for field in range(3):
        table[field, :MAIN] = full[inner_nodes[:MAIN]]
        for face_id in range(4):
            for r in range(8):
                if not corner_copy(face_id, r):
                    table[field, MAIN + 8 * face_id + r] = full[face_nodes[face_id][r]]
        start = MAIN + OUTER + 4 * field
        table[field, start : start + 4] = full[inner_nodes[MAIN:]]
    high, low = two_parts(table.reshape(-1, 192))
    return np.concatenate([high, high, low[:, 64:]], axis=1)


def child_tables():
    _, _, prolong = basis_tables()
    rows = np.concatenate([prolong.reshape(256, 64), np.eye(64)], axis=0)
    tables = []
    for shift in (0, 4):
        table = np.zeros((320, 80))
        table[:, :MAIN] = rows[:, inner_nodes[:MAIN]]
        for face_id in range(4):
            for r in range(8):
                table[:, MAIN + 8 * face_id + r] = rows[:, face_nodes[face_id][r]]
        start = MAIN + OUTER + shift
        table[:, start : start + 4] = rows[:, inner_nodes[MAIN:]]
        high, low = two_parts(table)
        tables.append(np.concatenate([high, high, low, np.zeros((320, 16), bf16)], axis=1))
    return np.stack(tables)


def distances(seed, far_first):
    order = [
        (z, y, x, c) for z in range(4) for y in range(4) for x in range(4) for c in range(2)
    ][1:]
    random.Random(seed).shuffle(order)
    if far_first:
        order.sort(key=lambda d: -sum(min(v, 4 - v) for v in d[:3]))
    return order


def split2(values):
    high = values.astype(bf16)
    return high, (values - high.astype(f32)).astype(bf16)


def face_flux(values, face_id):
    depth, moment_x, moment_y = values
    inv = 1.0 / depth
    pressure = 0.5 * earth_pressure * depth * depth
    sign = outward[face_id]
    if face_id < 2:
        normal = moment_x * inv
        terms = [moment_x, moment_x * normal + pressure, moment_y * normal]
    else:
        normal = moment_y * inv
        terms = [moment_y, moment_x * normal, moment_y * normal + pressure]
    return [sign * t for t in terms], jnp.abs(normal) + jnp.sqrt(earth_pressure * depth)


def mirror(values, face_id):
    if face_id < 2:
        return [values[0], -values[1], values[2]]
    return [values[0], values[1], -values[2]]


def step_kernel(
    state_in, neighbours_in, metric_in, flags_in, owner_in, table_in, tables_in,
    inner_turned_out, outer_in, tables_out,
    state, neighbours, metric, flags, owner, table,
    tiles, trace, own_flux, across, crossing, ghost,
    inner_out, outer_out, inner_in, inner_turned, onehot,
    load_sem, halo_send, halo_recv, inner_send, inner_recv, outer_send, outer_recv, own_sem,
):
    pairs = (
        (state_in, state), (neighbours_in, neighbours), (metric_in, metric),
        (flags_in, flags), (owner_in, owner), (table_in, table),
    )
    loads = [pltpu.make_async_copy(a, b, load_sem.at[i]) for i, (a, b) in enumerate(pairs)]
    for load in loads:
        load.start()

    me = lax.axis_index("curve")
    z_part = [lax.rem(me // 32 + z, 4) * 32 for z in range(4)]
    y_part = [lax.rem((me // 8) % 4 + y, 4) * 8 for y in range(4)]
    x_part = [lax.rem((me // 2) % 4 + x, 4) * 2 for x in range(4)]
    c_part = [lax.rem(me % 2 + c, 2) for c in range(2)]
    zy_part = [[z + y for y in y_part] for z in z_part]
    xc_part = [[x + c for c in c_part] for x in x_part]

    def others(seed, far_first):
        return [zy_part[z][y] + xc_part[x][c] for z, y, x, c in distances(seed, far_first)]

    barrier = pltpu.get_barrier_semaphore()
    for to in others(0, True):
        pl.semaphore_signal(barrier, inc=1, device_id=(to,), device_id_type=MESH)
    for load in loads:
        load.wait()

    partners = neighbours[...]
    distance = jnp.where(lax.broadcasted_iota(jnp.int32, (4, ELEMS), 0) < 2, 1, 32)
    homes = lax.shift_right_arithmetic(partners, 9)
    real = partners >= 0
    below = jnp.where(real & (homes == me - distance), 1.0, 0.0)
    above = jnp.where(real & (homes == me + distance), 1.0, 0.0)
    owners = owner[...]
    hits = owners == lax.broadcasted_iota(jnp.int32, (DEVICES, ELEMS), 0)
    hits = jnp.where(hits, 1.0, 0.0)
    nothing = jnp.zeros((4, ELEMS), f32)
    marks = jnp.concatenate([hits, below, nothing, above, nothing], axis=0).astype(bf16)
    at_row = lax.broadcasted_iota(jnp.int32, (LANES, 2 * LANES), 0)
    at_lane = lax.broadcasted_iota(jnp.int32, (LANES, 2 * LANES), 1)
    earlier = jnp.where((at_row < at_lane) | (at_lane >= LANES), 1.0, 0.0).astype(bf16)
    before, total = [], None
    for t in range(ELEMS // LANES):
        count = jnp.dot(
            marks[:, LANES * t : LANES * t + LANES], earlier, preferred_element_type=f32
        )
        before.append(count[:, :LANES] if t == 0 else count[:, :LANES] + total)
        total = count[:, LANES:] if t == 0 else count[:, LANES:] + total
    before = jnp.concatenate(before, axis=1)
    rank = jnp.sum(hits * before[:DEVICES], axis=0, keepdims=True)
    column = rank.astype(jnp.int32) * DEVICES + owners
    slot_rows = lax.broadcasted_iota(jnp.int32, (DEVICES * SLOTS, ELEMS), 0)
    onehot[...] = jnp.where(slot_rows == column, 1.0, 0.0).astype(bf16)
    spot = jnp.where(
        below > 0.5,
        before[DEVICES : DEVICES + 4],
        jnp.where(above > 0.5, before[DEVICES + 8 : DEVICES + 12] + CROSS, -1000.0),
    ).astype(jnp.int32)

    for t in range(ELEMS // LANES):
        tiles[192 * t : 192 * t + 192, :] = state[:, LANES * t : LANES * t + LANES]
    for face_id in range(4):
        for field in range(3):
            at = (face_id % 2) * 24 + field * 8
            if face_id < 2:
                for t in range(ELEMS // LANES):
                    start = 192 * t + 64 * field + 7 * face_id
                    trace[0, at : at + 8, LANES * t : LANES * t + LANES] = tiles[
                        pl.ds(start, 8, stride=8), :
                    ]
            else:
                start = 64 * field + 56 * (face_id - 2)
                trace[1, at : at + 8, :] = state[start : start + 8, :]

    first_row = lax.broadcasted_iota(jnp.int32, (8, ELEMS), 0) == 0
    name = (
        lax.broadcasted_iota(jnp.int32, (8, ELEMS), 1) + (me * ELEMS + NAME_BASE)
    ).astype(f32)
    name = jnp.where(first_row, name, 0.0)
    lane_rows = lax.broadcasted_iota(jnp.int32, (LANES, ELEMS), 0)
    nt_dims = (((1,), (1,)), ((), ()))
    for pair in (0, 1):
        packed = None
        for position in (0, 1):
            face_id = 2 * pair + position
            rows = jnp.concatenate([trace[pair, 24 * position : 24 * position + 24, :], name])
            chosen = lane_rows == spot[face_id : face_id + 1] + 2 * CROSS * position
            part = lax.dot_general(
                jnp.concatenate(split2(rows), axis=0),
                jnp.where(chosen, 1.0, 0.0).astype(bf16),
                nt_dims,
                preferred_element_type=f32,
            )
            packed = part if packed is None else packed + part
        crossing[pair] = packed[:32] + packed[32:]

    scale = (-time_step) * metric[...]
    depth, moment_x, moment_y = (state[64 * f : 64 * f + 64, :] for f in range(3))
    inv = 1.0 / depth
    speed_x, speed_y = moment_x * inv, moment_y * inv
    pressure = 0.5 * earth_pressure * depth * depth
    drag = friction / jnp.sqrt(speed_x * speed_x + speed_y * speed_y + 1.0)
    cross = moment_x * speed_y
    parts = [
        (depth, moment_x, moment_y),
        (
            moment_x + time_step * (depth * (slope_x - drag * speed_x)),
            moment_x * speed_x + pressure,
            cross,
        ),
        (
            moment_y + time_step * (depth * (slope_y - drag * speed_y)),
            cross,
            moment_y * speed_y + pressure,
        ),
    ]
    stepped = []
    for q, flux_x, flux_y in parts:
        q_high, q_low = split2(q)
        x_high, x_low = split2(scale * flux_x)
        y_high, y_low = split2(scale * flux_y)
        operand = jnp.concatenate(
            [q_high, x_high, y_high, q_low, x_low, y_low, x_high, y_high], axis=0
        )
        rows = slice(80 * len(stepped), 80 * len(stepped) + 80)
        stepped.append(jnp.dot(table[rows, :], operand, preferred_element_type=f32))

    def place(rows):
        both = lax.dot_general(
            onehot[...],
            jnp.concatenate(split2(rows), axis=0),
            nt_dims,
            preferred_element_type=f32,
        )
        both = both[:, :LANES] + both[:, LANES:]
        return [both[j * DEVICES : (j + 1) * DEVICES] for j in range(SLOTS)]

    lane_at = lax.broadcasted_iota(jnp.int32, (DEVICES, LANES), 1)
    extra = stepped[0][-EXTRA:] + stepped[1][-EXTRA:] + stepped[2][-EXTRA:]
    flag_row = lax.broadcasted_iota(jnp.int32, (EXTRA, ELEMS), 0) == FLAG
    extra = extra + jnp.where(flag_row, flags[...].astype(f32), 0.0)
    slots = place(
        jnp.concatenate(
            [s[:MAIN] for s in stepped] + [extra, jnp.zeros((LANES - INNER, ELEMS), f32)], axis=0
        )
    )
    for r in range(INNER_ROWS):
        tail = pltpu.roll(slots[7], INNER - 16 * r, 1)
        inner_out[pl.ds(r, DEVICES, stride=8), :] = jnp.where(lane_at < INNER, slots[r], tail)

    pl.semaphore_wait(barrier, DEVICES - 1)

    def halo(pair, upward):
        far = 32 if pair else 1
        target = lax.rem(me + (far if upward else DEVICES - far), DEVICES)
        side = 0 if upward else 1
        return pltpu.make_async_remote_copy(
            src_ref=crossing.at[pair],
            dst_ref=ghost.at[pair, side],
            send_sem=halo_send.at[pair, side],
            recv_sem=halo_recv.at[pair, side],
            device_id=(target,),
            device_id_type=MESH,
        )

    halos = [halo(pair, upward) for pair in (0, 1) for upward in (True, False)]
    for copy in halos:
        copy.start()

    def block(ref, device, rows):
        return ref.at[pl.ds(pl.multiple_of(device * 8, 8), rows)]

    def exchange(order, source, target, rows, send_sem, recv_sem):
        for to in order:
            pltpu.make_async_remote_copy(
                src_ref=block(source, to, rows),
                dst_ref=block(target, me, rows),
                send_sem=send_sem,
                recv_sem=recv_sem,
                device_id=(to,),
                device_id_type=MESH,
            ).start()

    exchange(others(2, False), inner_out, inner_in, INNER_ROWS, inner_send, inner_recv)
    own_inner = pltpu.make_async_copy(
        block(inner_out, me, INNER_ROWS), block(inner_in, me, INNER_ROWS), own_sem.at[0]
    )
    own_inner.start()

    for face_id in range(4):
        pair = face_id // 2
        at = (face_id % 2) * 24
        inside = [trace[pair, at + 8 * field : at + 8 * field + 8, :] for field in range(3)]
        flux_in, wave_in = face_flux(inside, face_id)
        for i, values in enumerate(flux_in + [wave_in]):
            own_flux[face_id, 8 * i : 8 * i + 8, :] = values
        partner = partners[face_id : face_id + 1]
        local = jnp.bitwise_and(partner, ELEMS - 1)
        piece = lax.shift_right_arithmetic(local, 7)
        lane = jnp.bitwise_and(local, LANES - 1)
        at = (opposite[face_id] % 2) * 24
        for t in range(ELEMS // LANES):
            cols = slice(t * LANES, (t + 1) * LANES)
            index = jnp.broadcast_to(lane[:, cols], (8, LANES))
            piece_t = jnp.broadcast_to(piece[:, cols], (8, LANES))
            for field in range(3):
                rows = slice(at + field * 8, at + field * 8 + 8)
                found = None
                for c in range(ELEMS // LANES):
                    values = trace[pair, rows, c * LANES : (c + 1) * LANES]
                    got = jnp.take_along_axis(values, index, axis=1, mode="promise_in_bounds")
                    found = got if c == 0 else jnp.where(piece_t == c, got, found)
                across[face_id, 8 * field : 8 * field + 8, cols] = found

    for copy in halos:
        copy.wait()

    lift_scale = (time_step * lift_weight * 0.5) * metric[...]
    from_below = jnp.bitwise_and(lax.broadcasted_iota(jnp.int32, (32, LANES), 1), CROSS) != 0
    named = (partners + NAME_BASE).astype(f32)
    lifted = [[None] * 4 for _ in range(3)]
    zeros = jnp.zeros((2 * CROSS, ELEMS), bf16)
    for pair in (0, 1):
        merged = jnp.where(from_below, ghost[pair, 0], ghost[pair, 1])
        names = jnp.transpose(merged[24:32])[:, 0:1]
        chosen = []
        for position in (0, 1):
            face_id = 2 * pair + position
            start = 2 * CROSS * (1 - position)
            match = names[start : start + 2 * CROSS] == named[face_id : face_id + 1]
            match = jnp.where(match, 1.0, 0.0).astype(bf16)
            chosen.append(jnp.concatenate([zeros, match] if start else [match, zeros], axis=0))
        got = jnp.dot(
            jnp.concatenate(split2(merged), axis=0),
            jnp.concatenate(chosen, axis=1),
            preferred_element_type=f32,
        )
        got = got[:32] + got[32:]
        for position in (0, 1):
            face_id = 2 * pair + position
            wall = jnp.logical_not(real[face_id : face_id + 1])
            local = homes[face_id : face_id + 1] == me
            at = position * 24
            inside = [trace[pair, at + 8 * field : at + 8 * field + 8, :] for field in range(3)]
            reflected = mirror(inside, face_id)
            outside = []
            for field in range(3):
                rows = slice(8 * field, 8 * field + 8)
                there = got[rows, ELEMS * position : ELEMS * position + ELEMS]
                there = jnp.where(local, across[face_id, rows, :], there)
                outside.append(jnp.where(wall, reflected[field], there))
            flux_out, wave_out = face_flux(outside, face_id)
            largest = jnp.maximum(own_flux[face_id, 24:32, :], wave_out)
            for field in range(3):
                jump = own_flux[face_id, 8 * field : 8 * field + 8, :] - flux_out[field]
                lifted[field][face_id] = lift_scale * (
                    jump + largest * (outside[field] - inside[field])
                )
    outer = [
        stepped[field][MAIN : MAIN + OUTER] + jnp.concatenate(lifted[field], axis=0)
        for field in range(3)
    ]
    slots = place(jnp.concatenate(outer + [jnp.zeros((LANES - 96, ELEMS), f32)], axis=0))
    for r in range(4):
        pair_of = jnp.where(lane_at < 64, slots[r], pltpu.roll(slots[r + 4], 64, 1))
        outer_out[pl.ds(r, DEVICES, stride=8), :] = pair_of
    for q in range(2):
        row = pltpu.roll(slots[4 * q], 64, 1)
        for k in range(1, 4):
            piece = slots[4 * q + k] if k == 2 else pltpu.roll(slots[4 * q + k], (32 * k - 64) % 128, 1)
            row = jnp.where(lane_at >= 32 * k, piece, row)
        outer_out[pl.ds(4 + q, DEVICES, stride=8), :] = row

    exchange(others(1, True), outer_out, outer_in, OUTER_ROWS, outer_send, outer_recv)
    own_outer = pltpu.make_async_copy(
        block(outer_out, me, OUTER_ROWS), block(outer_in, me, OUTER_ROWS), own_sem.at[1]
    )
    own_outer.start()

    def wait_all(source, target, rows, send_sem, recv_sem):
        every = pl.ds(0, (DEVICES - 1) * rows)
        copies = pltpu.make_async_remote_copy(
            src_ref=source.at[every],
            dst_ref=target.at[every],
            send_sem=send_sem,
            recv_sem=recv_sem,
            device_id=(me,),
            device_id_type=MESH,
        )
        copies.wait_send()
        copies.wait_recv()

    tables_load = pltpu.make_async_copy(tables_in, tables_out, own_sem.at[3])
    tables_load.start()
    own_inner.wait()
    wait_all(inner_out, inner_in, INNER_ROWS, inner_send, inner_recv)
    last = None
    for r in range(INNER_ROWS):
        tail = pltpu.roll(inner_in[pl.ds(r, DEVICES, stride=8), :], 16 * r + 16, 1)
        last = tail if r == 0 else jnp.where(lane_at >= 16 * r, tail, last)
    inner_in[pl.ds(7, DEVICES, stride=8), :] = last
    inner_turned[...] = jnp.transpose(inner_in[...])[:INNER]
    turned = pltpu.make_async_copy(inner_turned, inner_turned_out, own_sem.at[2])
    turned.start()
    own_outer.wait()
    turned.wait()
    tables_load.wait()
    wait_all(outer_out, outer_in, OUTER_ROWS, outer_send, outer_recv)


def child_kernel(inner, outer, tables, out_hbm, flat, out, store_sem):
    cuts = (0, 640, DEVICES * SLOTS)

    def unpack(part):
        first, slots = cuts[part], cuts[part + 1] - cuts[part]
        devices = slots // SLOTS
        lane_at = lax.broadcasted_iota(jnp.int32, (devices, LANES), 1)
        for j in range(SLOTS):
            body = outer[pl.ds(first + j % 4, devices, stride=8), :]
            rest = outer[pl.ds(first + 4 + j // 4, devices, stride=8), :]
            body = pltpu.roll(body, 64, 1) if j >= 4 else body
            rest = rest if j % 4 == 2 else pltpu.roll(rest, (64 - 32 * (j % 4)) % 128, 1)
            flat[pl.ds(first + j, devices, stride=8), :] = jnp.where(lane_at < 64, body, rest)
        return jnp.transpose(flat[first : first + slots, :])

    stores = []
    ahead = unpack(0)
    for part in range(2):
        slots = cuts[part + 1] - cuts[part]
        columns = slice(cuts[part], cuts[part + 1])
        faces = ahead
        refined = inner[3 * MAIN + FLAG : 3 * MAIN + FLAG + 1, columns] > 0.5
        for field in range(3):
            own = slice(MAIN * field, MAIN * field + MAIN)
            start = 3 * MAIN + 8 * (field // 2)
            values = jnp.concatenate(
                [
                    inner[own, columns],
                    faces[own],
                    inner[start : start + 8, columns],
                    jnp.zeros((8, slots), f32),
                ],
                axis=0,
            )
            high, low = split2(values)
            operand = jnp.concatenate([high, low, high, jnp.zeros((16, slots), bf16)], axis=0)
            nodes = jnp.dot(tables[field % 2], operand, preferred_element_type=f32)
            if field == 0 and part == 0:
                ahead = unpack(part + 1)
            for c in range(4):
                start = 192 * c + 64 * field
                other = nodes[256:320] if c == 0 else 0.0
                out[start : start + 64, columns] = jnp.where(
                    refined, nodes[64 * c : 64 * c + 64], other
                )
                box = (pl.ds(start, 64), pl.ds(cuts[part], slots))
                store = pltpu.make_async_copy(
                    out.at[box], out_hbm.at[box], store_sem.at[12 * part + 4 * field + c]
                )
                store.start()
                stores.append(store)
    for store in stores:
        store.wait()


def on_device(state, neighbours, metric, flags, new_owner):
    hbm = pl.BlockSpec(memory_space=pl.ANY)
    slots = DEVICES * SLOTS
    buffer = pltpu.VMEM((slots, LANES), f32)
    dma = pltpu.SemaphoreType.DMA
    inner, outer, tables = pl.pallas_call(
        step_kernel,
        out_shape=(
            jax.ShapeDtypeStruct((INNER, slots), f32),
            jax.ShapeDtypeStruct((slots, LANES), f32),
            jax.ShapeDtypeStruct((2, 320, 256), bf16),
        ),
        in_specs=[pl.BlockSpec(memory_space=pltpu.HBM)] * 7,
        out_specs=(hbm, hbm, hbm),
        scratch_shapes=[
            pltpu.VMEM((192, ELEMS), f32),
            pltpu.VMEM((4, ELEMS), jnp.int32),
            pltpu.VMEM((1, ELEMS), f32),
            pltpu.VMEM((1, ELEMS), jnp.int32),
            pltpu.VMEM((1, ELEMS), jnp.int32),
            pltpu.VMEM((240, 512), bf16),
            pltpu.VMEM((192 * ELEMS // LANES, LANES), f32),
            pltpu.VMEM((2, 48, ELEMS), f32),
            pltpu.VMEM((4, 32, ELEMS), f32),
            pltpu.VMEM((4, 24, ELEMS), f32),
            pltpu.VMEM((2, 32, LANES), f32),
            pltpu.VMEM((2, 2, 32, LANES), f32),
            buffer,
            buffer,
            buffer,
            pltpu.VMEM((INNER, slots), f32),
            pltpu.VMEM((slots, ELEMS), bf16),
            dma((6,)),
            dma((2, 2)),
            dma((2, 2)),
            dma,
            dma,
            dma,
            dma,
            dma((4,)),
        ],
        compiler_params=pltpu.CompilerParams(collective_id=0, has_side_effects=True, vmem_limit_bytes=16 << 20),
        name="step_and_migrate",
    )(
        *(
            pltpu.with_memory_space_constraint(x, pltpu.HBM)
            for x in (
                state.reshape(192, ELEMS),
                neighbours,
                metric.reshape(1, ELEMS),
                flags.reshape(1, ELEMS),
                new_owner.reshape(1, ELEMS),
                jnp.asarray(step_table(), bf16),
                jnp.asarray(child_tables(), bf16),
            )
        )
    )
    children = pl.pallas_call(
        child_kernel,
        out_shape=jax.ShapeDtypeStruct((768, slots), f32),
        in_specs=[pl.BlockSpec(memory_space=pltpu.VMEM)] * 3,
        out_specs=pl.BlockSpec(memory_space=pltpu.HBM),
        scratch_shapes=[
            buffer,
            pltpu.VMEM((768, slots), f32),
            dma((24,)),
        ],
        compiler_params=pltpu.CompilerParams(vmem_limit_bytes=16 << 20),
        name="make_children",
    )(inner, outer, tables)
    return children.reshape(4, 3, 64, slots)


def solution(mesh):
    placed = (P(None, None, "curve"), P(None, "curve"), P("curve"), P("curve"), P("curve", None))
    return jax.shard_map(
        on_device,
        mesh=mesh,
        in_specs=placed,
        out_specs=P(None, None, None, "curve"),
        check_vma=False,
    )
```
